128 devices in a mesh: field: 4 (over x), shard: 32 (over z, y, core).
Axes of the slice: x: 4, y: 4, z: 4, core: 2. Of those that a mesh axis runs over, the one named last changes fastest.
Arguments:
- focal_uv: float32 [2048, 6, 2, 128], P(('field', 'shard')), may hold values from -1 to 1
- offsets: float32 [2048, 6, 2, 128], P(('field', 'shard')), may hold values from -6 to 6
- w_diag: float32 [2048, 6, 2, 128], P(('field', 'shard')), may hold values from 0.5 to 8
- w_corr: float32 [2048, 6, 128], P(('field', 'shard')), may hold values from -0.6 to 0.6
- star_count: int32 [2048], P(('field', 'shard')), may hold values from 16 to 128
- exposure_ids: int32 [2048, 6], P(('field', 'shard')), may hold values from 0 to 16383, as said below
- ccd_ids: int32 [2048, 6], P(('field', 'shard')), may hold values from 0 to 188
- exp_slot: int32 [16384], replicated, may hold values from 0 to 16383, as said below
Outputs:
- star_update: float32 [2048, 2, 128], P(('field', 'shard'))
- exposure_update: float32 [56, 16384], P(None, ('field', 'shard'))
- ccd_update: float32 [189, 6], replicated
The draws below stay inside these ranges and needn't reach their ends.
Inputs may be any that keep to these rules, and one draw needn't show every extreme that they name: `exposure_ids`: exposure e belongs to owner (exp_slot[e] // 128) % 32 and field block exp_slot[e] // 4096. Among the 96 tile visits of one device (aligned blocks of 16 tiles), at most 4 have exposures of one owner, and exactly 4 for half of the owners; at most 2 have exposures of one owner in one field block, and exactly 2 for some pairs. `exp_slot`: A permutation.
All inputs are finite; a program needn't handle non-finite values.
Results may differ from the reference program's by a relative error of at most 0.0003.
Values sent between devices are 32-bit elements; how exact they have to be, the bound alone decides.
No kernel may reach another device: no remote copies, remote signals or barrier semaphores. Data moves between devices by JAX's collectives and lax.ppermute only.
A program may use at most 256 MiB of HBM per device.

```python
import math
import jax
import jax.numpy as jnp
import numpy as np
from jax import lax

ORDER = 6
POLY = 28
STARS = 128
VISITS = 6
NCCD = 189
TILES_DEV = 16
EXP_DEV = 128
TILES = 2048
EXPOSURES = 16384
CAP = 4
N_FIELD = 4
N_SHARD = 32


def owner_layout(key):
    return jax.random.permutation(jax.random.fold_in(key, 17), EXPOSURES).astype(jnp.int32)


def draw_exp_slot(key, part):
    return owner_layout(key)


def draw_exposure_ids(key, part):
    slot_of = owner_layout(key)
    inverse = jnp.zeros((EXPOSURES,), jnp.int32).at[slot_of].set(jnp.arange(EXPOSURES, dtype=jnp.int32))
    ranks = np.concatenate([np.repeat(np.arange(N_SHARD // 2), CAP), np.repeat(np.arange(N_SHARD // 2, N_SHARD), CAP // 2)]).astype(np.int32)
    devices_all = N_FIELD * N_SHARD
    visits_dev = TILES_DEV * VISITS
    field_keys = jax.random.split(jax.random.fold_in(key, 23), N_FIELD)
    orders = jax.vmap(lambda single: jax.random.permutation(single, N_SHARD))(field_keys).astype(jnp.int32)
    device_keys = jax.random.split(jax.random.fold_in(key, 29), devices_all)
    field_of = jnp.arange(devices_all, dtype=jnp.int32) // N_SHARD

    def arrange(single, field_index):
        return jax.random.permutation(single, orders[field_index][jnp.asarray(ranks)])
    owners = jax.vmap(arrange)(device_keys, field_of).astype(jnp.int32)
    marks = (owners[:, :, None] == jnp.arange(N_SHARD, dtype=jnp.int32)[None, None, :]).astype(jnp.int32)
    seen = jnp.cumsum(marks, axis=1) - marks
    rank_in = jnp.sum(seen * marks, axis=2)
    counts = jnp.sum(marks, axis=1)
    full = jnp.take_along_axis(counts, owners, axis=1) == CAP
    first = jax.random.randint(jax.random.fold_in(key, 41), (devices_all, N_SHARD), 0, N_FIELD)
    second = (first + jax.random.randint(jax.random.fold_in(key, 43), (devices_all, N_SHARD), 1, N_FIELD)) % N_FIELD
    first_of = jnp.take_along_axis(first, owners, axis=1)
    second_of = jnp.take_along_axis(second, owners, axis=1)
    loose = jax.random.randint(jax.random.fold_in(key, 31), (devices_all, visits_dev), 0, N_FIELD)
    fblock = jnp.where(full, jnp.where(rank_in < CAP // 2, first_of, second_of), loose)
    within = jax.random.randint(jax.random.fold_in(key, 37), (devices_all, visits_dev), 0, EXP_DEV)
    position = (fblock * N_SHARD + owners) * EXP_DEV + within
    return inverse[position].reshape(TILES, VISITS).astype(jnp.int32)


def place_ends(values, rng, least, high):
    longest = values.shape.index(max(values.shape))
    spots = []
    for shift in (0, 1):
        where = [jax.random.randint(jax.random.fold_in(rng, axis), (), 0, length) for axis, length in enumerate(values.shape)]
        where[longest] = (where[longest] + shift) % values.shape[longest]
        spots.append(tuple(where))
    return values.at[spots[0]].set(least).at[spots[1]].set(high)


def steps_of(rng, dims, cuts, least, top_value):
    def one(axis_at, parts):
        draws = jax.random.uniform(jax.random.fold_in(jax.random.fold_in(rng, 6), axis_at), (parts,), jnp.float32, least / len(cuts), top_value / len(cuts))
        return jnp.repeat(jnp.exp(draws), dims[axis_at] // parts).reshape((-1,) + (1,) * (len(dims) - axis_at - 1))

    loudness = one(*cuts[0])
    for cut in cuts[1:]:
        loudness = loudness * one(*cut)
    return loudness


def gaussian(key, dims, scale, most, cuts=(), held_as=jnp.bfloat16):
    values = scale * jax.random.normal(key, dims, jnp.float32)
    if cuts:
        values = values * steps_of(key, dims, cuts, -0.22, 0.18)
    return jnp.clip(values, -most, most).astype(held_as)


def setup_inputs(seed: int = 0) -> dict:
    seeds = jax.random.split(jax.random.key(seed), 9)
    return {
        "focal_uv": jnp.clip(jax.random.uniform(seeds[0], (TILES, VISITS, 2, STARS), jnp.float32, -1.0, 1.0) * steps_of(seeds[0], (TILES, VISITS, 2, STARS), ((0, 128),), -0.4, 0.0), -1.0, 1.0),
        "offsets": gaussian(seeds[1], (TILES, VISITS, 2, STARS), 1.0, 6.0, ((0, 128),), jnp.float32),
        "w_diag": jnp.clip(jnp.exp(math.log(8.0) - 2.7725887 * jax.random.uniform(seeds[2], (TILES, VISITS, 2, STARS), jnp.float32) ** steps_of(seeds[2], (TILES, VISITS, 2, STARS), ((0, 128),), -0.2, 0.2)), 0.5, 8.0),
        "w_corr": jnp.clip(jax.random.uniform(seeds[3], (TILES, VISITS, STARS), jnp.float32, -0.6, 0.6) * steps_of(seeds[3], (TILES, VISITS, STARS), ((0, 128),), -0.4, 0.0), -0.6, 0.6),
        "star_count": place_ends(jax.random.randint(seeds[4], (TILES,), 16, STARS + 1), jax.random.fold_in(seeds[4], 1), 16, STARS).astype(jnp.int32),
        "exposure_ids": draw_exposure_ids(jax.random.fold_in(seeds[8], 71), 0),
        "ccd_ids": place_ends(jax.random.randint(seeds[6], (TILES, VISITS), 0, NCCD), jax.random.fold_in(seeds[6], 1), 0, NCCD - 1).astype(jnp.int32),
        "exp_slot": draw_exp_slot(jax.random.fold_in(seeds[8], 71), 0),
    }


STAR_DAMP = 0.1
EXPOSURE_DAMP = 1.0
DETECTOR_DAMP = 1.0
HIGH = lax.Precision.HIGHEST

def legendre_terms(coord_u, coord_v):

    def series(value):
        values = [jnp.ones_like(value), value]
        for degree in range(1, ORDER):
            values.append(((2 * degree + 1) * value * values[degree] - degree * values[degree - 1]) / (degree + 1))
        return values
    series_u = series(coord_u)
    series_v = series(coord_v)
    terms = []
    for total in range(ORDER + 1):
        for first in range(total + 1):
            second = total - first
            terms.append(math.sqrt((2 * first + 1) * (2 * second + 1)) * series_u[first] * series_v[second])
    return jnp.stack(terms, axis=-2)

def plane_terms(coord_u, coord_v):
    return jnp.stack([jnp.ones_like(coord_u), coord_u, coord_v], axis=-2)

def star_terms(offsets, w_diag, w_corr, star_count):
    stars = offsets.shape[-1]
    present = (jnp.arange(stars, dtype=jnp.int32)[None, :] < star_count[:, None]).astype(jnp.float32)[:, None, :]
    weight_xx = w_diag[:, :, 0] * present
    weight_yy = w_diag[:, :, 1] * present
    weight_xy = w_corr * jnp.sqrt(w_diag[:, :, 0] * w_diag[:, :, 1]) * present
    resid_x = offsets[:, :, 0]
    resid_y = offsets[:, :, 1]
    hess_xx = lax.optimization_barrier(jnp.sum(weight_xx, 1)) + STAR_DAMP
    hess_yy = lax.optimization_barrier(jnp.sum(weight_yy, 1)) + STAR_DAMP
    hess_xy = lax.optimization_barrier(jnp.sum(weight_xy, 1))
    determ = hess_xx * hess_yy - hess_xy * hess_xy
    inv_xx = (hess_yy / determ)[:, None]
    inv_yy = (hess_xx / determ)[:, None]
    inv_xy = (-hess_xy / determ)[:, None]
    grad_x = lax.optimization_barrier(jnp.sum(weight_xx * resid_x + weight_xy * resid_y, 1))[:, None]
    grad_y = lax.optimization_barrier(jnp.sum(weight_xy * resid_x + weight_yy * resid_y, 1))[:, None]
    left_x = resid_x - (inv_xx * grad_x + inv_xy * grad_y)
    left_y = resid_y - (inv_xy * grad_x + inv_yy * grad_y)
    pull_x = weight_xx * left_x + weight_xy * left_y
    pull_y = weight_xy * left_x + weight_yy * left_y
    prod_11 = inv_xx * weight_xx + inv_xy * weight_xy
    prod_12 = inv_xx * weight_xy + inv_xy * weight_yy
    prod_21 = inv_xy * weight_xx + inv_yy * weight_xy
    prod_22 = inv_xy * weight_xy + inv_yy * weight_yy
    schur_xx = weight_xx - (weight_xx * prod_11 + weight_xy * prod_21)
    schur_yy = weight_yy - (weight_xy * prod_12 + weight_yy * prod_22)
    schur_xy = weight_xy - (weight_xx * prod_12 + weight_xy * prod_22)
    return ((inv_xx, inv_yy, inv_xy), (weight_xx, weight_yy, weight_xy), (schur_xx, schur_yy, schur_xy, pull_x, pull_y))

def normal_vectors(basis, schur_xx, schur_yy, schur_xy, pull_x, pull_y):

    def outer(scale):
        product = jnp.einsum('...ps,...qs->...pq', basis * scale[..., None, :], basis, precision=HIGH)
        return product.reshape(scale.shape[:-1] + (-1,))
    grad_x = jnp.einsum('...ps,...s->...p', basis, pull_x, precision=HIGH)
    grad_y = jnp.einsum('...ps,...s->...p', basis, pull_y, precision=HIGH)
    return jnp.concatenate([outer(schur_xx), outer(schur_yy), outer(schur_xy), grad_x, grad_y], axis=-1)

def batched_cholesky_solve(matrix, rhs):
    order_n = matrix.shape[0]
    rows_idx = jnp.arange(order_n, dtype=jnp.int32)
    work = matrix
    columns = []
    for step in range(order_n):
        pivot = jnp.sqrt(work[step, step])
        column = work[:, step] / pivot[None, :]
        column = jnp.where((rows_idx >= step)[:, None], column, jnp.float32(0.0))
        columns.append(column)
        work = work - column[:, None, :] * column[None, :, :]
    lower = jnp.stack(columns, axis=1)
    remain = rhs
    forward = []
    for step in range(order_n):
        value = remain[step] / lower[step, step]
        forward.append(value)
        remain = remain - lower[:, step] * value[None, :]
    remain = jnp.stack(forward, axis=0)
    backward = [None] * order_n
    for step in range(order_n - 1, -1, -1):
        value = remain[step] / lower[step, step]
        backward[step] = value
        remain = remain - lower[step] * value[None, :]
    return jnp.stack(backward, axis=0)

def solve_blocks(vectors, width, damping):
    square = width * width
    flipped = vectors.T
    count = vectors.shape[0]
    part_xx = flipped[:square].reshape(width, width, count)
    part_yy = flipped[square:2 * square].reshape(width, width, count)
    part_xy = flipped[2 * square:3 * square].reshape(width, width, count)
    matrix = jnp.concatenate([jnp.concatenate([part_xx, part_xy], 1), jnp.concatenate([part_xy, part_yy], 1)], 0)
    matrix = matrix + damping * jnp.eye(2 * width, dtype=jnp.float32)[:, :, None]
    rhs = flipped[3 * square:3 * square + 2 * width]
    return batched_cholesky_solve(matrix, rhs).T

def star_solve(inverse, weights, offsets, model_x, model_y):
    inv_xx, inv_yy, inv_xy = inverse
    weight_xx, weight_yy, weight_xy = weights
    left_x = offsets[:, :, 0] - model_x
    left_y = offsets[:, :, 1] - model_y
    grad_x = lax.optimization_barrier(jnp.sum(weight_xx * left_x + weight_xy * left_y, 1))
    grad_y = lax.optimization_barrier(jnp.sum(weight_xy * left_x + weight_yy * left_y, 1))
    return jnp.stack([inv_xx[:, 0] * grad_x + inv_xy[:, 0] * grad_y, inv_xy[:, 0] * grad_x + inv_yy[:, 0] * grad_y], axis=1)

def reference(focal_uv, offsets, w_diag, w_corr, star_count, exposure_ids, ccd_ids, exp_slot):
    tiles = offsets.shape[0]
    block = math.gcd(tiles, 256)
    count_blocks = tiles // block
    width_exp = 3 * POLY * POLY + 2 * POLY
    width_ccd = 33

    def split_blocks(array):
        return array.reshape((count_blocks, block) + array.shape[1:])
    inputs = tuple((split_blocks(array) for array in (focal_uv, offsets, w_diag, w_corr, star_count, exposure_ids, ccd_ids)))

    def accumulate(carry, item):
        exp_table, ccd_table = carry
        coords, offs, diag, corr, count, exp_ids, det_ids = item
        terms = star_terms(offs, diag, corr, count)
        basis = legendre_terms(coords[:, :, 0], coords[:, :, 1])
        plane = plane_terms(coords[:, :, 0], coords[:, :, 1])
        exp_vec = normal_vectors(basis, *terms[2]).reshape(-1, width_exp)
        ccd_vec = normal_vectors(plane, *terms[2]).reshape(-1, width_ccd)
        exp_table = exp_table + jax.ops.segment_sum(exp_vec, exp_ids.reshape(-1), num_segments=EXPOSURES)
        ccd_table = ccd_table + jax.ops.segment_sum(ccd_vec, det_ids.reshape(-1), num_segments=NCCD)
        return ((exp_table, ccd_table), None)
    start = (jnp.zeros((EXPOSURES, width_exp), jnp.float32), jnp.zeros((NCCD, width_ccd), jnp.float32))
    (exp_table, ccd_table), _ = lax.scan(accumulate, start, inputs)
    exp_solution = solve_blocks(exp_table, POLY, EXPOSURE_DAMP)
    ccd_update = solve_blocks(ccd_table, 3, DETECTOR_DAMP)
    exposure_update = jnp.zeros((2 * POLY, EXPOSURES), jnp.float32).at[:, exp_slot].set(exp_solution.T)

    def star_block(item):
        coords, offs, diag, corr, count, exp_ids, det_ids = item
        terms = star_terms(offs, diag, corr, count)
        basis = legendre_terms(coords[:, :, 0], coords[:, :, 1])
        plane = plane_terms(coords[:, :, 0], coords[:, :, 1])
        coeff = exp_solution[exp_ids]
        det_coeff = ccd_update[det_ids]
        model_x = jnp.einsum('tkp,tkps->tks', coeff[..., :POLY], basis, precision=HIGH) + jnp.einsum('tkp,tkps->tks', det_coeff[..., :3], plane, precision=HIGH)
        model_y = jnp.einsum('tkp,tkps->tks', coeff[..., POLY:], basis, precision=HIGH) + jnp.einsum('tkp,tkps->tks', det_coeff[..., 3:], plane, precision=HIGH)
        return star_solve(terms[0], terms[1], offs, model_x, model_y)
    star_update = lax.map(star_block, inputs).reshape(tiles, 2, offsets.shape[-1])
    return (star_update, exposure_update, ccd_update)
```

```python
import math

import jax
import jax.numpy as jnp
import numpy as np
from jax import lax
from jax.experimental import pallas as pl
from jax.experimental.pallas import tpu as pltpu
from jax.sharding import PartitionSpec as P

ORDER = 6
POLY = 28
VISITS = 6
NCCD = 189
LANES = 128
STAR_DAMP = 0.1
EXPOSURE_DAMP = 1.0
DETECTOR_DAMP = 1.0
HIGH = lax.Precision.HIGHEST
DEG2 = 2 * ORDER
F32 = jnp.float32

TERMS = [(i, n - i) for n in range(DEG2 + 1) for i in range(n + 1)]
TERM_INDEX = {term: at for at, term in enumerate(TERMS)}
SCALE = [math.sqrt((2 * i + 1) * (2 * j + 1)) for i, j in TERMS[:POLY]]

ROW_GX = 288
ROW_GY = 320
ROW_DET = 352
ROWS = 384
MARK = 95


def linearisation():
    from numpy.polynomial import legendre

    table = np.zeros((ORDER + 1, ORDER + 1, DEG2 + 1))
    for m in range(ORDER + 1):
        for n in range(ORDER + 1):
            product = legendre.legmul([0] * m + [1], [0] * n + [1])
            table[m, n, : len(product)] = product
    return table


def expansion():
    table = linearisation()
    matrix = np.zeros((POLY * 32, 96))
    for q, (iq, jq) in enumerate(TERMS[:POLY]):
        for p, (ip, jp) in enumerate(TERMS[:POLY]):
            for at, (a, b) in enumerate(TERMS):
                matrix[q * 32 + p, at] = SCALE[p] * SCALE[q] * table[ip, iq, a] * table[jp, jq, b]
    return matrix.astype(np.float32)


def scale_rows():
    rows = np.zeros((32, LANES), np.float32)
    rows[:POLY] = np.array(SCALE, np.float32)[:, None]
    return rows


def dot(a, b, dims):
    return lax.dot_general(a, b, (dims, ((), ())), precision=HIGH, preferred_element_type=F32)


def iota(shape, axis):
    return lax.broadcasted_iota(jnp.int32, shape, axis)


def legendre(value, count):
    values = [None, value]
    for degree in range(1, count - 1):
        lower = (degree / (degree + 1)) * (values[degree - 1] if degree > 1 else 1.0)
        values.append(((2 * degree + 1) / (degree + 1)) * value * values[degree] - lower)
    return values


def star_terms(uv_ref, off_ref, diag_ref, corr_ref, count_ref):
    tiles = corr_ref.shape[0]
    lanes = iota((tiles, LANES), 1)
    counts = jnp.broadcast_to(count_ref[...].astype(F32), (tiles, tiles))
    square = (iota((tiles, tiles), 0) == iota((tiles, tiles), 1)).astype(F32)
    column = jnp.sum(counts * square, axis=1, keepdims=True)
    present = (lanes.astype(F32) < column).astype(F32)

    def rows(ref, visit, part):
        return ref[pl.ds(2 * visit + part, tiles, stride=2 * VISITS), :]

    weights = []
    resid = []
    for visit in range(VISITS):
        d0 = rows(diag_ref, visit, 0)
        d1 = rows(diag_ref, visit, 1)
        weights.append((d0 * present, d1 * present, corr_ref[:, visit, :] * jnp.sqrt(d0 * d1) * present))
        resid.append((rows(off_ref, visit, 0), rows(off_ref, visit, 1)))
    hess_xx = sum(w[0] for w in weights) + STAR_DAMP
    hess_yy = sum(w[1] for w in weights) + STAR_DAMP
    hess_xy = sum(w[2] for w in weights)
    determ = hess_xx * hess_yy - hess_xy * hess_xy
    inverse = (hess_yy / determ, hess_xx / determ, -hess_xy / determ)
    return weights, resid, inverse


def apply_inverse(inverse, x, y):
    inv_xx, inv_yy, inv_xy = inverse
    return inv_xx * x + inv_xy * y, inv_xy * x + inv_yy * y


def combine(values, sub):
    for shift in (4, 2, 1):
        low = (sub & shift) == 0
        half = len(values) // 2
        merged = []
        for at in range(half):
            a, b = values[at], values[at + half]
            if shift == 4:
                merged.append(jnp.where(low, a, b) + pltpu.roll(jnp.where(low, b, a), 4, 0))
            else:
                merged.append(jnp.where(low, a + pltpu.roll(a, 8 - shift, 0), b + pltpu.roll(b, shift, 0)))
        values = merged
    return values[0]


def transpose8(values, sub):
    values = list(values)
    for shift in (4, 2, 1):
        low = (sub & shift) == 0
        for at in range(8):
            if at & shift:
                continue
            a, b = values[at], values[at + shift]
            values[at] = jnp.where(low, a, pltpu.roll(b, shift, 0))
            values[at + shift] = jnp.where(low, pltpu.roll(a, 8 - shift, 0), b)
    return values


def moments_kernel(uv_ref, off_ref, diag_ref, corr_ref, count_ref, ids_ref, ccd_ref, slot_ref,
                   out_ref, uvt_ref, where_ref, chan, pu, pv, acc, mom):
    tiles = corr_ref.shape[0]
    visits_all = tiles * VISITS
    sub8 = iota((8, LANES), 0)

    lane16 = iota((tiles, LANES), 1)
    pad = jnp.zeros((LANES - visits_all, LANES), F32)
    ids = [
        jnp.where(lane16 < 64, ids_ref[:, k : k + 1], ccd_ref[:, k : k + 1]).astype(F32)
        for k in range(VISITS)
    ]
    turned = jnp.concatenate(ids + [pad], axis=0).T
    ident = turned[0:1].astype(jnp.int32)
    ccd = turned[64:65].astype(jnp.int32)
    rows128 = iota((LANES, LANES), 0)
    lanes128 = iota((LANES, LANES), 1)
    valid = iota((1, LANES), 1) < visits_all
    picked = dot(slot_ref[...].astype(F32), (rows128 == ident // LANES).astype(F32), ((0,), (0,)))
    position = jnp.sum(jnp.where(rows128 == ident % LANES, picked, 0.0), axis=0, keepdims=True)
    position = (position + 0.5).astype(jnp.int32)
    dest = jnp.where(valid, position // LANES, -1)
    ccd = jnp.where(valid, ccd, -2)
    dest_t = jnp.broadcast_to(dest.astype(F32), (LANES, LANES)).T.astype(jnp.int32)
    same = (dest_t == dest) & (rows128 < lanes128)
    copy_at = jnp.sum(same.astype(F32), axis=0, keepdims=True).astype(jnp.int32)
    mark = (position % LANES + 1).astype(F32)
    where_ref[...] = jnp.where(sub8 == 0, dest, jnp.where(sub8 == 1, copy_at, ccd))

    weights, resid, inverse = star_terms(uv_ref, off_ref, diag_ref, corr_ref, count_ref)
    grad_x = sum(w[0] * r[0] + w[2] * r[1] for w, r in zip(weights, resid))
    grad_y = sum(w[2] * r[0] + w[1] * r[1] for w, r in zip(weights, resid))
    shift_x, shift_y = apply_inverse(inverse, grad_x, grad_y)
    inv_xx, inv_yy, inv_xy = inverse
    channels = [[] for _ in range(7)]
    for visit in range(VISITS):
        w_xx, w_yy, w_xy = weights[visit]
        left_x = resid[visit][0] - shift_x
        left_y = resid[visit][1] - shift_y
        prod_11 = inv_xx * w_xx + inv_xy * w_xy
        prod_12 = inv_xx * w_xy + inv_xy * w_yy
        prod_21 = inv_xy * w_xx + inv_yy * w_xy
        prod_22 = inv_xy * w_xy + inv_yy * w_yy
        values = (
            uv_ref[pl.ds(2 * visit, tiles, stride=2 * VISITS), :],
            uv_ref[pl.ds(2 * visit + 1, tiles, stride=2 * VISITS), :],
            w_xx - (w_xx * prod_11 + w_xy * prod_21),
            w_yy - (w_xy * prod_12 + w_yy * prod_22),
            w_xy - (w_xx * prod_12 + w_xy * prod_22),
            w_xx * left_x + w_xy * left_y,
            w_xy * left_x + w_yy * left_y,
        )
        for at, value in enumerate(values):
            channels[at].append(value)
    for at in range(7):
        chan[at] = jnp.concatenate(channels[at] + [pad], axis=0).T
    uvt_ref[0] = chan[0]
    uvt_ref[1] = chan[1]

    groups = LANES // 8

    def tables(g, carry):
        at = pl.ds(pl.multiple_of(g * 8, 8), 8)
        for ref, source in ((pu, 0), (pv, 1)):
            for degree, value in enumerate(legendre(chan[source, at, :], DEG2 + 1)):
                if degree:
                    ref[degree, at, :] = value
        return carry

    lax.fori_loop(0, groups, tables, 0)

    def sweep(i, top, first, count, row0, width):
        heights = top - i + 1

        def step(g, carry):
            at = pl.ds(pl.multiple_of(g * 8, 8), 8)
            scaled = [chan[first + w, at, :] for w in range(count)]
            if i:
                factor = pu[i, at, :]
                scaled = [value * factor for value in scaled]
            new = []
            for j in range(heights):
                other = pv[j, at, :] if j else None
                for w in range(count):
                    term = scaled[w] * other if j else scaled[w]
                    new.append(carry[j * count + w] + term)
            return tuple(new)

        start = tuple(jnp.zeros((8, LANES), F32) for _ in range(heights * count))
        sums = lax.fori_loop(0, groups, step, start, unroll=2)
        for j in range(heights):
            for w in range(count):
                row = row0 + w * width + TERM_INDEX[(i, j)]
                acc[pl.ds(row * 8, 8), :] = sums[j * count + w]

    for i in range(DEG2 + 1):
        sweep(i, DEG2, 2, 3, 0, 96)
    for i in range(ORDER + 1):
        sweep(i, ORDER, 5, 2, ROW_GX, 32)
    zero = jnp.zeros((8, LANES), F32)
    for block in range(3):
        for row in range(len(TERMS), 96):
            acc[pl.ds((block * 96 + row) * 8, 8), :] = zero
    for block in range(2):
        for row in range(POLY, 32):
            acc[pl.ds((ROW_GX + block * 32 + row) * 8, 8), :] = zero

    def reduce_rows(g, carry):
        base = pl.multiple_of(g * 64, 64)
        mom[pl.ds(pl.multiple_of(g * 8, 8), 8), :] = combine(
            [acc[pl.ds(base + 8 * s, 8), :] for s in range(8)], sub8
        )
        return carry

    lax.fori_loop(0, ROW_DET // 8, reduce_rows, 0, unroll=2)
    mom[88:96, :] = jnp.where(sub8 == 7, mark, mom[88:96, :])

    zeros96 = jnp.zeros((96, LANES), F32)
    pulls = jnp.where(sub8 < 4, mom[ROW_GX : ROW_GX + 8], pltpu.roll(mom[ROW_GY : ROW_GY + 8], 4, 0))
    last = jnp.concatenate(
        [
            jnp.concatenate([mom[256:352], jnp.zeros((32, LANES), F32)], axis=0),
            jnp.concatenate([zeros96, mom[0:8], mom[96:104], mom[192:200], pulls], axis=0),
        ],
        axis=1,
    )
    for copy in range(2):
        place = ((rows128 == dest) & (copy_at == copy)).astype(F32)
        place_det = (rows128 * 2 + copy == ccd).astype(F32)
        out_ref[:, 3 * copy, :] = dot(place, mom[0:128], ((1,), (1,)))
        out_ref[:, 3 * copy + 1, :] = dot(place, mom[128:256], ((1,), (1,)))
        out_ref[:, 3 * copy + 2, :] = dot(
            jnp.concatenate([place, place_det], axis=1), last, ((1,), (1,))
        )


def detector_solve(table):
    def moment(block, i, j):
        return table[8 * block + TERM_INDEX[(i, j)] : 8 * block + TERM_INDEX[(i, j)] + 1]

    def block_of(block):
        one, u, v = moment(block, 0, 0), moment(block, 1, 0), moment(block, 0, 1)
        uu = (2.0 * moment(block, 2, 0) + one) * (1.0 / 3.0)
        vv = (2.0 * moment(block, 0, 2) + one) * (1.0 / 3.0)
        uv = moment(block, 1, 1)
        return [[one, u, v], [u, uu, uv], [v, uv, vv]]

    part_xx, part_yy, part_xy = block_of(0), block_of(1), block_of(2)
    matrix = [part_xx[p] + part_xy[p] for p in range(3)] + [part_xy[p] + part_yy[p] for p in range(3)]
    at = [TERM_INDEX[term] for term in ((0, 0), (1, 0), (0, 1))]
    rhs = [table[24 + a : 25 + a] for a in at] + [table[28 + a : 29 + a] for a in at]
    for p in range(6):
        matrix[p][p] = matrix[p][p] + DETECTOR_DAMP
    inverse = [None] * 6
    lower = [[None] * 6 for _ in range(6)]
    for step in range(6):
        pivot = matrix[step][step]
        for before in range(step):
            pivot = pivot - lower[step][before] * lower[step][before]
        inverse[step] = 1.0 / jnp.sqrt(pivot)
        for row in range(step + 1, 6):
            value = matrix[row][step]
            for before in range(step):
                value = value - lower[row][before] * lower[step][before]
            lower[row][step] = value * inverse[step]
    forward = []
    for step in range(6):
        value = rhs[step]
        for before in range(step):
            value = value - lower[step][before] * forward[before]
        forward.append(value * inverse[step])
    answer = [None] * 6
    for step in range(5, -1, -1):
        value = forward[step]
        for after in range(step + 1, 6):
            value = value - lower[after][step] * answer[after]
        answer[step] = value * inverse[step]
    return answer


UNKNOWNS = [("x", q) for q in range(28)] + [("y", q) for q in range(24, 28)] + [("y", q) for q in range(24)]
SIZE = 2 * POLY
BLOCKS = SIZE // 8
PANEL = 4


def solve_kernel(arr_ref, expand_ref, scale_ref, upd_ref, resp_ref, table, wide, mat, rhs, invs):
    sub8 = iota((8, LANES), 0)
    rows128 = iota((LANES, LANES), 0)
    lanes128 = iota((LANES, LANES), 1)

    picks = []
    for copy in range(2):
        column = arr_ref[:, 3 * copy, :][:, MARK : MARK + 1]
        picks.append((column.astype(jnp.int32) == lanes128 + 1).astype(F32))
    pick = jnp.concatenate(picks, axis=0)
    for block in range(3):
        both = jnp.concatenate([arr_ref[:, block, :], arr_ref[:, 3 + block, :]], axis=0)
        table[pl.ds(block * LANES, LANES), :] = dot(both, pick, ((0,), (0,)))

    sums = [jnp.sum(arr_ref[:, 3 * copy + 2, :], axis=0, keepdims=True) for copy in range(2)]
    turned = jnp.where(rows128 == 0, sums[0], jnp.where(rows128 == 1, sums[1], 0.0)).T
    answer = detector_solve(turned[96:128])

    moments = jnp.concatenate([table[0:96], table[96:192], table[192:288]], axis=1)
    chunk = 224
    for at in range(0, POLY * 32, chunk):
        wide[pl.ds(at, chunk), :] = dot(expand_ref[pl.ds(at, chunk), :], moments, ((1,), (0,)))

    def part(which, q, group):
        return wide[q * 32 + group * 8 : q * 32 + group * 8 + 8, which * LANES : (which + 1) * LANES]

    for col, (kind, q) in enumerate(UNKNOWNS):
        for group in range(col // 8, BLOCKS):
            if kind == "x":
                if group < 3:
                    value = part(0, q, group)
                elif group == 3:
                    value = jnp.where(sub8 < 4, part(0, q, 3), pltpu.roll(part(2, q, 3), 4, 0))
                else:
                    value = part(2, q, group - 4)
            elif group == 3:
                value = jnp.where(sub8 < 4, 0.0, pltpu.roll(part(1, q, 3), 4, 0))
            else:
                value = part(1, q, group - 4)
            if group == col // 8:
                value = value + jnp.where(sub8 == col % 8, EXPOSURE_DAMP, 0.0)
            mat[pl.ds(col * SIZE + group * 8, 8), :] = value
    grad_x = table[ROW_GX : ROW_GX + 32] * scale_ref[...]
    grad_y = table[ROW_GY : ROW_GY + 32] * scale_ref[...]
    rhs[0:24, :] = grad_x[0:24]
    rhs[24:32, :] = jnp.where(sub8 < 4, grad_x[24:32], pltpu.roll(grad_y[24:32], 4, 0))
    rhs[32:56, :] = grad_y[0:24]

    for k0 in range(0, SIZE, PANEL):
        g0 = k0 // 8
        count = BLOCKS - g0

        def update(j, carry):
            base = j * SIZE
            column = [mat[pl.ds(pl.multiple_of(base + g * 8, 8), 8), :] for g in range(g0, BLOCKS)]
            new = []
            for c in range(PANEL):
                factor = mat[pl.ds(base + k0 + c, 1), :]
                for g in range(count):
                    new.append(carry[c * count + g] - column[g] * factor)
            return tuple(new)

        panel = tuple(
            mat[pl.ds((k0 + c) * SIZE + g * 8, 8), :] for c in range(PANEL) for g in range(g0, BLOCKS)
        )
        if k0:
            panel = lax.fori_loop(0, k0, update, panel, unroll=4)
        panel = [list(panel[c * count : (c + 1) * count]) for c in range(PANEL)]
        right = [rhs[pl.ds(g * 8, 8), :] for g in range(g0, BLOCKS)]
        for c in range(PANEL):
            k = k0 + c
            row = k % 8
            inverse = lax.rsqrt(panel[c][0][row : row + 1])
            column = [value * inverse for value in panel[c]]
            for other in range(c + 1, PANEL):
                factor = column[0][k0 % 8 + other : k0 % 8 + other + 1]
                panel[other] = [panel[other][g] - column[g] * factor for g in range(count)]
            forward = right[0][row : row + 1] * inverse
            keep = jnp.where(sub8 <= row, right[0], right[0] - column[0] * forward)
            keep = jnp.where(sub8 == row, forward, keep)
            right = [keep] + [right[g] - column[g] * forward for g in range(1, count)]
            invs[k : k + 1, :] = inverse
            for g in range(count):
                mat[pl.ds(k * SIZE + (g0 + g) * 8, 8), :] = column[g]
        for g in range(count):
            rhs[pl.ds((g0 + g) * 8, 8), :] = right[g]

    solved = [None] * BLOCKS
    for b in range(BLOCKS - 1, -1, -1):
        right = rhs[b * 8 : b * 8 + 8]
        if b < BLOCKS - 1:
            partial = []
            for c in range(8):
                total = None
                for g in range(b + 1, BLOCKS):
                    term = mat[pl.ds((b * 8 + c) * SIZE + g * 8, 8), :] * solved[g]
                    total = term if total is None else total + term
                partial.append(total)
            right = right - combine(partial, sub8)
        diagonal = transpose8([mat[pl.ds((b * 8 + c) * SIZE + b * 8, 8), :] for c in range(8)], sub8)
        for c in range(7, -1, -1):
            value = right[c : c + 1] * invs[b * 8 + c : b * 8 + c + 1]
            right = jnp.where(sub8 < c, right - diagonal[c] * value, jnp.where(sub8 == c, value, right))
        solved[b] = right
    whole = jnp.concatenate(
        solved[0:3] + [solved[3][0:4]] + solved[4:7] + [solved[3][4:8]], axis=0
    )
    upd_ref[...] = whole

    lane1 = iota((1, LANES), 1)
    first = [jnp.where(lane1 == 0, value, 0.0) for value in answer]
    second = [jnp.where(lane1 == 1, value, 0.0) for value in answer]
    zeros = jnp.zeros((SIZE, LANES), F32)
    zero16 = jnp.zeros((16, LANES), F32)
    gap = [jnp.zeros((2, LANES), F32)]
    left = jnp.concatenate(picks + [(lanes128 < 2).astype(F32)], axis=1)
    right = jnp.concatenate(
        [
            jnp.concatenate([whole, zeros, zero16], axis=0),
            jnp.concatenate([zeros, whole, zero16], axis=0),
            jnp.concatenate([zeros, zeros] + first + gap + second + gap, axis=0),
        ],
        axis=1,
    )
    resp_ref[...] = dot(left, right, ((1,), (1,)))


def star_kernel(uv_ref, off_ref, diag_ref, corr_ref, count_ref, uvt_ref, where_ref, scale_ref, resp_ref,
                star_ref, det_ref, coeff, model):
    tiles = corr_ref.shape[0]
    rows128 = iota((LANES, LANES), 0)
    for c in range(2):
        count = (NCCD + 1 - c) // 2
        det_ref[pl.ds(c, count, stride=2), :] = resp_ref[0:count, 112 + 8 * c : 118 + 8 * c]
    turned = resp_ref[...].T
    dest = where_ref[0:1]
    copy_at = where_ref[1:2]
    ccd = where_ref[2:3]
    picks = [((rows128 == dest) & (copy_at == c)).astype(F32) for c in range(2)]
    picks += [(rows128 * 2 + c == ccd).astype(F32) for c in range(2)]
    exposure = dot(turned[0:56], picks[0], ((1,), (0,))) + dot(turned[56:112], picks[1], ((1,), (0,)))
    detector = dot(turned[112:120], picks[2], ((1,), (0,))) + dot(turned[120:128], picks[3], ((1,), (0,)))
    scale = scale_ref[...]
    coeff[0:28, :] = exposure[0:28] * scale[0:28]
    coeff[32:60, :] = exposure[28:56] * scale[0:28]
    for axis in range(2):
        for m, term in enumerate(((0, 0), (1, 0), (0, 1))):
            row = 32 * axis + TERM_INDEX[term]
            coeff[row : row + 1, :] = coeff[row : row + 1, :] + detector[3 * axis + m : 3 * axis + m + 1]

    def evaluate(g, carry):
        at = pl.ds(pl.multiple_of(g * 8, 8), 8)
        in_u = legendre(uvt_ref[0, at, :], ORDER + 1)
        in_v = legendre(uvt_ref[1, at, :], ORDER + 1)
        for axis in range(2):
            total = None
            for i in range(ORDER + 1):
                inner = None
                for j in range(ORDER - i + 1):
                    row = 32 * axis + TERM_INDEX[(i, j)]
                    term = coeff[row : row + 1, :]
                    if j:
                        term = term * in_v[j]
                    inner = term if inner is None else inner + term
                if i:
                    inner = inner * in_u[i]
                total = inner if total is None else total + inner
            model[axis, at, :] = total
        return carry

    lax.fori_loop(0, LANES // 8, evaluate, 0, unroll=2)
    model_x = model[0].T
    model_y = model[1].T
    weights, resid, inverse = star_terms(uv_ref, off_ref, diag_ref, corr_ref, count_ref)
    grad_x = None
    for visit in range(VISITS):
        w_xx, w_yy, w_xy = weights[visit]
        left_x = resid[visit][0] - model_x[visit * tiles : (visit + 1) * tiles]
        left_y = resid[visit][1] - model_y[visit * tiles : (visit + 1) * tiles]
        part_x = w_xx * left_x + w_xy * left_y
        part_y = w_xy * left_x + w_yy * left_y
        grad_x = part_x if grad_x is None else grad_x + part_x
        grad_y = part_y if visit == 0 else grad_y + part_y
    out_x, out_y = apply_inverse(inverse, grad_x, grad_y)
    star_ref[:, 0, :] = out_x
    star_ref[:, 1, :] = out_y


def vmem(count):
    return [pl.BlockSpec(memory_space=pltpu.VMEM)] * count


def shards(focal_uv, offsets, w_diag, w_corr, star_count, exposure_ids, ccd_ids, exp_slot):
    tiles = offsets.shape[0]
    flat = (tiles * VISITS * 2, LANES)
    stars = (
        focal_uv.reshape(flat),
        offsets.reshape(flat),
        w_diag.reshape(flat),
        w_corr,
        star_count.reshape(1, tiles),
    )
    shape = jax.ShapeDtypeStruct
    outgoing, turned, where = pl.pallas_call(
        moments_kernel,
        out_shape=(
            shape((LANES, 6, LANES), F32),
            shape((2, LANES, LANES), F32),
            shape((8, LANES), jnp.int32),
        ),
        in_specs=vmem(8),
        out_specs=tuple(vmem(3)),
        scratch_shapes=[
            pltpu.VMEM((7, LANES, LANES), F32),
            pltpu.VMEM((DEG2 + 1, LANES, LANES), F32),
            pltpu.VMEM((DEG2 + 1, LANES, LANES), F32),
            pltpu.VMEM((ROW_DET * 8, LANES), F32),
            pltpu.VMEM((ROW_DET, LANES), F32),
        ],
        name="moments",
    )(*stars, exposure_ids, ccd_ids, exp_slot.reshape(LANES, LANES))
    arrived = lax.all_to_all(outgoing, ("field", "shard"), 0, 0, tiled=True)
    scale = jnp.asarray(scale_rows())
    update, answers = pl.pallas_call(
        solve_kernel,
        out_shape=(shape((SIZE, LANES), F32), shape((LANES, LANES), F32)),
        in_specs=vmem(3),
        out_specs=tuple(vmem(2)),
        scratch_shapes=[
            pltpu.VMEM((ROWS, LANES), F32),
            pltpu.VMEM((POLY * 32, 3 * LANES), F32),
            pltpu.VMEM((SIZE * SIZE, LANES), F32),
            pltpu.VMEM((SIZE, LANES), F32),
            pltpu.VMEM((SIZE, LANES), F32),
        ],
        name="solve",
    )(arrived, jnp.asarray(expansion()), scale)
    replies = lax.all_to_all(answers.reshape(LANES, 1, LANES), ("field", "shard"), 0, 0, tiled=True)
    star_update, ccd_update = pl.pallas_call(
        star_kernel,
        out_shape=(shape((tiles, 2, LANES), F32), shape((NCCD, 6), F32)),
        in_specs=vmem(9),
        out_specs=tuple(vmem(2)),
        scratch_shapes=[pltpu.VMEM((64, LANES), F32), pltpu.VMEM((2, LANES, LANES), F32)],
        name="stars",
    )(*stars, turned, where, scale, replies.reshape(LANES, LANES))
    return star_update, update, ccd_update


def solution(mesh):
    both = ("field", "shard")
    in_specs = (
        P(both, None, None, None),
        P(both, None, None, None),
        P(both, None, None, None),
        P(both, None, None),
        P(both),
        P(both, None),
        P(both, None),
        P(),
    )
    out_specs = (P(both, None, None), P(None, both), P())
    return jax.shard_map(shards, mesh=mesh, in_specs=in_specs, out_specs=out_specs, check_vma=False)
```

```python
import math

import jax
import jax.numpy as jnp
import numpy as np
from jax import lax
from jax.experimental import pallas as pl
from jax.experimental.pallas import tpu as pltpu
from jax.sharding import PartitionSpec as P

ORDER = 6
POLY = 28
VISITS = 6
NCCD = 189
LANES = 128
STAR_DAMP = 0.1
EXPOSURE_DAMP = 1.0
DETECTOR_DAMP = 1.0
HIGH = lax.Precision.HIGHEST
DEG2 = 2 * ORDER
F32 = jnp.float32

TERMS = [(i, n - i) for n in range(DEG2 + 1) for i in range(n + 1)]
TERM_INDEX = {term: at for at, term in enumerate(TERMS)}
SCALE = [math.sqrt((2 * i + 1) * (2 * j + 1)) for i, j in TERMS[:POLY]]

ROW_GX = 288
ROW_GY = 320
ROW_DET = 352
ROWS = 384
MARK = 95


def linearisation():
    from numpy.polynomial import legendre

    table = np.zeros((ORDER + 1, ORDER + 1, DEG2 + 1))
    for m in range(ORDER + 1):
        for n in range(ORDER + 1):
            product = legendre.legmul([0] * m + [1], [0] * n + [1])
            table[m, n, : len(product)] = product
    return table


def expansion():
    table = linearisation()
    matrix = np.zeros((POLY * 32, 96))
    for q, (iq, jq) in enumerate(TERMS[:POLY]):
        for p, (ip, jp) in enumerate(TERMS[:POLY]):
            for at, (a, b) in enumerate(TERMS):
                matrix[q * 32 + p, at] = SCALE[p] * SCALE[q] * table[ip, iq, a] * table[jp, jq, b]
    return matrix.astype(np.float32)


def scale_rows():
    rows = np.zeros((32, LANES), np.float32)
    rows[:POLY] = np.array(SCALE, np.float32)[:, None]
    return rows


def dot(a, b, dims):
    return lax.dot_general(a, b, (dims, ((), ())), precision=HIGH, preferred_element_type=F32)


def rows_of(part):
    return pl.ds(part, LANES, stride=6)


def iota(shape, axis):
    return lax.broadcasted_iota(jnp.int32, shape, axis)


def legendre(value, count):
    values = [None, value]
    for degree in range(1, count - 1):
        lower = (degree / (degree + 1)) * (values[degree - 1] if degree > 1 else 1.0)
        values.append(((2 * degree + 1) / (degree + 1)) * value * values[degree] - lower)
    return values


def star_terms(off_ref, diag_ref, corr_ref, counts):
    tiles = corr_ref.shape[1]
    lanes = iota((tiles, LANES), 1)
    counts = jnp.broadcast_to(counts.astype(F32), (tiles, tiles))
    square = (iota((tiles, tiles), 0) == iota((tiles, tiles), 1)).astype(F32)
    column = jnp.sum(counts * square, axis=1, keepdims=True)
    present = (lanes.astype(F32) < column).astype(F32)

    def rows(ref, visit, part):
        return ref[pl.ds(2 * visit + part, tiles, stride=2 * VISITS), :]

    weights = []
    resid = []
    for visit in range(VISITS):
        d0 = rows(diag_ref, visit, 0)
        d1 = rows(diag_ref, visit, 1)
        weights.append((d0 * present, d1 * present, corr_ref[visit] * jnp.sqrt(d0 * d1) * present))
        resid.append((rows(off_ref, visit, 0), rows(off_ref, visit, 1)))
    hess_xx = sum(w[0] for w in weights) + STAR_DAMP
    hess_yy = sum(w[1] for w in weights) + STAR_DAMP
    hess_xy = sum(w[2] for w in weights)
    determ = hess_xx * hess_yy - hess_xy * hess_xy
    inverse = (hess_yy / determ, hess_xx / determ, -hess_xy / determ)
    return weights, resid, inverse


def apply_inverse(inverse, x, y):
    inv_xx, inv_yy, inv_xy = inverse
    return inv_xx * x + inv_xy * y, inv_xy * x + inv_yy * y


def combine(values, sub):
    for shift in (4, 2, 1):
        low = (sub & shift) == 0
        half = len(values) // 2
        merged = []
        for at in range(half):
            a, b = values[at], values[at + half]
            if shift == 4:
                merged.append(jnp.where(low, a, b) + pltpu.roll(jnp.where(low, b, a), 4, 0))
            else:
                merged.append(jnp.where(low, a + pltpu.roll(a, 8 - shift, 0), b + pltpu.roll(b, shift, 0)))
        values = merged
    return values[0]


def transpose8(values, sub):
    values = list(values)
    for shift in (4, 2, 1):
        low = (sub & shift) == 0
        for at in range(8):
            if at & shift:
                continue
            a, b = values[at], values[at + shift]
            values[at] = jnp.where(low, a, pltpu.roll(b, shift, 0))
            values[at + shift] = jnp.where(low, pltpu.roll(a, 8 - shift, 0), b)
    return values


def moments_kernel(*refs):
    sources, out_refs, buffers, (sems, *scratch) = refs[:8], refs[8:11], refs[11:19], refs[19:]
    copies = [
        pltpu.make_async_copy(source, buffer, sems.at[at])
        for at, (source, buffer) in enumerate(zip(sources, buffers))
    ]
    for copy in copies:
        copy.start()
    for copy in copies:
        copy.wait()
    moments_body(*buffers, *out_refs, *scratch)


def moments_body(uv_ref, off_ref, diag_ref, corr_ref, count_ref, ids_ref, ccd_ref, slot_ref,
                 out_ref, uvt_ref, where_ref, chan, pu, pv, acc, mom):
    tiles = corr_ref.shape[1]
    visits_all = tiles * VISITS
    sub8 = iota((8, LANES), 0)

    pad = jnp.zeros((LANES - visits_all, LANES), F32)
    mine = iota((VISITS, LANES), 1) // tiles == iota((VISITS, LANES), 0)

    def along_lanes(ref):
        spread = jnp.concatenate([ref[...]] * (LANES // tiles), axis=1)
        return jnp.sum(jnp.where(mine, spread, 0), axis=0, keepdims=True)

    ident = along_lanes(ids_ref)
    ccd = along_lanes(ccd_ref)
    rows128 = iota((LANES, LANES), 0)
    lanes128 = iota((LANES, LANES), 1)
    valid = iota((1, LANES), 1) < visits_all
    picked = dot(slot_ref[...].astype(F32), (rows128 == ident // LANES).astype(F32), ((0,), (0,)))
    position = jnp.sum(jnp.where(rows128 == ident % LANES, picked, 0.0), axis=0, keepdims=True)
    position = (position + 0.5).astype(jnp.int32)
    dest = jnp.where(valid, position // LANES, -1)
    ccd = jnp.where(valid, ccd, -1)
    dest_t = jnp.broadcast_to(dest.astype(F32), (LANES, LANES)).T.astype(jnp.int32)
    same = (dest_t == dest) & (rows128 < lanes128)
    copy_at = jnp.sum(same.astype(F32), axis=0, keepdims=True).astype(jnp.int32)
    mark = (position % LANES + 1).astype(F32)
    counts = jnp.concatenate([count_ref[...]] * (LANES // tiles), axis=1)
    where_ref[...] = jnp.where(
        sub8 == 0, dest, jnp.where(sub8 == 1, copy_at, jnp.where(sub8 == 2, ccd, counts))
    )

    weights, resid, inverse = star_terms(off_ref, diag_ref, corr_ref, count_ref[...])
    grad_x = sum(w[0] * r[0] + w[2] * r[1] for w, r in zip(weights, resid))
    grad_y = sum(w[2] * r[0] + w[1] * r[1] for w, r in zip(weights, resid))
    shift_x, shift_y = apply_inverse(inverse, grad_x, grad_y)
    inv_xx, inv_yy, inv_xy = inverse
    channels = [[] for _ in range(7)]
    for visit in range(VISITS):
        w_xx, w_yy, w_xy = weights[visit]
        left_x = resid[visit][0] - shift_x
        left_y = resid[visit][1] - shift_y
        prod_11 = inv_xx * w_xx + inv_xy * w_xy
        prod_12 = inv_xx * w_xy + inv_xy * w_yy
        prod_21 = inv_xy * w_xx + inv_yy * w_xy
        prod_22 = inv_xy * w_xy + inv_yy * w_yy
        values = (
            uv_ref[pl.ds(2 * visit, tiles, stride=2 * VISITS), :],
            uv_ref[pl.ds(2 * visit + 1, tiles, stride=2 * VISITS), :],
            w_xx - (w_xx * prod_11 + w_xy * prod_21),
            w_yy - (w_xy * prod_12 + w_yy * prod_22),
            w_xy - (w_xx * prod_12 + w_xy * prod_22),
            w_xx * left_x + w_xy * left_y,
            w_xy * left_x + w_yy * left_y,
        )
        for at, value in enumerate(values):
            channels[at].append(value)
    for at in range(7):
        chan[at] = jnp.concatenate(channels[at] + [pad], axis=0).T
    uvt_ref[0] = chan[0]
    uvt_ref[1] = chan[1]

    groups = LANES // 8

    def tables(g, carry):
        at = pl.ds(pl.multiple_of(g * 8, 8), 8)
        for ref, source in ((pu, 0), (pv, 1)):
            for degree, value in enumerate(legendre(chan[source, at, :], DEG2 + 1)):
                if degree:
                    ref[degree, at, :] = value
        return carry

    lax.fori_loop(0, groups, tables, 0)

    def sweep(i, top, first, count, row0, width):
        heights = top - i + 1

        def step(g, carry):
            at = pl.ds(pl.multiple_of(g * 8, 8), 8)
            scaled = [chan[first + w, at, :] for w in range(count)]
            if i:
                factor = pu[i, at, :]
                scaled = [value * factor for value in scaled]
            new = []
            for j in range(heights):
                other = pv[j, at, :] if j else None
                for w in range(count):
                    term = scaled[w] * other if j else scaled[w]
                    new.append(carry[j * count + w] + term)
            return tuple(new)

        start = tuple(jnp.zeros((8, LANES), F32) for _ in range(heights * count))
        sums = lax.fori_loop(0, groups, step, start, unroll=2)
        for j in range(heights):
            for w in range(count):
                row = row0 + w * width + TERM_INDEX[(i, j)]
                acc[pl.ds(row * 8, 8), :] = sums[j * count + w]

    for i in range(DEG2 + 1):
        sweep(i, DEG2, 2, 3, 0, 96)
    for i in range(ORDER + 1):
        sweep(i, ORDER, 5, 2, ROW_GX, 32)
    zero = jnp.zeros((8, LANES), F32)
    for block in range(3):
        for row in range(len(TERMS), 96):
            acc[pl.ds((block * 96 + row) * 8, 8), :] = zero
    for block in range(2):
        for row in range(POLY, 32):
            acc[pl.ds((ROW_GX + block * 32 + row) * 8, 8), :] = zero

    def reduce_rows(g, carry):
        base = pl.multiple_of(g * 64, 64)
        mom[pl.ds(pl.multiple_of(g * 8, 8), 8), :] = combine(
            [acc[pl.ds(base + 8 * s, 8), :] for s in range(8)], sub8
        )
        return carry

    lax.fori_loop(0, ROW_DET // 8, reduce_rows, 0, unroll=2)
    mom[88:96, :] = jnp.where(sub8 == 7, mark, mom[88:96, :])

    zeros96 = jnp.zeros((96, LANES), F32)
    pulls = jnp.where(sub8 < 4, mom[ROW_GX : ROW_GX + 8], pltpu.roll(mom[ROW_GY : ROW_GY + 8], 4, 0))
    last = jnp.concatenate(
        [
            jnp.concatenate([mom[256:352], jnp.zeros((32, LANES), F32)], axis=0),
            jnp.concatenate([zeros96, mom[0:8], mom[96:104], mom[192:200], pulls], axis=0),
        ],
        axis=1,
    )
    for copy in range(2):
        place = ((rows128 == dest) & (copy_at == copy)).astype(F32)
        place_det = (rows128 + LANES * copy == ccd).astype(F32)
        out_ref[rows_of(3 * copy), :] = dot(place, mom[0:128], ((1,), (1,)))
        out_ref[rows_of(3 * copy + 1), :] = dot(place, mom[128:256], ((1,), (1,)))
        out_ref[rows_of(3 * copy + 2), :] = dot(
            jnp.concatenate([place, place_det], axis=1), last, ((1,), (1,))
        )


def detector_solve(table):
    def moment(block, i, j):
        return table[8 * block + TERM_INDEX[(i, j)] : 8 * block + TERM_INDEX[(i, j)] + 1]

    def block_of(block):
        one, u, v = moment(block, 0, 0), moment(block, 1, 0), moment(block, 0, 1)
        uu = (2.0 * moment(block, 2, 0) + one) * (1.0 / 3.0)
        vv = (2.0 * moment(block, 0, 2) + one) * (1.0 / 3.0)
        uv = moment(block, 1, 1)
        return [[one, u, v], [u, uu, uv], [v, uv, vv]]

    part_xx, part_yy, part_xy = block_of(0), block_of(1), block_of(2)
    matrix = [part_xx[p] + part_xy[p] for p in range(3)] + [part_xy[p] + part_yy[p] for p in range(3)]
    at = [TERM_INDEX[term] for term in ((0, 0), (1, 0), (0, 1))]
    rhs = [table[24 + a : 25 + a] for a in at] + [table[28 + a : 29 + a] for a in at]
    for p in range(6):
        matrix[p][p] = matrix[p][p] + DETECTOR_DAMP
    inverse = [None] * 6
    lower = [[None] * 6 for _ in range(6)]
    for step in range(6):
        pivot = matrix[step][step]
        for before in range(step):
            pivot = pivot - lower[step][before] * lower[step][before]
        inverse[step] = 1.0 / jnp.sqrt(pivot)
        for row in range(step + 1, 6):
            value = matrix[row][step]
            for before in range(step):
                value = value - lower[row][before] * lower[step][before]
            lower[row][step] = value * inverse[step]
    forward = []
    for step in range(6):
        value = rhs[step]
        for before in range(step):
            value = value - lower[step][before] * forward[before]
        forward.append(value * inverse[step])
    answer = [None] * 6
    for step in range(5, -1, -1):
        value = forward[step]
        for after in range(step + 1, 6):
            value = value - lower[after][step] * answer[after]
        answer[step] = value * inverse[step]
    return answer


UNKNOWNS = [("x", q) for q in range(28)] + [("y", q) for q in range(24, 28)] + [("y", q) for q in range(24)]
SIZE = 2 * POLY
BLOCKS = SIZE // 8
PANEL = 4


def solve_kernel(arr_ref, expand_ref, scale_ref, upd_ref, resp_ref, table, wide, mat, rhs, invs):
    sub8 = iota((8, LANES), 0)
    rows128 = iota((LANES, LANES), 0)
    lanes128 = iota((LANES, LANES), 1)

    picks = []
    for copy in range(2):
        column = arr_ref[rows_of(3 * copy), :][:, MARK : MARK + 1]
        picks.append((column.astype(jnp.int32) == lanes128 + 1).astype(F32))
    pick = jnp.concatenate(picks, axis=0)
    for block in range(3):
        both = jnp.concatenate([arr_ref[rows_of(block), :], arr_ref[rows_of(3 + block), :]], axis=0)
        table[pl.ds(block * LANES, LANES), :] = dot(both, pick, ((0,), (0,)))

    sums = [jnp.sum(arr_ref[rows_of(3 * copy + 2), :], axis=0, keepdims=True) for copy in range(2)]
    turned = jnp.where(rows128 == 0, sums[0], jnp.where(rows128 == 1, sums[1], 0.0)).T
    answer = detector_solve(turned[96:128])

    moments = jnp.concatenate([table[0:96], table[96:192], table[192:288]], axis=1)
    chunk = 224
    for at in range(0, POLY * 32, chunk):
        wide[pl.ds(at, chunk), :] = dot(expand_ref[pl.ds(at, chunk), :], moments, ((1,), (0,)))

    def part(which, q, group):
        return wide[q * 32 + group * 8 : q * 32 + group * 8 + 8, which * LANES : (which + 1) * LANES]

    for col, (kind, q) in enumerate(UNKNOWNS):
        for group in range(col // 8, BLOCKS):
            if kind == "x":
                if group < 3:
                    value = part(0, q, group)
                elif group == 3:
                    value = jnp.where(sub8 < 4, part(0, q, 3), pltpu.roll(part(2, q, 3), 4, 0))
                else:
                    value = part(2, q, group - 4)
            elif group == 3:
                value = jnp.where(sub8 < 4, 0.0, pltpu.roll(part(1, q, 3), 4, 0))
            else:
                value = part(1, q, group - 4)
            if group == col // 8:
                value = value + jnp.where(sub8 == col % 8, EXPOSURE_DAMP, 0.0)
            mat[pl.ds(col * SIZE + group * 8, 8), :] = value
    grad_x = table[ROW_GX : ROW_GX + 32] * scale_ref[...]
    grad_y = table[ROW_GY : ROW_GY + 32] * scale_ref[...]
    rhs[0:24, :] = grad_x[0:24]
    rhs[24:32, :] = jnp.where(sub8 < 4, grad_x[24:32], pltpu.roll(grad_y[24:32], 4, 0))
    rhs[32:56, :] = grad_y[0:24]

    for k0 in range(0, SIZE, PANEL):
        g0 = k0 // 8
        count = BLOCKS - g0

        def update(j, carry):
            base = j * SIZE
            column = [mat[pl.ds(pl.multiple_of(base + g * 8, 8), 8), :] for g in range(g0, BLOCKS)]
            new = []
            for c in range(PANEL):
                factor = mat[pl.ds(base + k0 + c, 1), :]
                for g in range(count):
                    new.append(carry[c * count + g] - column[g] * factor)
            return tuple(new)

        panel = tuple(
            mat[pl.ds((k0 + c) * SIZE + g * 8, 8), :] for c in range(PANEL) for g in range(g0, BLOCKS)
        )
        if k0:
            panel = lax.fori_loop(0, k0, update, panel, unroll=4)
        panel = [list(panel[c * count : (c + 1) * count]) for c in range(PANEL)]
        right = [rhs[pl.ds(g * 8, 8), :] for g in range(g0, BLOCKS)]
        for c in range(PANEL):
            k = k0 + c
            row = k % 8
            inverse = lax.rsqrt(panel[c][0][row : row + 1])
            column = [value * inverse for value in panel[c]]
            for other in range(c + 1, PANEL):
                factor = column[0][k0 % 8 + other : k0 % 8 + other + 1]
                panel[other] = [panel[other][g] - column[g] * factor for g in range(count)]
            forward = right[0][row : row + 1] * inverse
            keep = jnp.where(sub8 <= row, right[0], right[0] - column[0] * forward)
            keep = jnp.where(sub8 == row, forward, keep)
            right = [keep] + [right[g] - column[g] * forward for g in range(1, count)]
            invs[k : k + 1, :] = inverse
            for g in range(count):
                mat[pl.ds(k * SIZE + (g0 + g) * 8, 8), :] = column[g]
        for g in range(count):
            rhs[pl.ds((g0 + g) * 8, 8), :] = right[g]

    solved = [None] * BLOCKS
    for b in range(BLOCKS - 1, -1, -1):
        right = rhs[b * 8 : b * 8 + 8]
        if b < BLOCKS - 1:
            partial = []
            for c in range(8):
                total = None
                for g in range(b + 1, BLOCKS):
                    term = mat[pl.ds((b * 8 + c) * SIZE + g * 8, 8), :] * solved[g]
                    total = term if total is None else total + term
                partial.append(total)
            right = right - combine(partial, sub8)
        diagonal = transpose8([mat[pl.ds((b * 8 + c) * SIZE + b * 8, 8), :] for c in range(8)], sub8)
        for c in range(7, -1, -1):
            value = right[c : c + 1] * invs[b * 8 + c : b * 8 + c + 1]
            right = jnp.where(sub8 < c, right - diagonal[c] * value, jnp.where(sub8 == c, value, right))
        solved[b] = right
    whole = jnp.concatenate(
        solved[0:3] + [solved[3][0:4]] + solved[4:7] + [solved[3][4:8]], axis=0
    )
    upd_ref[...] = whole

    lane1 = iota((1, LANES), 1)
    first = [jnp.where(lane1 == 0, value, 0.0) for value in answer]
    second = [jnp.where(lane1 == 1, value, 0.0) for value in answer]
    zeros = jnp.zeros((SIZE, LANES), F32)
    zero16 = jnp.zeros((16, LANES), F32)
    gap = [jnp.zeros((2, LANES), F32)]
    left = jnp.concatenate(picks + [(lanes128 < 2).astype(F32)], axis=1)
    right = jnp.concatenate(
        [
            jnp.concatenate([whole, zeros, zero16], axis=0),
            jnp.concatenate([zeros, whole, zero16], axis=0),
            jnp.concatenate([zeros, zeros] + first + gap + second + gap, axis=0),
        ],
        axis=1,
    )
    resp_ref[...] = dot(left, right, ((1,), (1,)))


def star_kernel(off_ref, diag_ref, corr_ref, uvt_ref, where_ref, scale_ref, resp_ref,
                star_ref, det_ref, coeff, model):
    tiles = corr_ref.shape[1]
    rows128 = iota((LANES, LANES), 0)
    turned = resp_ref[...].T
    det_ref[:, 0:LANES] = turned[112:118]
    det_ref[:, LANES:NCCD] = turned[120:126, 0 : NCCD - LANES]
    dest = where_ref[0:1]
    copy_at = where_ref[1:2]
    ccd = where_ref[2:3]
    picks = [((rows128 == dest) & (copy_at == c)).astype(F32) for c in range(2)]
    picks += [(rows128 + LANES * c == ccd).astype(F32) for c in range(2)]
    exposure = dot(turned[0:56], picks[0], ((1,), (0,))) + dot(turned[56:112], picks[1], ((1,), (0,)))
    detector = dot(turned[112:120], picks[2], ((1,), (0,))) + dot(turned[120:128], picks[3], ((1,), (0,)))
    scale = scale_ref[...]
    coeff[0:28, :] = exposure[0:28] * scale[0:28]
    coeff[32:60, :] = exposure[28:56] * scale[0:28]
    for axis in range(2):
        for m, term in enumerate(((0, 0), (1, 0), (0, 1))):
            row = 32 * axis + TERM_INDEX[term]
            coeff[row : row + 1, :] = coeff[row : row + 1, :] + detector[3 * axis + m : 3 * axis + m + 1]

    def evaluate(g, carry):
        at = pl.ds(pl.multiple_of(g * 8, 8), 8)
        in_u = legendre(uvt_ref[0, at, :], ORDER + 1)
        in_v = legendre(uvt_ref[1, at, :], ORDER + 1)
        for axis in range(2):
            total = None
            for i in range(ORDER + 1):
                inner = None
                for j in range(ORDER - i + 1):
                    row = 32 * axis + TERM_INDEX[(i, j)]
                    term = coeff[row : row + 1, :]
                    if j:
                        term = term * in_v[j]
                    inner = term if inner is None else inner + term
                if i:
                    inner = inner * in_u[i]
                total = inner if total is None else total + inner
            model[axis, at, :] = total
        return carry

    lax.fori_loop(0, LANES // 8, evaluate, 0, unroll=2)
    model_x = model[0].T
    model_y = model[1].T
    weights, resid, inverse = star_terms(off_ref, diag_ref, corr_ref, where_ref[3:4, 0:tiles])
    grad_x = None
    for visit in range(VISITS):
        w_xx, w_yy, w_xy = weights[visit]
        left_x = resid[visit][0] - model_x[visit * tiles : (visit + 1) * tiles]
        left_y = resid[visit][1] - model_y[visit * tiles : (visit + 1) * tiles]
        part_x = w_xx * left_x + w_xy * left_y
        part_y = w_xy * left_x + w_yy * left_y
        grad_x = part_x if grad_x is None else grad_x + part_x
        grad_y = part_y if visit == 0 else grad_y + part_y
    out_x, out_y = apply_inverse(inverse, grad_x, grad_y)
    star_ref[:, 0, :] = out_x
    star_ref[:, 1, :] = out_y


def vmem(count):
    return [pl.BlockSpec(memory_space=pltpu.VMEM)] * count


def shards(focal_uv, offsets, w_diag, w_corr, star_count, exposure_ids, ccd_ids, exp_slot):
    tiles = offsets.shape[0]
    flat = (tiles * VISITS * 2, LANES)
    inputs = (
        focal_uv.reshape(flat),
        offsets.reshape(flat),
        w_diag.reshape(flat),
        jnp.transpose(w_corr, (1, 0, 2)),
        star_count.reshape(1, tiles),
        exposure_ids.T,
        ccd_ids.T,
        exp_slot.reshape(LANES, LANES),
    )
    shape = jax.ShapeDtypeStruct
    outgoing, turned, where = pl.pallas_call(
        moments_kernel,
        out_shape=(
            shape((6 * LANES, LANES), F32),
            shape((2, LANES, LANES), F32),
            shape((8, LANES), jnp.int32),
        ),
        in_specs=[pl.BlockSpec(memory_space=pltpu.HBM)] * 8,
        out_specs=tuple(vmem(3)),
        scratch_shapes=[pltpu.VMEM(array.shape, array.dtype) for array in inputs]
        + [
            pltpu.SemaphoreType.DMA((8,)),
            pltpu.VMEM((7, LANES, LANES), F32),
            pltpu.VMEM((DEG2 + 1, LANES, LANES), F32),
            pltpu.VMEM((DEG2 + 1, LANES, LANES), F32),
            pltpu.VMEM((ROW_DET * 8, LANES), F32),
            pltpu.VMEM((ROW_DET, LANES), F32),
        ],
        compiler_params=pltpu.CompilerParams(vmem_limit_bytes=12 << 20),
        name="moments",
    )(*(pltpu.with_memory_space_constraint(array, pltpu.HBM) for array in inputs))
    arrived = lax.all_to_all(outgoing.reshape(LANES, 1, 6 * LANES), ("field", "shard"), 0, 0, tiled=True)
    arrived = arrived.reshape(6 * LANES, LANES)
    scale = jnp.asarray(scale_rows())
    update, answers = pl.pallas_call(
        solve_kernel,
        out_shape=(shape((SIZE, LANES), F32), shape((LANES, LANES), F32)),
        in_specs=vmem(3),
        out_specs=tuple(vmem(2)),
        scratch_shapes=[
            pltpu.VMEM((ROWS, LANES), F32),
            pltpu.VMEM((POLY * 32, 3 * LANES), F32),
            pltpu.VMEM((SIZE * SIZE, LANES), F32),
            pltpu.VMEM((SIZE, LANES), F32),
            pltpu.VMEM((SIZE, LANES), F32),
        ],
        compiler_params=pltpu.CompilerParams(vmem_limit_bytes=12 << 20),
        name="solve",
    )(arrived, jnp.asarray(expansion()), scale)
    replies = lax.all_to_all(answers.reshape(LANES, 1, LANES), ("field", "shard"), 0, 0, tiled=True)
    star_update, ccd_update = pl.pallas_call(
        star_kernel,
        out_shape=(shape((tiles, 2, LANES), F32), shape((6, NCCD), F32)),
        in_specs=vmem(7),
        out_specs=tuple(vmem(2)),
        scratch_shapes=[pltpu.VMEM((64, LANES), F32), pltpu.VMEM((2, LANES, LANES), F32)],
        compiler_params=pltpu.CompilerParams(vmem_limit_bytes=12 << 20),
        name="stars",
    )(*inputs[1:4], turned, where, scale, replies.reshape(LANES, LANES))
    return star_update, update, ccd_update.T


def solution(mesh):
    both = ("field", "shard")
    in_specs = (
        P(both, None, None, None),
        P(both, None, None, None),
        P(both, None, None, None),
        P(both, None, None),
        P(both),
        P(both, None),
        P(both, None),
        P(),
    )
    out_specs = (P(both, None, None), P(None, both), P())
    return jax.shard_map(shards, mesh=mesh, in_specs=in_specs, out_specs=out_specs, check_vma=False)
```

```python
import math

import jax
import jax.numpy as jnp
import numpy as np
from jax import lax
from jax.experimental import pallas as pl
from jax.experimental.pallas import tpu as pltpu
from jax.sharding import PartitionSpec as P

ORDER = 6
POLY = 28
VISITS = 6
NCCD = 189
LANES = 128
STAR_DAMP = 0.1
EXPOSURE_DAMP = 1.0
DETECTOR_DAMP = 1.0
HIGH = lax.Precision.HIGHEST
DEG2 = 2 * ORDER
F32 = jnp.float32

TERMS = [(i, n - i) for n in range(DEG2 + 1) for i in range(n + 1)]
TERM_INDEX = {term: at for at, term in enumerate(TERMS)}
SCALE = [math.sqrt((2 * i + 1) * (2 * j + 1)) for i, j in TERMS[:POLY]]

ROW_GX = 288
ROW_GY = 320
ROW_DET = 352
ROWS = 384
MARK = 95


def linearisation():
    from numpy.polynomial import legendre

    table = np.zeros((ORDER + 1, ORDER + 1, DEG2 + 1))
    for m in range(ORDER + 1):
        for n in range(ORDER + 1):
            product = legendre.legmul([0] * m + [1], [0] * n + [1])
            table[m, n, : len(product)] = product
    return table


def expansion():
    table = linearisation()
    matrix = np.zeros((POLY * 32, 96))
    for q, (iq, jq) in enumerate(TERMS[:POLY]):
        for p, (ip, jp) in enumerate(TERMS[:POLY]):
            for at, (a, b) in enumerate(TERMS):
                matrix[q * 32 + p, at] = SCALE[p] * SCALE[q] * table[ip, iq, a] * table[jp, jq, b]
    parts = []
    rest = matrix
    for _ in range(3):
        part = rest.astype(jnp.bfloat16)
        parts.append(part)
        rest = rest - part.astype(np.float64)
    high, middle, low = parts
    return np.stack([np.concatenate(pair, 1) for pair in ((high, high), (middle, middle), (high, low))])


def scale_rows():
    rows = np.zeros((32, LANES), np.float32)
    rows[:POLY] = np.array(SCALE, np.float32)[:, None]
    return rows


def dot(a, b, dims):
    return lax.dot_general(a, b, (dims, ((), ())), precision=HIGH, preferred_element_type=F32)


def split3(value):
    high = value.astype(jnp.bfloat16)
    rest = value - high.astype(F32)
    middle = rest.astype(jnp.bfloat16)
    return high, middle, (rest - middle.astype(F32)).astype(jnp.bfloat16)


def dot16(a, b, dims):
    return lax.dot_general(a, b, (dims, ((), ())), preferred_element_type=F32)


def rows_of(part):
    return pl.ds(part, LANES, stride=6)


def iota(shape, axis):
    return lax.broadcasted_iota(jnp.int32, shape, axis)


def legendre(value, count):
    values = [None, value]
    for degree in range(1, count - 1):
        lower = (degree / (degree + 1)) * (values[degree - 1] if degree > 1 else 1.0)
        values.append(((2 * degree + 1) / (degree + 1)) * value * values[degree] - lower)
    return values


def star_terms(off_ref, diag_ref, corr_ref, counts):
    tiles = corr_ref.shape[1]
    lanes = iota((tiles, LANES), 1)
    counts = jnp.broadcast_to(counts.astype(F32), (tiles, tiles))
    square = (iota((tiles, tiles), 0) == iota((tiles, tiles), 1)).astype(F32)
    column = jnp.sum(counts * square, axis=1, keepdims=True)
    present = (lanes.astype(F32) < column).astype(F32)

    def rows(ref, visit, part):
        return ref[pl.ds(2 * visit + part, tiles, stride=2 * VISITS), :]

    weights = []
    resid = []
    for visit in range(VISITS):
        d0 = rows(diag_ref, visit, 0)
        d1 = rows(diag_ref, visit, 1)
        weights.append((d0 * present, d1 * present, corr_ref[visit] * jnp.sqrt(d0 * d1) * present))
        resid.append((rows(off_ref, visit, 0), rows(off_ref, visit, 1)))
    hess_xx = sum(w[0] for w in weights) + STAR_DAMP
    hess_yy = sum(w[1] for w in weights) + STAR_DAMP
    hess_xy = sum(w[2] for w in weights)
    determ = hess_xx * hess_yy - hess_xy * hess_xy
    inverse = (hess_yy / determ, hess_xx / determ, -hess_xy / determ)
    return weights, resid, inverse


def apply_inverse(inverse, x, y):
    inv_xx, inv_yy, inv_xy = inverse
    return inv_xx * x + inv_xy * y, inv_xy * x + inv_yy * y


def combine(values, sub):
    for shift in (4, 2, 1):
        low = (sub & shift) == 0
        half = len(values) // 2
        merged = []
        for at in range(half):
            a, b = values[at], values[at + half]
            if shift == 4:
                merged.append(jnp.where(low, a, b) + pltpu.roll(jnp.where(low, b, a), 4, 0))
            else:
                merged.append(jnp.where(low, a + pltpu.roll(a, 8 - shift, 0), b + pltpu.roll(b, shift, 0)))
        values = merged
    return values[0]


def transpose8(values, sub):
    values = list(values)
    for shift in (4, 2, 1):
        low = (sub & shift) == 0
        for at in range(8):
            if at & shift:
                continue
            a, b = values[at], values[at + shift]
            values[at] = jnp.where(low, a, pltpu.roll(b, shift, 0))
            values[at + shift] = jnp.where(low, pltpu.roll(a, 8 - shift, 0), b)
    return values


def moments_kernel(*refs):
    sources, out_refs, buffers, (sems, *scratch) = refs[:10], refs[10:15], refs[15:23], refs[23:]
    copies = [
        pltpu.make_async_copy(source, buffer, sems.at[at])
        for at, (source, buffer) in enumerate(zip(sources, (*buffers, *out_refs[3:])))
    ]
    for copy in copies:
        copy.start()
    for copy in copies[:8]:
        copy.wait()
    moments_body(*buffers, *out_refs[:3], *scratch)
    for copy in copies[8:]:
        copy.wait()


def moments_body(uv_ref, off_ref, diag_ref, corr_ref, count_ref, ids_ref, ccd_ref, slot_ref,
                 out_ref, uvt_ref, where_ref, chan, pu, pv, acc, mom):
    tiles = corr_ref.shape[1]
    visits_all = tiles * VISITS
    sub8 = iota((8, LANES), 0)

    pad = jnp.zeros((LANES - visits_all, LANES), F32)
    mine = iota((VISITS, LANES), 1) // tiles == iota((VISITS, LANES), 0)

    def along_lanes(ref):
        spread = jnp.concatenate([ref[...]] * (LANES // tiles), axis=1)
        return jnp.sum(jnp.where(mine, spread, 0), axis=0, keepdims=True)

    ident = along_lanes(ids_ref)
    ccd = along_lanes(ccd_ref)
    rows128 = iota((LANES, LANES), 0)
    lanes128 = iota((LANES, LANES), 1)
    valid = iota((1, LANES), 1) < visits_all
    picked = dot(slot_ref[...].astype(F32), (rows128 == ident // LANES).astype(F32), ((0,), (0,)))
    position = jnp.sum(jnp.where(rows128 == ident % LANES, picked, 0.0), axis=0, keepdims=True)
    position = (position + 0.5).astype(jnp.int32)
    dest = jnp.where(valid, position // LANES, -1)
    ccd = jnp.where(valid, ccd, -1)
    dest_t = jnp.broadcast_to(dest.astype(F32), (LANES, LANES)).T.astype(jnp.int32)
    same = (dest_t == dest) & (rows128 < lanes128)
    copy_at = jnp.sum(same.astype(F32), axis=0, keepdims=True).astype(jnp.int32)
    mark = (position % LANES + 1).astype(F32)
    counts = jnp.concatenate([count_ref[...]] * (LANES // tiles), axis=1)
    where_ref[...] = jnp.where(
        sub8 == 0, dest, jnp.where(sub8 == 1, copy_at, jnp.where(sub8 == 2, ccd, counts))
    )

    weights, resid, inverse = star_terms(off_ref, diag_ref, corr_ref, count_ref[...])
    grad_x = sum(w[0] * r[0] + w[2] * r[1] for w, r in zip(weights, resid))
    grad_y = sum(w[2] * r[0] + w[1] * r[1] for w, r in zip(weights, resid))
    shift_x, shift_y = apply_inverse(inverse, grad_x, grad_y)
    inv_xx, inv_yy, inv_xy = inverse
    channels = [[] for _ in range(7)]
    for visit in range(VISITS):
        w_xx, w_yy, w_xy = weights[visit]
        left_x = resid[visit][0] - shift_x
        left_y = resid[visit][1] - shift_y
        prod_11 = inv_xx * w_xx + inv_xy * w_xy
        prod_12 = inv_xx * w_xy + inv_xy * w_yy
        prod_21 = inv_xy * w_xx + inv_yy * w_xy
        prod_22 = inv_xy * w_xy + inv_yy * w_yy
        values = (
            uv_ref[pl.ds(2 * visit, tiles, stride=2 * VISITS), :],
            uv_ref[pl.ds(2 * visit + 1, tiles, stride=2 * VISITS), :],
            w_xx - (w_xx * prod_11 + w_xy * prod_21),
            w_yy - (w_xy * prod_12 + w_yy * prod_22),
            w_xy - (w_xx * prod_12 + w_xy * prod_22),
            w_xx * left_x + w_xy * left_y,
            w_xy * left_x + w_yy * left_y,
        )
        for at, value in enumerate(values):
            channels[at].append(value)
    for at in range(7):
        chan[at] = jnp.concatenate(channels[at] + [pad], axis=0).T
    uvt_ref[0] = chan[0]
    uvt_ref[1] = chan[1]

    groups = LANES // 8

    for g in range(groups):
        at = pl.ds(g * 8, 8)
        for ref, source in ((pu, 0), (pv, 1)):
            for degree, value in enumerate(legendre(chan[source, at, :], DEG2 + 1)):
                if degree:
                    ref[degree, at, :] = value

    def sweep(i, top, first, count, row0, width):
        heights = top - i + 1
        sums = [None] * (heights * count)
        for g in range(groups):
            at = pl.ds(g * 8, 8)
            scaled = [chan[first + w, at, :] for w in range(count)]
            if i:
                factor = pu[i, at, :]
                scaled = [value * factor for value in scaled]
            for j in range(heights):
                other = pv[j, at, :] if j else None
                for w in range(count):
                    term = scaled[w] * other if j else scaled[w]
                    before = sums[j * count + w]
                    sums[j * count + w] = term if before is None else before + term
        for j in range(heights):
            for w in range(count):
                row = row0 + w * width + TERM_INDEX[(i, j)]
                acc[pl.ds(row * 8, 8), :] = sums[j * count + w]

    for i in range(DEG2 + 1):
        sweep(i, DEG2, 2, 3, 0, 96)
    for i in range(ORDER + 1):
        sweep(i, ORDER, 5, 2, ROW_GX, 32)
    zero = jnp.zeros((8, LANES), F32)
    for block in range(3):
        for row in range(len(TERMS), 96):
            acc[pl.ds((block * 96 + row) * 8, 8), :] = zero
    for block in range(2):
        for row in range(POLY, 32):
            acc[pl.ds((ROW_GX + block * 32 + row) * 8, 8), :] = zero

    for g in range(ROW_DET // 8):
        mom[pl.ds(g * 8, 8), :] = combine([acc[pl.ds(g * 64 + 8 * s, 8), :] for s in range(8)], sub8)
    mom[88:96, :] = jnp.where(sub8 == 7, mark, mom[88:96, :])

    pulls = jnp.where(sub8 < 4, mom[ROW_GX : ROW_GX + 8], pltpu.roll(mom[ROW_GY : ROW_GY + 8], 4, 0))
    zero32 = jnp.zeros((32, LANES), F32)
    zero96 = jnp.zeros((96, LANES), F32)
    first = split3(mom[0:256])
    third = split3(jnp.concatenate([mom[256:352], zero32], axis=0))
    fourth = split3(jnp.concatenate([zero96, mom[0:8], mom[96:104], mom[192:200], pulls], axis=0))
    pair = jnp.concatenate(first[:2], axis=1)
    for copy in range(2):
        place = ((rows128 == dest) & (copy_at == copy)).astype(jnp.bfloat16)
        place_det = (rows128 + LANES * copy == ccd).astype(jnp.bfloat16)
        twice = jnp.concatenate([place, place], axis=1)
        front = dot16(twice, pair, ((1,), (1,))) + dot16(place, first[2], ((1,), (1,)))
        out_ref[rows_of(3 * copy), :] = front[:, 0:LANES]
        out_ref[rows_of(3 * copy + 1), :] = front[:, LANES:]
        both = jnp.concatenate([place, place_det], axis=1)
        out_ref[rows_of(3 * copy + 2), :] = sum(
            dot16(both, jnp.concatenate(parts, axis=1), ((1,), (1,))) for parts in zip(third, fourth)
        )


def detector_solve(table):
    def moment(block, i, j):
        return table[8 * block + TERM_INDEX[(i, j)] : 8 * block + TERM_INDEX[(i, j)] + 1]

    def block_of(block):
        one, u, v = moment(block, 0, 0), moment(block, 1, 0), moment(block, 0, 1)
        uu = (2.0 * moment(block, 2, 0) + one) * (1.0 / 3.0)
        vv = (2.0 * moment(block, 0, 2) + one) * (1.0 / 3.0)
        uv = moment(block, 1, 1)
        return [[one, u, v], [u, uu, uv], [v, uv, vv]]

    part_xx, part_yy, part_xy = block_of(0), block_of(1), block_of(2)
    matrix = [part_xx[p] + part_xy[p] for p in range(3)] + [part_xy[p] + part_yy[p] for p in range(3)]
    at = [TERM_INDEX[term] for term in ((0, 0), (1, 0), (0, 1))]
    rhs = [table[24 + a : 25 + a] for a in at] + [table[28 + a : 29 + a] for a in at]
    for p in range(6):
        matrix[p][p] = matrix[p][p] + DETECTOR_DAMP
    inverse = [None] * 6
    lower = [[None] * 6 for _ in range(6)]
    for step in range(6):
        pivot = matrix[step][step]
        for before in range(step):
            pivot = pivot - lower[step][before] * lower[step][before]
        inverse[step] = 1.0 / jnp.sqrt(pivot)
        for row in range(step + 1, 6):
            value = matrix[row][step]
            for before in range(step):
                value = value - lower[row][before] * lower[step][before]
            lower[row][step] = value * inverse[step]
    forward = []
    for step in range(6):
        value = rhs[step]
        for before in range(step):
            value = value - lower[step][before] * forward[before]
        forward.append(value * inverse[step])
    answer = [None] * 6
    for step in range(5, -1, -1):
        value = forward[step]
        for after in range(step + 1, 6):
            value = value - lower[after][step] * answer[after]
        answer[step] = value * inverse[step]
    return answer


UNKNOWNS = [("x", q) for q in range(28)] + [("y", q) for q in range(24, 28)] + [("y", q) for q in range(24)]
SIZE = 2 * POLY
BLOCKS = SIZE // 8
PANEL = 4


def solve_kernel(arr_ref, expand_ref, scale_ref, upd_ref, resp_ref, table, wide, mat, rhs, invs):
    sub8 = iota((8, LANES), 0)
    rows128 = iota((LANES, LANES), 0)
    lanes128 = iota((LANES, LANES), 1)

    picks = []
    for copy in range(2):
        column = arr_ref[rows_of(3 * copy), :][:, MARK : MARK + 1]
        picks.append((column.astype(jnp.int32) == lanes128 + 1).astype(jnp.bfloat16))
    pick = jnp.concatenate(picks, axis=0)
    for block in range(3):
        both = jnp.concatenate([arr_ref[rows_of(block), :], arr_ref[rows_of(3 + block), :]], axis=0)
        table[pl.ds(block * LANES, LANES), :] = sum(
            dot16(value, pick, ((0,), (0,))) for value in split3(both)
        )

    sums = [jnp.sum(arr_ref[rows_of(3 * copy + 2), :], axis=0, keepdims=True) for copy in range(2)]
    turned = jnp.where(rows128 == 0, sums[0], jnp.where(rows128 == 1, sums[1], 0.0)).T
    answer = detector_solve(turned[96:128])

    high, middle, low = split3(jnp.concatenate([table[0:96], table[96:192], table[192:288]], axis=1))
    upper = jnp.concatenate([high, middle], axis=0)
    lower = jnp.concatenate([low, high], axis=0)
    chunk = 128
    for at in range(0, POLY * 32, chunk):
        sides = ((0, upper), (1, upper), (2, lower))
        wide[pl.ds(at, chunk), :] = sum(
            dot16(expand_ref[side, pl.ds(at, chunk), :], values, ((1,), (0,))) for side, values in sides
        )

    def part(which, q, group):
        return wide[q * 32 + group * 8 : q * 32 + group * 8 + 8, which * LANES : (which + 1) * LANES]

    for col, (kind, q) in enumerate(UNKNOWNS):
        for group in range(col // 8, BLOCKS):
            if kind == "x":
                if group < 3:
                    value = part(0, q, group)
                elif group == 3:
                    value = jnp.where(sub8 < 4, part(0, q, 3), pltpu.roll(part(2, q, 3), 4, 0))
                else:
                    value = part(2, q, group - 4)
            elif group == 3:
                value = jnp.where(sub8 < 4, 0.0, pltpu.roll(part(1, q, 3), 4, 0))
            else:
                value = part(1, q, group - 4)
            if group == col // 8:
                value = value + jnp.where(sub8 == col % 8, EXPOSURE_DAMP, 0.0)
            mat[pl.ds(col * SIZE + group * 8, 8), :] = value
    grad_x = table[ROW_GX : ROW_GX + 32] * scale_ref[...]
    grad_y = table[ROW_GY : ROW_GY + 32] * scale_ref[...]
    rhs[0:24, :] = grad_x[0:24]
    rhs[24:32, :] = jnp.where(sub8 < 4, grad_x[24:32], pltpu.roll(grad_y[24:32], 4, 0))
    rhs[32:56, :] = grad_y[0:24]

    for k0 in range(0, SIZE, PANEL):
        g0 = k0 // 8
        count = BLOCKS - g0

        def update(j, carry):
            base = j * SIZE
            column = [mat[pl.ds(base + g * 8, 8), :] for g in range(g0, BLOCKS)]
            new = []
            for c in range(PANEL):
                factor = mat[pl.ds(base + k0 + c, 1), :]
                for g in range(count):
                    new.append(carry[c * count + g] - column[g] * factor)
            return tuple(new)

        panel = tuple(
            mat[pl.ds((k0 + c) * SIZE + g * 8, 8), :] for c in range(PANEL) for g in range(g0, BLOCKS)
        )
        for j in range(k0):
            panel = update(j, panel)
        panel = [list(panel[c * count : (c + 1) * count]) for c in range(PANEL)]
        right = [rhs[pl.ds(g * 8, 8), :] for g in range(g0, BLOCKS)]
        for c in range(PANEL):
            k = k0 + c
            row = k % 8
            inverse = lax.rsqrt(panel[c][0][row : row + 1])
            column = [value * inverse for value in panel[c]]
            for other in range(c + 1, PANEL):
                factor = column[0][k0 % 8 + other : k0 % 8 + other + 1]
                panel[other] = [panel[other][g] - column[g] * factor for g in range(count)]
            forward = right[0][row : row + 1] * inverse
            keep = jnp.where(sub8 <= row, right[0], right[0] - column[0] * forward)
            keep = jnp.where(sub8 == row, forward, keep)
            right = [keep] + [right[g] - column[g] * forward for g in range(1, count)]
            invs[k : k + 1, :] = inverse
            for g in range(count):
                mat[pl.ds(k * SIZE + (g0 + g) * 8, 8), :] = column[g]
        for g in range(count):
            rhs[pl.ds((g0 + g) * 8, 8), :] = right[g]

    solved = [None] * BLOCKS
    for b in range(BLOCKS - 1, -1, -1):
        right = rhs[b * 8 : b * 8 + 8]
        if b < BLOCKS - 1:
            partial = []
            for c in range(8):
                total = None
                for g in range(b + 1, BLOCKS):
                    term = mat[pl.ds((b * 8 + c) * SIZE + g * 8, 8), :] * solved[g]
                    total = term if total is None else total + term
                partial.append(total)
            right = right - combine(partial, sub8)
        diagonal = transpose8([mat[pl.ds((b * 8 + c) * SIZE + b * 8, 8), :] for c in range(8)], sub8)
        for c in range(7, -1, -1):
            value = right[c : c + 1] * invs[b * 8 + c : b * 8 + c + 1]
            right = jnp.where(sub8 < c, right - diagonal[c] * value, jnp.where(sub8 == c, value, right))
        solved[b] = right
    whole = jnp.concatenate(
        solved[0:3] + [solved[3][0:4]] + solved[4:7] + [solved[3][4:8]], axis=0
    )
    upd_ref[...] = whole

    lane1 = iota((1, LANES), 1)
    first = [jnp.where(lane1 == 0, value, 0.0) for value in answer]
    second = [jnp.where(lane1 == 1, value, 0.0) for value in answer]
    zeros = jnp.zeros((SIZE, LANES), F32)
    zero16 = jnp.zeros((16, LANES), F32)
    gap = [jnp.zeros((2, LANES), F32)]
    left = jnp.concatenate(picks + [(lanes128 < 2).astype(jnp.bfloat16)], axis=1)
    right = jnp.concatenate(
        [
            jnp.concatenate([whole, zeros, zero16], axis=0),
            jnp.concatenate([zeros, whole, zero16], axis=0),
            jnp.concatenate([zeros, zeros] + first + gap + second + gap, axis=0),
        ],
        axis=1,
    )
    resp_ref[...] = sum(dot16(left, value, ((1,), (1,))) for value in split3(right))


def star_kernel(off_ref, diag_ref, corr_ref, uvt_ref, where_ref, scale_ref, resp_ref,
                star_ref, det_ref, coeff, model):
    tiles = corr_ref.shape[1]
    rows128 = iota((LANES, LANES), 0)
    turned = resp_ref[...].T
    det_ref[:, 0:LANES] = turned[112:118]
    det_ref[:, LANES:NCCD] = turned[120:126, 0 : NCCD - LANES]
    dest = where_ref[0:1]
    copy_at = where_ref[1:2]
    ccd = where_ref[2:3]
    picks = [((rows128 == dest) & (copy_at == c)).astype(F32) for c in range(2)]
    picks += [(rows128 + LANES * c == ccd).astype(F32) for c in range(2)]
    exposure = dot(turned[0:56], picks[0], ((1,), (0,))) + dot(turned[56:112], picks[1], ((1,), (0,)))
    detector = dot(turned[112:120], picks[2], ((1,), (0,))) + dot(turned[120:128], picks[3], ((1,), (0,)))
    scale = scale_ref[...]
    coeff[0:28, :] = exposure[0:28] * scale[0:28]
    coeff[32:60, :] = exposure[28:56] * scale[0:28]
    for axis in range(2):
        for m, term in enumerate(((0, 0), (1, 0), (0, 1))):
            row = 32 * axis + TERM_INDEX[term]
            coeff[row : row + 1, :] = coeff[row : row + 1, :] + detector[3 * axis + m : 3 * axis + m + 1]

    def evaluate(g, carry):
        at = pl.ds(pl.multiple_of(g * 8, 8), 8)
        in_u = legendre(uvt_ref[0, at, :], ORDER + 1)
        in_v = legendre(uvt_ref[1, at, :], ORDER + 1)
        for axis in range(2):
            total = None
            for i in range(ORDER + 1):
                inner = None
                for j in range(ORDER - i + 1):
                    row = 32 * axis + TERM_INDEX[(i, j)]
                    term = coeff[row : row + 1, :]
                    if j:
                        term = term * in_v[j]
                    inner = term if inner is None else inner + term
                if i:
                    inner = inner * in_u[i]
                total = inner if total is None else total + inner
            model[axis, at, :] = total
        return carry

    lax.fori_loop(0, LANES // 8, evaluate, 0, unroll=2)
    model_x = model[0].T
    model_y = model[1].T
    weights, resid, inverse = star_terms(off_ref, diag_ref, corr_ref, where_ref[3:4, 0:tiles])
    grad_x = None
    for visit in range(VISITS):
        w_xx, w_yy, w_xy = weights[visit]
        left_x = resid[visit][0] - model_x[visit * tiles : (visit + 1) * tiles]
        left_y = resid[visit][1] - model_y[visit * tiles : (visit + 1) * tiles]
        part_x = w_xx * left_x + w_xy * left_y
        part_y = w_xy * left_x + w_yy * left_y
        grad_x = part_x if grad_x is None else grad_x + part_x
        grad_y = part_y if visit == 0 else grad_y + part_y
    out_x, out_y = apply_inverse(inverse, grad_x, grad_y)
    star_ref[:, 0, :] = out_x
    star_ref[:, 1, :] = out_y


def vmem(count):
    return [pl.BlockSpec(memory_space=pltpu.VMEM)] * count


def shards(focal_uv, offsets, w_diag, w_corr, star_count, exposure_ids, ccd_ids, exp_slot):
    tiles = offsets.shape[0]
    flat = (tiles * VISITS * 2, LANES)
    inputs = (
        focal_uv.reshape(flat),
        offsets.reshape(flat),
        w_diag.reshape(flat),
        jnp.transpose(w_corr, (1, 0, 2)),
        star_count.reshape(1, tiles),
        exposure_ids.T,
        ccd_ids.T,
        exp_slot.reshape(LANES, LANES),
    )
    shape = jax.ShapeDtypeStruct
    tables = (jnp.asarray(expansion()), jnp.asarray(scale_rows()))
    outgoing, turned, where, expand, scale = pl.pallas_call(
        moments_kernel,
        out_shape=(
            shape((6 * LANES, LANES), F32),
            shape((2, LANES, LANES), F32),
            shape((8, LANES), jnp.int32),
            *(shape(array.shape, array.dtype) for array in tables),
        ),
        in_specs=[pl.BlockSpec(memory_space=pltpu.HBM)] * 10,
        out_specs=tuple(vmem(5)),
        scratch_shapes=[pltpu.VMEM(array.shape, array.dtype) for array in inputs]
        + [
            pltpu.SemaphoreType.DMA((10,)),
            pltpu.VMEM((7, LANES, LANES), F32),
            pltpu.VMEM((DEG2 + 1, LANES, LANES), F32),
            pltpu.VMEM((DEG2 + 1, LANES, LANES), F32),
            pltpu.VMEM((ROW_DET * 8, LANES), F32),
            pltpu.VMEM((ROW_DET, LANES), F32),
        ],
        compiler_params=pltpu.CompilerParams(vmem_limit_bytes=12 << 20),
        name="moments",
    )(*(pltpu.with_memory_space_constraint(array, pltpu.HBM) for array in (*inputs, *tables)))
    arrived = lax.all_to_all(outgoing.reshape(LANES, 1, 6 * LANES), ("field", "shard"), 0, 0, tiled=True)
    arrived = arrived.reshape(6 * LANES, LANES)
    update, answers = pl.pallas_call(
        solve_kernel,
        out_shape=(shape((SIZE, LANES), F32), shape((LANES, LANES), F32)),
        in_specs=vmem(3),
        out_specs=tuple(vmem(2)),
        scratch_shapes=[
            pltpu.VMEM((ROWS, LANES), F32),
            pltpu.VMEM((POLY * 32, 3 * LANES), F32),
            pltpu.VMEM((SIZE * SIZE, LANES), F32),
            pltpu.VMEM((SIZE, LANES), F32),
            pltpu.VMEM((SIZE, LANES), F32),
        ],
        compiler_params=pltpu.CompilerParams(vmem_limit_bytes=12 << 20),
        name="solve",
    )(arrived, expand, scale)
    replies = lax.all_to_all(answers.reshape(LANES, 1, LANES), ("field", "shard"), 0, 0, tiled=True)
    star_update, ccd_update = pl.pallas_call(
        star_kernel,
        out_shape=(shape((tiles, 2, LANES), F32), shape((6, NCCD), F32)),
        in_specs=vmem(7),
        out_specs=tuple(vmem(2)),
        scratch_shapes=[pltpu.VMEM((64, LANES), F32), pltpu.VMEM((2, LANES, LANES), F32)],
        compiler_params=pltpu.CompilerParams(vmem_limit_bytes=12 << 20),
        name="stars",
    )(*inputs[1:4], turned, where, scale, replies.reshape(LANES, LANES))
    return star_update, update, ccd_update.T


def solution(mesh):
    both = ("field", "shard")
    in_specs = (
        P(both, None, None, None),
        P(both, None, None, None),
        P(both, None, None, None),
        P(both, None, None),
        P(both),
        P(both, None),
        P(both, None),
        P(),
    )
    out_specs = (P(both, None, None), P(None, both), P())
    return jax.shard_map(shards, mesh=mesh, in_specs=in_specs, out_specs=out_specs, check_vma=False)
```

```python
import math

import jax
import jax.numpy as jnp
import numpy as np
from jax import lax
from jax.experimental import pallas as pl
from jax.experimental.pallas import tpu as pltpu
from jax.sharding import PartitionSpec as P

ORDER = 6
POLY = 28
VISITS = 6
NCCD = 189
LANES = 128
STAR_DAMP = 0.1
EXPOSURE_DAMP = 1.0
DETECTOR_DAMP = 1.0
HIGH = lax.Precision.HIGHEST
DEG2 = 2 * ORDER
F32 = jnp.float32

TERMS = [(i, n - i) for n in range(DEG2 + 1) for i in range(n + 1)]
TERM_INDEX = {term: at for at, term in enumerate(TERMS)}
SCALE = [math.sqrt((2 * i + 1) * (2 * j + 1)) for i, j in TERMS[:POLY]]

ROW_GX = 288
ROW_GY = 320
ROW_DET = 352
ROWS = 384
MARK = 95


def linearisation():
    from numpy.polynomial import legendre

    table = np.zeros((ORDER + 1, ORDER + 1, DEG2 + 1))
    for m in range(ORDER + 1):
        for n in range(ORDER + 1):
            product = legendre.legmul([0] * m + [1], [0] * n + [1])
            table[m, n, : len(product)] = product
    return table


def expansion():
    table = linearisation()
    matrix = np.zeros((POLY * 32, 96))
    for q, (iq, jq) in enumerate(TERMS[:POLY]):
        for p, (ip, jp) in enumerate(TERMS[:POLY]):
            for at, (a, b) in enumerate(TERMS):
                matrix[q * 32 + p, at] = SCALE[p] * SCALE[q] * table[ip, iq, a] * table[jp, jq, b]
    parts = []
    rest = matrix
    for _ in range(3):
        part = rest.astype(jnp.bfloat16)
        parts.append(part)
        rest = rest - part.astype(np.float64)
    high, middle, low = parts
    return np.concatenate([high, high, middle, middle, high, low], 1)


def scale_rows():
    rows = np.zeros((32, LANES), np.float32)
    rows[:POLY] = np.array(SCALE, np.float32)[:, None]
    return rows


def dot(a, b, dims):
    return lax.dot_general(a, b, (dims, ((), ())), precision=HIGH, preferred_element_type=F32)


def split3(value):
    high = value.astype(jnp.bfloat16)
    rest = value - high.astype(F32)
    middle = rest.astype(jnp.bfloat16)
    return high, middle, (rest - middle.astype(F32)).astype(jnp.bfloat16)


def dot16(a, b, dims):
    return lax.dot_general(a, b, (dims, ((), ())), preferred_element_type=F32)


def rows_of(part):
    return pl.ds(part, LANES, stride=6)


def iota(shape, axis):
    return lax.broadcasted_iota(jnp.int32, shape, axis)


def legendre(value, count):
    values = [None, value]
    for degree in range(1, count - 1):
        lower = (degree / (degree + 1)) * (values[degree - 1] if degree > 1 else 1.0)
        values.append(((2 * degree + 1) / (degree + 1)) * value * values[degree] - lower)
    return values


def star_terms(off_ref, diag_ref, corr_ref, counts):
    tiles = corr_ref.shape[1]
    lanes = iota((tiles, LANES), 1)
    counts = jnp.broadcast_to(counts.astype(F32), (tiles, tiles))
    square = (iota((tiles, tiles), 0) == iota((tiles, tiles), 1)).astype(F32)
    column = jnp.sum(counts * square, axis=1, keepdims=True)
    present = (lanes.astype(F32) < column).astype(F32)

    def rows(ref, visit, part):
        return ref[pl.ds(2 * visit + part, tiles, stride=2 * VISITS), :]

    weights = []
    resid = []
    for visit in range(VISITS):
        d0 = rows(diag_ref, visit, 0)
        d1 = rows(diag_ref, visit, 1)
        weights.append((d0 * present, d1 * present, corr_ref[visit] * jnp.sqrt(d0 * d1) * present))
        resid.append((rows(off_ref, visit, 0), rows(off_ref, visit, 1)))
    hess_xx = sum(w[0] for w in weights) + STAR_DAMP
    hess_yy = sum(w[1] for w in weights) + STAR_DAMP
    hess_xy = sum(w[2] for w in weights)
    determ = hess_xx * hess_yy - hess_xy * hess_xy
    inverse = (hess_yy / determ, hess_xx / determ, -hess_xy / determ)
    return weights, resid, inverse


def apply_inverse(inverse, x, y):
    inv_xx, inv_yy, inv_xy = inverse
    return inv_xx * x + inv_xy * y, inv_xy * x + inv_yy * y


def combine(values, sub):
    for shift in (4, 2, 1):
        low = (sub & shift) == 0
        half = len(values) // 2
        merged = []
        for at in range(half):
            a, b = values[at], values[at + half]
            if shift == 4:
                merged.append(jnp.where(low, a, b) + pltpu.roll(jnp.where(low, b, a), 4, 0))
            else:
                merged.append(jnp.where(low, a + pltpu.roll(a, 8 - shift, 0), b + pltpu.roll(b, shift, 0)))
        values = merged
    return values[0]


def transpose8(values, sub):
    values = list(values)
    for shift in (4, 2, 1):
        low = (sub & shift) == 0
        for at in range(8):
            if at & shift:
                continue
            a, b = values[at], values[at + shift]
            values[at] = jnp.where(low, a, pltpu.roll(b, shift, 0))
            values[at + shift] = jnp.where(low, pltpu.roll(a, 8 - shift, 0), b)
    return values


def moments_kernel(*refs):
    sources, out_refs, buffers, (sems, *scratch) = refs[:10], refs[10:17], refs[17:25], refs[25:]
    copies = [
        pltpu.make_async_copy(source, buffer, sems.at[at])
        for at, (source, buffer) in enumerate(zip(sources, (*buffers, *out_refs[5:])))
    ]
    for copy in copies:
        copy.start()
    for copy in copies[:8]:
        copy.wait()
    moments_body(*buffers, *out_refs[:5], *scratch)
    for copy in copies[8:]:
        copy.wait()


def moments_body(uv_ref, off_ref, diag_ref, corr_ref, count_ref, ids_ref, ccd_ref, slot_ref,
                 out_ref, power_ref, where_ref, base_ref, gain_ref, chan, high_power, acc, mom):
    tiles = corr_ref.shape[1]
    visits_all = tiles * VISITS
    sub8 = iota((8, LANES), 0)

    pad = jnp.zeros((LANES - visits_all, LANES), F32)
    mine = iota((VISITS, LANES), 1) // tiles == iota((VISITS, LANES), 0)

    def along_lanes(ref):
        spread = jnp.concatenate([ref[...]] * (LANES // tiles), axis=1)
        return jnp.sum(jnp.where(mine, spread, 0), axis=0, keepdims=True)

    ident = along_lanes(ids_ref)
    ccd = along_lanes(ccd_ref)
    rows128 = iota((LANES, LANES), 0)
    lanes128 = iota((LANES, LANES), 1)
    valid = iota((1, LANES), 1) < visits_all
    picked = dot(slot_ref[...].astype(F32), (rows128 == ident // LANES).astype(F32), ((0,), (0,)))
    position = jnp.sum(jnp.where(rows128 == ident % LANES, picked, 0.0), axis=0, keepdims=True)
    position = (position + 0.5).astype(jnp.int32)
    home = position // LANES
    dest = jnp.where(valid, home % 32 * 4 + home // 32, -1)
    ccd = jnp.where(valid, ccd, -1)
    dest_t = jnp.broadcast_to(dest.astype(F32), (LANES, LANES)).T.astype(jnp.int32)
    same = (dest_t == dest) & (rows128 < lanes128)
    copy_at = jnp.sum(same.astype(F32), axis=0, keepdims=True).astype(jnp.int32)
    mark = (position % LANES + 1).astype(F32)
    counts = jnp.concatenate([count_ref[...]] * (LANES // tiles), axis=1)
    where_ref[...] = jnp.where(
        sub8 == 0, dest, jnp.where(sub8 == 1, copy_at, jnp.where(sub8 == 2, ccd, counts))
    )

    weights, resid, inverse = star_terms(off_ref, diag_ref, corr_ref, count_ref[...])
    grad_x = sum(w[0] * r[0] + w[2] * r[1] for w, r in zip(weights, resid))
    grad_y = sum(w[2] * r[0] + w[1] * r[1] for w, r in zip(weights, resid))
    shift_x, shift_y = apply_inverse(inverse, grad_x, grad_y)
    base_ref[0] = shift_x
    base_ref[1] = shift_y
    inv_xx, inv_yy, inv_xy = inverse
    channels = [[] for _ in range(7)]
    for visit in range(VISITS):
        w_xx, w_yy, w_xy = weights[visit]
        left_x = resid[visit][0] - shift_x
        left_y = resid[visit][1] - shift_y
        prod_11 = inv_xx * w_xx + inv_xy * w_xy
        prod_12 = inv_xx * w_xy + inv_xy * w_yy
        prod_21 = inv_xy * w_xx + inv_yy * w_xy
        prod_22 = inv_xy * w_xy + inv_yy * w_yy
        for at, product in enumerate((prod_11, prod_12, prod_21, prod_22)):
            gain_ref[at, pl.ds(visit * tiles, tiles), :] = product
        values = (
            uv_ref[pl.ds(2 * visit, tiles, stride=2 * VISITS), :],
            uv_ref[pl.ds(2 * visit + 1, tiles, stride=2 * VISITS), :],
            w_xx - (w_xx * prod_11 + w_xy * prod_21),
            w_yy - (w_xy * prod_12 + w_yy * prod_22),
            w_xy - (w_xx * prod_12 + w_xy * prod_22),
            w_xx * left_x + w_xy * left_y,
            w_xy * left_x + w_yy * left_y,
        )
        for at, value in enumerate(values):
            channels[at].append(value)
    for at in range(7):
        chan[at] = jnp.concatenate(channels[at] + [pad], axis=0).T

    groups = LANES // 8

    for g in range(groups):
        at = pl.ds(g * 8, 8)
        for source in range(2):
            for degree, value in enumerate(legendre(chan[source, at, :], DEG2 + 1)):
                if degree > ORDER:
                    high_power[source, degree - ORDER - 1, at, :] = value
                elif degree:
                    power_ref[source, degree - 1, at, :] = value

    def power(source, degree, at):
        if degree > ORDER:
            return high_power[source, degree - ORDER - 1, at, :]
        return power_ref[source, degree - 1, at, :]

    def sweep(i, top, first, count, row0, width):
        heights = top - i + 1
        sums = [None] * (heights * count)
        for g in range(groups):
            at = pl.ds(g * 8, 8)
            scaled = [chan[first + w, at, :] for w in range(count)]
            if i:
                factor = power(0, i, at)
                scaled = [value * factor for value in scaled]
            for j in range(heights):
                other = power(1, j, at) if j else None
                for w in range(count):
                    term = scaled[w] * other if j else scaled[w]
                    before = sums[j * count + w]
                    sums[j * count + w] = term if before is None else before + term
        for j in range(heights):
            for w in range(count):
                row = row0 + w * width + TERM_INDEX[(i, j)]
                acc[pl.ds(row * 8, 8), :] = sums[j * count + w]

    for i in range(DEG2 + 1):
        sweep(i, DEG2, 2, 3, 0, 96)
    for i in range(ORDER + 1):
        sweep(i, ORDER, 5, 2, ROW_GX, 32)
    zero = jnp.zeros((8, LANES), F32)
    for block in range(3):
        for row in range(len(TERMS), 96):
            acc[pl.ds((block * 96 + row) * 8, 8), :] = zero
    for block in range(2):
        for row in range(POLY, 32):
            acc[pl.ds((ROW_GX + block * 32 + row) * 8, 8), :] = zero

    for g in range(ROW_DET // 8):
        mom[pl.ds(g * 8, 8), :] = combine([acc[pl.ds(g * 64 + 8 * s, 8), :] for s in range(8)], sub8)
    mom[88:96, :] = jnp.where(sub8 == 7, mark, mom[88:96, :])

    pulls = jnp.where(sub8 < 4, mom[ROW_GX : ROW_GX + 8], pltpu.roll(mom[ROW_GY : ROW_GY + 8], 4, 0))
    zero32 = jnp.zeros((32, LANES), F32)
    zero96 = jnp.zeros((96, LANES), F32)
    first = split3(mom[0:256])
    third = split3(jnp.concatenate([mom[256:352], zero32], axis=0))
    fourth = split3(jnp.concatenate([zero96, mom[0:8], mom[96:104], mom[192:200], pulls], axis=0))
    first = jnp.concatenate(first, axis=1)
    last = jnp.concatenate([piece for parts in zip(third, fourth) for piece in parts], axis=1)
    for copy in range(2):
        place = ((rows128 == dest) & (copy_at == copy)).astype(jnp.bfloat16)
        place_det = (rows128 + LANES * copy == ccd).astype(jnp.bfloat16)
        front = dot16(jnp.concatenate([place] * 3, axis=1), first, ((1,), (1,)))
        out_ref[rows_of(3 * copy), :] = front[:, 0:LANES]
        out_ref[rows_of(3 * copy + 1), :] = front[:, LANES:]
        both = jnp.concatenate([place, place_det] * 3, axis=1)
        out_ref[rows_of(3 * copy + 2), :] = dot16(both, last, ((1,), (1,)))


def detector_solve(table):
    def moment(block, i, j):
        return table[8 * block + TERM_INDEX[(i, j)] : 8 * block + TERM_INDEX[(i, j)] + 1]

    def block_of(block):
        one, u, v = moment(block, 0, 0), moment(block, 1, 0), moment(block, 0, 1)
        uu = (2.0 * moment(block, 2, 0) + one) * (1.0 / 3.0)
        vv = (2.0 * moment(block, 0, 2) + one) * (1.0 / 3.0)
        uv = moment(block, 1, 1)
        return [[one, u, v], [u, uu, uv], [v, uv, vv]]

    part_xx, part_yy, part_xy = block_of(0), block_of(1), block_of(2)
    matrix = [part_xx[p] + part_xy[p] for p in range(3)] + [part_xy[p] + part_yy[p] for p in range(3)]
    at = [TERM_INDEX[term] for term in ((0, 0), (1, 0), (0, 1))]
    rhs = [table[24 + a : 25 + a] for a in at] + [table[28 + a : 29 + a] for a in at]
    for p in range(6):
        matrix[p][p] = matrix[p][p] + DETECTOR_DAMP
    inverse = [None] * 6
    lower = [[None] * 6 for _ in range(6)]
    for step in range(6):
        pivot = matrix[step][step]
        for before in range(step):
            pivot = pivot - lower[step][before] * lower[step][before]
        inverse[step] = 1.0 / jnp.sqrt(pivot)
        for row in range(step + 1, 6):
            value = matrix[row][step]
            for before in range(step):
                value = value - lower[row][before] * lower[step][before]
            lower[row][step] = value * inverse[step]
    forward = []
    for step in range(6):
        value = rhs[step]
        for before in range(step):
            value = value - lower[step][before] * forward[before]
        forward.append(value * inverse[step])
    answer = [None] * 6
    for step in range(5, -1, -1):
        value = forward[step]
        for after in range(step + 1, 6):
            value = value - lower[after][step] * answer[after]
        answer[step] = value * inverse[step]
    return answer


UNKNOWNS = [("x", q) for q in range(28)] + [("y", q) for q in range(24, 28)] + [("y", q) for q in range(24)]
SIZE = 2 * POLY
BLOCKS = SIZE // 8
PANEL = 4


def solve_kernel(arr_ref, expand_ref, scale_ref, upd_ref, resp_ref, table, wide, mat, rhs, invs):
    sub8 = iota((8, LANES), 0)
    rows128 = iota((LANES, LANES), 0)
    lanes128 = iota((LANES, LANES), 1)

    picks = []
    for copy in range(2):
        column = arr_ref[rows_of(3 * copy), :][:, MARK : MARK + 1]
        picks.append((column.astype(jnp.int32) == lanes128 + 1).astype(jnp.bfloat16))
    pick = jnp.concatenate(picks * 3, axis=0)
    for block in range(3):
        both = jnp.concatenate([arr_ref[rows_of(block), :], arr_ref[rows_of(3 + block), :]], axis=0)
        table[pl.ds(block * LANES, LANES), :] = dot16(
            jnp.concatenate(split3(both), axis=0), pick, ((0,), (0,))
        )

    sums = [jnp.sum(arr_ref[rows_of(3 * copy + 2), :], axis=0, keepdims=True) for copy in range(2)]
    turned = jnp.where(rows128 == 0, sums[0], jnp.where(rows128 == 1, sums[1], 0.0)).T
    answer = detector_solve(turned[96:128])

    high, middle, low = split3(jnp.concatenate([table[0:96], table[96:192], table[192:288]], axis=1))
    parts = jnp.concatenate([high, middle, high, middle, low, high], axis=0)
    chunk = 128
    for at in range(0, POLY * 32, chunk):
        wide[pl.ds(at, chunk), :] = dot16(expand_ref[pl.ds(at, chunk), :], parts, ((1,), (0,)))

    def part(which, q, group):
        return wide[q * 32 + group * 8 : q * 32 + group * 8 + 8, which * LANES : (which + 1) * LANES]

    for col, (kind, q) in enumerate(UNKNOWNS):
        for group in range(col // 8, BLOCKS):
            if kind == "x":
                if group < 3:
                    value = part(0, q, group)
                elif group == 3:
                    value = jnp.where(sub8 < 4, part(0, q, 3), pltpu.roll(part(2, q, 3), 4, 0))
                else:
                    value = part(2, q, group - 4)
            elif group == 3:
                value = jnp.where(sub8 < 4, 0.0, pltpu.roll(part(1, q, 3), 4, 0))
            else:
                value = part(1, q, group - 4)
            if group == col // 8:
                value = value + jnp.where(sub8 == col % 8, EXPOSURE_DAMP, 0.0)
            mat[pl.ds(col * SIZE + group * 8, 8), :] = value
    grad_x = table[ROW_GX : ROW_GX + 32] * scale_ref[...]
    grad_y = table[ROW_GY : ROW_GY + 32] * scale_ref[...]
    rhs[0:24, :] = grad_x[0:24]
    rhs[24:32, :] = jnp.where(sub8 < 4, grad_x[24:32], pltpu.roll(grad_y[24:32], 4, 0))
    rhs[32:56, :] = grad_y[0:24]

    for k0 in range(0, SIZE, PANEL):
        g0 = k0 // 8
        count = BLOCKS - g0

        def update(j, carry):
            base = j * SIZE
            column = [mat[pl.ds(base + g * 8, 8), :] for g in range(g0, BLOCKS)]
            new = []
            for c in range(PANEL):
                factor = mat[pl.ds(base + k0 + c, 1), :]
                for g in range(count):
                    new.append(carry[c * count + g] - column[g] * factor)
            return tuple(new)

        panel = tuple(
            mat[pl.ds((k0 + c) * SIZE + g * 8, 8), :] for c in range(PANEL) for g in range(g0, BLOCKS)
        )
        for j in range(k0):
            panel = update(j, panel)
        panel = [list(panel[c * count : (c + 1) * count]) for c in range(PANEL)]
        right = [rhs[pl.ds(g * 8, 8), :] for g in range(g0, BLOCKS)]
        for c in range(PANEL):
            k = k0 + c
            row = k % 8
            inverse = lax.rsqrt(panel[c][0][row : row + 1])
            column = [value * inverse for value in panel[c]]
            for other in range(c + 1, PANEL):
                factor = column[0][k0 % 8 + other : k0 % 8 + other + 1]
                panel[other] = [panel[other][g] - column[g] * factor for g in range(count)]
            forward = right[0][row : row + 1] * inverse
            keep = jnp.where(sub8 <= row, right[0], right[0] - column[0] * forward)
            keep = jnp.where(sub8 == row, forward, keep)
            right = [keep] + [right[g] - column[g] * forward for g in range(1, count)]
            invs[k : k + 1, :] = inverse
            for g in range(count):
                mat[pl.ds(k * SIZE + (g0 + g) * 8, 8), :] = column[g]
        for g in range(count):
            rhs[pl.ds((g0 + g) * 8, 8), :] = right[g]

    solved = [None] * BLOCKS
    for b in range(BLOCKS - 1, -1, -1):
        right = rhs[b * 8 : b * 8 + 8]
        if b < BLOCKS - 1:
            partial = []
            for c in range(8):
                total = None
                for g in range(b + 1, BLOCKS):
                    term = mat[pl.ds((b * 8 + c) * SIZE + g * 8, 8), :] * solved[g]
                    total = term if total is None else total + term
                partial.append(total)
            right = right - combine(partial, sub8)
        diagonal = transpose8([mat[pl.ds((b * 8 + c) * SIZE + b * 8, 8), :] for c in range(8)], sub8)
        for c in range(7, -1, -1):
            value = right[c : c + 1] * invs[b * 8 + c : b * 8 + c + 1]
            right = jnp.where(sub8 < c, right - diagonal[c] * value, jnp.where(sub8 == c, value, right))
        solved[b] = right
    whole = jnp.concatenate(
        solved[0:3] + [solved[3][0:4]] + solved[4:7] + [solved[3][4:8]], axis=0
    )
    upd_ref[...] = whole

    lane1 = iota((1, LANES), 1)
    first = [jnp.where(lane1 == 0, value, 0.0) for value in answer]
    second = [jnp.where(lane1 == 1, value, 0.0) for value in answer]
    zeros = jnp.zeros((SIZE, LANES), F32)
    zero16 = jnp.zeros((16, LANES), F32)
    gap = [jnp.zeros((2, LANES), F32)]
    left = jnp.concatenate(picks + [(lanes128 < 2).astype(jnp.bfloat16)], axis=1)
    right = jnp.concatenate(
        [
            jnp.concatenate([whole, zeros, zero16], axis=0),
            jnp.concatenate([zeros, whole, zero16], axis=0),
            jnp.concatenate([zeros, zeros] + first + gap + second + gap, axis=0),
        ],
        axis=1,
    )
    left = jnp.concatenate([left] * 3, axis=1)
    resp_ref[...] = dot16(left, jnp.concatenate(split3(right), axis=1), ((1,), (1,)))


def star_kernel(base_ref, gain_ref, power_ref, where_ref, scale_ref, update_ref, resp_ref,
                star_ref, det_ref, update_out, coeff, model, sem):
    write = pltpu.make_async_copy(update_ref, update_out, sem)
    write.start()
    tiles = base_ref.shape[1]
    rows128 = iota((LANES, LANES), 0)
    turned = resp_ref[...].T
    det_ref[:, 0:LANES] = turned[112:118]
    det_ref[:, LANES:NCCD] = turned[120:126, 0 : NCCD - LANES]
    dest = where_ref[0:1]
    copy_at = where_ref[1:2]
    ccd = where_ref[2:3]
    picks = [((rows128 == dest) & (copy_at == c)).astype(jnp.bfloat16) for c in range(2)]
    dets = [(rows128 + LANES * c == ccd).astype(jnp.bfloat16) for c in range(2)]
    halves = split3(jnp.concatenate([turned[0:56], turned[56:112]], axis=1))
    exposure = dot16(jnp.concatenate(halves, axis=1), jnp.concatenate(picks * 3, axis=0), ((1,), (0,)))
    halves = split3(jnp.concatenate([turned[112:120], turned[120:128]], axis=1))
    detector = dot16(jnp.concatenate(halves, axis=1), jnp.concatenate(dets * 3, axis=0), ((1,), (0,)))
    scale = scale_ref[...]
    coeff[0:28, :] = exposure[0:28] * scale[0:28]
    coeff[32:60, :] = exposure[28:56] * scale[0:28]
    for axis in range(2):
        for m, term in enumerate(((0, 0), (1, 0), (0, 1))):
            row = 32 * axis + TERM_INDEX[term]
            coeff[row : row + 1, :] = coeff[row : row + 1, :] + detector[3 * axis + m : 3 * axis + m + 1]

    for g in range(LANES // 8):
        at = pl.ds(g * 8, 8)
        in_u = [None] + [power_ref[0, i, at, :] for i in range(ORDER)]
        in_v = [None] + [power_ref[1, i, at, :] for i in range(ORDER)]
        for axis in range(2):
            total = None
            for i in range(ORDER + 1):
                inner = None
                for j in range(ORDER - i + 1):
                    row = 32 * axis + TERM_INDEX[(i, j)]
                    term = coeff[row : row + 1, :]
                    if j:
                        term = term * in_v[j]
                    inner = term if inner is None else inner + term
                if i:
                    inner = inner * in_u[i]
                total = inner if total is None else total + inner
            model[axis, at, :] = total
    model_x = model[0].T
    model_y = model[1].T
    out_x = base_ref[0]
    out_y = base_ref[1]
    for visit in range(VISITS):
        at = slice(visit * tiles, (visit + 1) * tiles)
        out_x = out_x - (gain_ref[0, at, :] * model_x[at] + gain_ref[1, at, :] * model_y[at])
        out_y = out_y - (gain_ref[2, at, :] * model_x[at] + gain_ref[3, at, :] * model_y[at])
    star_ref[:, 0, :] = out_x
    star_ref[:, 1, :] = out_y
    write.wait()


def vmem(count):
    return [pl.BlockSpec(memory_space=pltpu.VMEM)] * count


def shards(focal_uv, offsets, w_diag, w_corr, star_count, exposure_ids, ccd_ids, exp_slot):
    tiles = offsets.shape[0]
    flat = (tiles * VISITS * 2, LANES)
    inputs = (
        focal_uv.reshape(flat),
        offsets.reshape(flat),
        w_diag.reshape(flat),
        jnp.transpose(w_corr, (1, 0, 2)),
        star_count.reshape(1, tiles),
        exposure_ids.T,
        ccd_ids.T,
        exp_slot.reshape(LANES, LANES),
    )
    shape = jax.ShapeDtypeStruct
    tables = (jnp.asarray(expansion()), jnp.asarray(scale_rows()))
    outgoing, powers, where, base, gain, expand, scale = pl.pallas_call(
        moments_kernel,
        out_shape=(
            shape((6 * LANES, LANES), F32),
            shape((2, ORDER, LANES, LANES), F32),
            shape((8, LANES), jnp.int32),
            shape((2, tiles, LANES), F32),
            shape((4, tiles * VISITS, LANES), F32),
            *(shape(array.shape, array.dtype) for array in tables),
        ),
        in_specs=[pl.BlockSpec(memory_space=pltpu.HBM)] * 10,
        out_specs=tuple(vmem(7)),
        scratch_shapes=[pltpu.VMEM(array.shape, array.dtype) for array in inputs]
        + [
            pltpu.SemaphoreType.DMA((10,)),
            pltpu.VMEM((7, LANES, LANES), F32),
            pltpu.VMEM((2, ORDER, LANES, LANES), F32),
            pltpu.VMEM((ROW_DET * 8, LANES), F32),
            pltpu.VMEM((ROW_DET, LANES), F32),
        ],
        compiler_params=pltpu.CompilerParams(vmem_limit_bytes=12 << 20),
        name="moments",
    )(*(pltpu.with_memory_space_constraint(array, pltpu.HBM) for array in (*inputs, *tables)))
    arrived = lax.all_to_all(outgoing.reshape(LANES, 1, 6 * LANES), ("shard", "field"), 0, 0, tiled=True)
    arrived = arrived.reshape(6 * LANES, LANES)
    update, answers = pl.pallas_call(
        solve_kernel,
        out_shape=(shape((SIZE, LANES), F32), shape((LANES, LANES), F32)),
        in_specs=vmem(3),
        out_specs=tuple(vmem(2)),
        scratch_shapes=[
            pltpu.VMEM((ROWS, LANES), F32),
            pltpu.VMEM((POLY * 32, 3 * LANES), F32),
            pltpu.VMEM((SIZE * SIZE, LANES), F32),
            pltpu.VMEM((SIZE, LANES), F32),
            pltpu.VMEM((SIZE, LANES), F32),
        ],
        compiler_params=pltpu.CompilerParams(vmem_limit_bytes=12 << 20),
        name="solve",
    )(arrived, expand, scale)
    replies = lax.all_to_all(answers.reshape(LANES, 1, LANES), ("shard", "field"), 0, 0, tiled=True)
    star_update, ccd_update, update = pl.pallas_call(
        star_kernel,
        out_shape=(shape((tiles, 2, LANES), F32), shape((6, NCCD), F32), shape((SIZE, LANES), F32)),
        in_specs=vmem(7),
        out_specs=(*vmem(2), pl.BlockSpec(memory_space=pltpu.HBM)),
        scratch_shapes=[
            pltpu.VMEM((64, LANES), F32),
            pltpu.VMEM((2, LANES, LANES), F32),
            pltpu.SemaphoreType.DMA,
        ],
        compiler_params=pltpu.CompilerParams(vmem_limit_bytes=12 << 20),
        name="stars",
    )(base, gain, powers, where, scale, update, replies.reshape(LANES, LANES))
    return star_update, update, ccd_update.T


def solution(mesh):
    both = ("field", "shard")
    in_specs = (
        P(both, None, None, None),
        P(both, None, None, None),
        P(both, None, None, None),
        P(both, None, None),
        P(both),
        P(both, None),
        P(both, None),
        P(),
    )
    out_specs = (P(both, None, None), P(None, both), P())
    return jax.shard_map(shards, mesh=mesh, in_specs=in_specs, out_specs=out_specs, check_vma=False)
```

```python
import math

import jax
import jax.numpy as jnp
import numpy as np
from jax import lax
from jax.experimental import pallas as pl
from jax.experimental.pallas import tpu as pltpu
from jax.sharding import PartitionSpec as P

ORDER = 6
POLY = 28
VISITS = 6
NCCD = 189
LANES = 128
STAR_DAMP = 0.1
EXPOSURE_DAMP = 1.0
DETECTOR_DAMP = 1.0
HIGH = lax.Precision.HIGHEST
DEG2 = 2 * ORDER
UNROLL = 8
F32 = jnp.float32

TERMS = [(i, n - i) for n in range(DEG2 + 1) for i in range(n + 1)]
TERM_INDEX = {term: at for at, term in enumerate(TERMS)}
LEAD = [math.factorial(2 * n) / (2**n * math.factorial(n) ** 2) for n in range(DEG2 + 1)]
NORM = [math.sqrt((2 * i + 1) * (2 * j + 1)) for i, j in TERMS[:POLY]]
SCALE = [norm * LEAD[i] * LEAD[j] for norm, (i, j) in zip(NORM, TERMS)]

ROW_GX = 96
ROW_GY = 224
ROW_DET = 352
MARK = 95


def linearisation():
    from numpy.polynomial import legendre

    table = np.zeros((ORDER + 1, ORDER + 1, DEG2 + 1))
    for m in range(ORDER + 1):
        for n in range(ORDER + 1):
            product = legendre.legmul([0] * m + [1], [0] * n + [1])
            table[m, n, : len(product)] = product
    return table


def expansion():
    table = linearisation()
    matrix = np.zeros((POLY * 32, LANES))
    for q, (iq, jq) in enumerate(TERMS[:POLY]):
        for p, (ip, jp) in enumerate(TERMS[:POLY]):
            for at, (a, b) in enumerate(TERMS):
                product = table[ip, iq, a] * LEAD[a] * table[jp, jq, b] * LEAD[b]
                matrix[q * 32 + p, at] = NORM[p] * NORM[q] * product
    parts = []
    rest = matrix
    for _ in range(3):
        part = rest.astype(jnp.bfloat16)
        parts.append(part)
        rest = rest - part.astype(np.float64)
    high, middle, low = parts
    return np.concatenate([high, middle, low], 1)


def scale_rows():
    rows = np.zeros((32, LANES), np.float32)
    rows[:POLY] = np.array(SCALE, np.float32)[:, None]
    return rows


def dot(a, b, dims):
    return lax.dot_general(a, b, (dims, ((), ())), precision=HIGH, preferred_element_type=F32)


def split3(value):
    high = value.astype(jnp.bfloat16)
    rest = value - high.astype(F32)
    middle = rest.astype(jnp.bfloat16)
    return high, middle, (rest - middle.astype(F32)).astype(jnp.bfloat16)


def dot16(a, b, dims):
    return lax.dot_general(a, b, (dims, ((), ())), preferred_element_type=F32)


def rows_of(part):
    return pl.ds(part, LANES, stride=6)


def iota(shape, axis):
    return lax.broadcasted_iota(jnp.int32, shape, axis)


def legendre(value, count):
    values = [None, value]
    for degree in range(1, count - 1):
        before = values[degree - 1] if degree > 1 else 1.0
        values.append(value * values[degree] - (degree * degree / (4 * degree * degree - 1)) * before)
    return values


def star_terms(off_ref, diag_ref, corr_ref, counts):
    tiles = corr_ref.shape[1]
    lanes = iota((tiles, LANES), 1)
    counts = jnp.broadcast_to(counts.astype(F32), (tiles, tiles))
    square = (iota((tiles, tiles), 0) == iota((tiles, tiles), 1)).astype(F32)
    column = jnp.sum(counts * square, axis=1, keepdims=True)
    present = (lanes.astype(F32) < column).astype(F32)

    def rows(ref, visit, part):
        return ref[pl.ds(2 * visit + part, tiles, stride=2 * VISITS), :]

    weights = []
    resid = []
    for visit in range(VISITS):
        d0 = rows(diag_ref, visit, 0)
        d1 = rows(diag_ref, visit, 1)
        weights.append((d0 * present, d1 * present, corr_ref[visit] * jnp.sqrt(d0 * d1) * present))
        resid.append((rows(off_ref, visit, 0), rows(off_ref, visit, 1)))
    hess_xx = sum(w[0] for w in weights) + STAR_DAMP
    hess_yy = sum(w[1] for w in weights) + STAR_DAMP
    hess_xy = sum(w[2] for w in weights)
    determ = hess_xx * hess_yy - hess_xy * hess_xy
    inverse = (hess_yy / determ, hess_xx / determ, -hess_xy / determ)
    return weights, resid, inverse


def apply_inverse(inverse, x, y):
    inv_xx, inv_yy, inv_xy = inverse
    return inv_xx * x + inv_xy * y, inv_xy * x + inv_yy * y


def combine(values, sub):
    for shift in (4, 2, 1):
        low = (sub & shift) == 0
        half = len(values) // 2
        merged = []
        for at in range(half):
            a, b = values[at], values[at + half]
            if shift == 4:
                merged.append(jnp.where(low, a, b) + pltpu.roll(jnp.where(low, b, a), 4, 0))
            else:
                merged.append(jnp.where(low, a + pltpu.roll(a, 8 - shift, 0), b + pltpu.roll(b, shift, 0)))
        values = merged
    return values[0]


def moments_kernel(*refs):
    sources, out_refs, buffers, (sems, *scratch) = refs[:10], refs[10:17], refs[17:25], refs[25:]
    copies = [
        pltpu.make_async_copy(source, buffer, sems.at[at])
        for at, (source, buffer) in enumerate(zip(sources, (*buffers, *out_refs[5:])))
    ]
    for copy in copies:
        copy.start()
    for copy in copies[:8]:
        copy.wait()
    moments_body(*buffers, *out_refs[:5], *scratch)
    for copy in copies[8:]:
        copy.wait()


def moments_body(uv_ref, off_ref, diag_ref, corr_ref, count_ref, ids_ref, ccd_ref, slot_ref,
                 out_ref, power_ref, where_ref, base_ref, gain_ref, chan, high_power, acc, mom):
    tiles = corr_ref.shape[1]
    visits_all = tiles * VISITS
    sub8 = iota((8, LANES), 0)

    pad = jnp.zeros((LANES - visits_all, LANES), F32)
    mine = iota((VISITS, LANES), 1) // tiles == iota((VISITS, LANES), 0)

    def along_lanes(ref):
        spread = jnp.concatenate([ref[...]] * (LANES // tiles), axis=1)
        return jnp.sum(jnp.where(mine, spread, 0), axis=0, keepdims=True)

    ident = along_lanes(ids_ref)
    ccd = along_lanes(ccd_ref)
    rows128 = iota((LANES, LANES), 0)
    lanes128 = iota((LANES, LANES), 1)
    valid = iota((1, LANES), 1) < visits_all
    picked = dot(slot_ref[...].astype(F32), (rows128 == ident // LANES).astype(F32), ((0,), (0,)))
    position = jnp.sum(jnp.where(rows128 == ident % LANES, picked, 0.0), axis=0, keepdims=True)
    position = (position + 0.5).astype(jnp.int32)
    home = position // LANES
    dest = jnp.where(valid, home % 32 * 4 + home // 32, -1)
    ccd = jnp.where(valid, ccd, -1)
    dest_t = jnp.broadcast_to(dest.astype(F32), (LANES, LANES)).T.astype(jnp.int32)
    same = (dest_t == dest) & (rows128 < lanes128)
    copy_at = jnp.sum(same.astype(F32), axis=0, keepdims=True).astype(jnp.int32)
    mark = (position % LANES + 1).astype(F32)
    counts = jnp.concatenate([count_ref[...]] * (LANES // tiles), axis=1)
    where_ref[...] = jnp.where(
        sub8 == 0, dest, jnp.where(sub8 == 1, copy_at, jnp.where(sub8 == 2, ccd, counts))
    )

    weights, resid, inverse = star_terms(off_ref, diag_ref, corr_ref, count_ref[...])
    grad_x = sum(w[0] * r[0] + w[2] * r[1] for w, r in zip(weights, resid))
    grad_y = sum(w[2] * r[0] + w[1] * r[1] for w, r in zip(weights, resid))
    shift_x, shift_y = apply_inverse(inverse, grad_x, grad_y)
    base_ref[0] = shift_x
    base_ref[1] = shift_y
    inv_xx, inv_yy, inv_xy = inverse
    channels = [[] for _ in range(7)]
    for visit in range(VISITS):
        w_xx, w_yy, w_xy = weights[visit]
        left_x = resid[visit][0] - shift_x
        left_y = resid[visit][1] - shift_y
        prod_11 = inv_xx * w_xx + inv_xy * w_xy
        prod_12 = inv_xx * w_xy + inv_xy * w_yy
        prod_21 = inv_xy * w_xx + inv_yy * w_xy
        prod_22 = inv_xy * w_xy + inv_yy * w_yy
        for at, product in enumerate((prod_11, prod_12, prod_21, prod_22)):
            gain_ref[at, pl.ds(visit * tiles, tiles), :] = product
        values = (
            uv_ref[pl.ds(2 * visit, tiles, stride=2 * VISITS), :],
            uv_ref[pl.ds(2 * visit + 1, tiles, stride=2 * VISITS), :],
            w_xx - (w_xx * prod_11 + w_xy * prod_21),
            w_yy - (w_xy * prod_12 + w_yy * prod_22),
            w_xy - (w_xx * prod_12 + w_xy * prod_22),
            w_xx * left_x + w_xy * left_y,
            w_xy * left_x + w_yy * left_y,
        )
        for at, value in enumerate(values):
            channels[at].append(value)
    for at in range(7):
        chan[at] = jnp.concatenate(channels[at] + [pad], axis=0).T

    groups = LANES // 8

    for g in range(groups):
        at = pl.ds(g * 8, 8)
        for source in range(2):
            for degree, value in enumerate(legendre(chan[source, at, :], DEG2 + 1)):
                if degree > ORDER:
                    high_power[source, degree - ORDER - 1, at, :] = value
                elif degree:
                    power_ref[source, degree - 1, at, :] = value

    def power(source, degree, at):
        if degree > ORDER:
            return high_power[source, degree - ORDER - 1, at, :]
        return power_ref[source, degree - 1, at, :]

    def sweep(i, top, first, count, row0, width):
        heights = top - i + 1

        def step(g, sums):
            at = pl.ds(pl.multiple_of(g * 8, 8), 8)
            scaled = [chan[first + w, at, :] for w in range(count)]
            if i:
                factor = power(0, i, at)
                scaled = [value * factor for value in scaled]
            new = []
            for j in range(heights):
                other = power(1, j, at) if j else None
                for w in range(count):
                    term = scaled[w] * other if j else scaled[w]
                    new.append(sums[j * count + w] + term)
            return tuple(new)

        start = tuple(jnp.zeros((8, LANES), F32) for _ in range(heights * count))
        sums = lax.fori_loop(0, groups, step, start, unroll=UNROLL)
        for j in range(heights):
            for w in range(count):
                row = row0 + w * width + TERM_INDEX[(i, j)]
                acc[pl.ds(row * 8, 8), :] = sums[j * count + w]

    for i in range(DEG2 + 1):
        sweep(i, DEG2, 2, 3, 0, LANES)
    for i in range(ORDER + 1):
        sweep(i, ORDER, 5, 2, ROW_GX, LANES)
    zero = jnp.zeros((8, LANES), F32)
    for block in range(3):
        for row in range(len(TERMS), 96):
            acc[pl.ds((block * LANES + row) * 8, 8), :] = zero
    for block in range(2):
        for row in range(POLY, 32):
            acc[pl.ds((ROW_GX + block * LANES + row) * 8, 8), :] = zero

    for g in range(ROW_DET // 8):
        mom[pl.ds(g * 8, 8), :] = combine([acc[pl.ds(g * 64 + 8 * s, 8), :] for s in range(8)], sub8)
    mom[88:96, :] = jnp.where(sub8 == 7, mark, mom[88:96, :])

    pulls = jnp.where(sub8 < 4, mom[ROW_GX : ROW_GX + 8], pltpu.roll(mom[ROW_GY : ROW_GY + 8], 4, 0))
    zero32 = jnp.zeros((32, LANES), F32)
    zero96 = jnp.zeros((96, LANES), F32)
    first = split3(mom[0:256])
    third = split3(jnp.concatenate([mom[256:352], zero32], axis=0))
    fourth = split3(jnp.concatenate([zero96, mom[0:8], mom[128:136], mom[256:264], pulls], axis=0))
    first = jnp.concatenate(first, axis=1)
    last = jnp.concatenate([piece for parts in zip(third, fourth) for piece in parts], axis=1)
    for copy in range(2):
        place = ((rows128 == dest) & (copy_at == copy)).astype(jnp.bfloat16)
        place_det = (rows128 + LANES * copy == ccd).astype(jnp.bfloat16)
        front = dot16(jnp.concatenate([place] * 3, axis=1), first, ((1,), (1,)))
        out_ref[rows_of(3 * copy), :] = front[:, 0:LANES]
        out_ref[rows_of(3 * copy + 1), :] = front[:, LANES:]
        both = jnp.concatenate([place, place_det] * 3, axis=1)
        out_ref[rows_of(3 * copy + 2), :] = dot16(both, last, ((1,), (1,)))


def detector_solve(table):
    def moment(block, i, j):
        return table[8 * block + TERM_INDEX[(i, j)] : 8 * block + TERM_INDEX[(i, j)] + 1]

    def block_of(block):
        one, u, v = moment(block, 0, 0), moment(block, 1, 0), moment(block, 0, 1)
        uu = moment(block, 2, 0) + one * (1.0 / 3.0)
        vv = moment(block, 0, 2) + one * (1.0 / 3.0)
        uv = moment(block, 1, 1)
        return [[one, u, v], [u, uu, uv], [v, uv, vv]]

    part_xx, part_yy, part_xy = block_of(0), block_of(1), block_of(2)
    matrix = [part_xx[p] + part_xy[p] for p in range(3)] + [part_xy[p] + part_yy[p] for p in range(3)]
    at = [TERM_INDEX[term] for term in ((0, 0), (1, 0), (0, 1))]
    rhs = [table[24 + a : 25 + a] for a in at] + [table[28 + a : 29 + a] for a in at]
    for p in range(6):
        matrix[p][p] = matrix[p][p] + DETECTOR_DAMP
    inverse = [None] * 6
    lower = [[None] * 6 for _ in range(6)]
    for step in range(6):
        pivot = matrix[step][step]
        for before in range(step):
            pivot = pivot - lower[step][before] * lower[step][before]
        inverse[step] = 1.0 / jnp.sqrt(pivot)
        for row in range(step + 1, 6):
            value = matrix[row][step]
            for before in range(step):
                value = value - lower[row][before] * lower[step][before]
            lower[row][step] = value * inverse[step]
    forward = []
    for step in range(6):
        value = rhs[step]
        for before in range(step):
            value = value - lower[step][before] * forward[before]
        forward.append(value * inverse[step])
    answer = [None] * 6
    for step in range(5, -1, -1):
        value = forward[step]
        for after in range(step + 1, 6):
            value = value - lower[after][step] * answer[after]
        answer[step] = value * inverse[step]
    return answer


UNKNOWNS = [("x", q) for q in range(28)] + [("y", q) for q in range(24, 28)] + [("y", q) for q in range(24)]
SIZE = 2 * POLY
BLOCKS = SIZE // 8
PANEL = 4


def solve_kernel(arr_ref, expand_ref, scale_ref, upd_ref, resp_ref, wide, mat, rhs, invs, inv_rows):
    sub8 = iota((8, LANES), 0)
    rows128 = iota((LANES, LANES), 0)
    lanes128 = iota((LANES, LANES), 1)

    marks = [arr_ref[rows_of(3 * copy), :] for copy in range(2)]
    picks = [(mark[:, MARK : MARK + 1].astype(jnp.int32) == lanes128 + 1).astype(jnp.bfloat16) for mark in marks]
    pick = [
        (mark.T[MARK : MARK + 1].astype(jnp.int32) == rows128 + 1).astype(jnp.bfloat16) for mark in marks
    ]
    slots = [
        jnp.concatenate([marks[copy]] + [arr_ref[rows_of(3 * copy + block), :] for block in (1, 2)], axis=1)
        for copy in range(2)
    ]
    slots = split3(jnp.concatenate(slots, axis=0))
    table = dot16(jnp.concatenate(pick * 3, axis=1), jnp.concatenate(slots, axis=0), ((1,), (0,)))

    sums = [jnp.sum(arr_ref[rows_of(3 * copy + 2), :], axis=0, keepdims=True) for copy in range(2)]
    turned = jnp.where(rows128 == 0, sums[0], jnp.where(rows128 == 1, sums[1], 0.0)).T
    answer = detector_solve(turned[96:128])

    pieces = []
    for block in range(3):
        high, middle, low = split3(table[:, block * LANES : (block + 1) * LANES])
        pieces.append(jnp.concatenate([high, middle, high, middle, low, high], axis=1))
    parts = jnp.concatenate(pieces, axis=0)

    def expand(q0):
        at = pl.ds(q0 * 32, PANEL * 32)
        left = [expand_ref[at, side * LANES : (side + 1) * LANES] for side in (0, 0, 1, 1, 0, 2)]
        wide[at, :] = dot16(jnp.concatenate(left, axis=1), parts, ((1,), (1,)))

    def part(which, q, group):
        return wide[q * 32 + group * 8 : q * 32 + group * 8 + 8, which * LANES : (which + 1) * LANES]

    def entry(col, group):
        kind, q = UNKNOWNS[col]
        if kind == "x":
            if group < 3:
                value = part(0, q, group)
            elif group == 3:
                value = jnp.where(sub8 < 4, part(0, q, 3), pltpu.roll(part(2, q, 3), 4, 0))
            else:
                value = part(2, q, group - 4)
        elif group == 3:
            value = jnp.where(sub8 < 4, 0.0, pltpu.roll(part(1, q, 3), 4, 0))
        else:
            value = part(1, q, group - 4)
        if group == col // 8:
            value = value + jnp.where(sub8 == col % 8, EXPOSURE_DAMP, 0.0)
        return value

    expand(0)
    grad_x = table[:, 0:LANES].T[96:128] * scale_ref[...]
    grad_y = table[:, LANES : 2 * LANES].T[96:128] * scale_ref[...]
    rhs[0:24, :] = grad_x[0:24]
    rhs[24:32, :] = jnp.where(sub8 < 4, grad_x[24:32], pltpu.roll(grad_y[24:32], 4, 0))
    rhs[32:56, :] = grad_y[0:24]

    for k0 in range(0, SIZE, PANEL):
        g0 = k0 // 8
        count = BLOCKS - g0

        def update(j, carry):
            base = j * SIZE
            column = [mat[pl.ds(base + g * 8, 8), :] for g in range(g0, BLOCKS)]
            new = []
            for c in range(PANEL):
                factor = mat[pl.ds(base + k0 + c, 1), :]
                for g in range(count):
                    new.append(carry[c * count + g] - column[g] * factor)
            return tuple(new)

        if k0 + PANEL < POLY:
            expand(k0 + PANEL)
        panel = tuple(entry(k0 + c, g) for c in range(PANEL) for g in range(g0, BLOCKS))
        for j in range(k0):
            panel = update(j, panel)
        panel = [list(panel[c * count : (c + 1) * count]) for c in range(PANEL)]
        right = [rhs[pl.ds(g * 8, 8), :] for g in range(g0, BLOCKS)]
        for c in range(PANEL):
            k = k0 + c
            row = k % 8
            inverse = lax.rsqrt(panel[c][0][row : row + 1])
            column = [value * inverse for value in panel[c]]
            for other in range(c + 1, PANEL):
                factor = column[0][k0 % 8 + other : k0 % 8 + other + 1]
                panel[other] = [panel[other][g] - column[g] * factor for g in range(count)]
            forward = right[0][row : row + 1] * inverse
            keep = jnp.where(sub8 <= row, right[0], right[0] - column[0] * forward)
            keep = jnp.where(sub8 == row, forward, keep)
            right = [keep] + [right[g] - column[g] * forward for g in range(1, count)]
            invs[k : k + 1, :] = inverse
            for g in range(count):
                mat[pl.ds(k * SIZE + (g0 + g) * 8, 8), :] = column[g]
        if (k0 + PANEL) % 8 == 0:
            inverted = []
            for row in range(8):
                value = jnp.where(sub8 == row, 1.0, 0.0)
                for before in range(row):
                    factor = mat[pl.ds((g0 * 8 + before) * SIZE + g0 * 8 + row, 1), :]
                    value = value - factor * inverted[before]
                value = value * invs[pl.ds(g0 * 8 + row, 1), :]
                inverted.append(value)
                inv_rows[pl.ds((g0 * 8 + row) * 8, 8), :] = value
        for g in range(count):
            rhs[pl.ds((g0 + g) * 8, 8), :] = right[g]

    solved = [None] * BLOCKS
    for b in range(BLOCKS - 1, -1, -1):
        right = rhs[b * 8 : b * 8 + 8]
        if b < BLOCKS - 1:
            partial = []
            for c in range(8):
                total = None
                for g in range(b + 1, BLOCKS):
                    term = mat[pl.ds((b * 8 + c) * SIZE + g * 8, 8), :] * solved[g]
                    total = term if total is None else total + term
                partial.append(total)
            right = right - combine(partial, sub8)
        terms = [inv_rows[pl.ds((b * 8 + c) * 8, 8), :] * right[c : c + 1] for c in range(8)]
        while len(terms) > 1:
            terms = [terms[at] + terms[at + 1] for at in range(0, len(terms), 2)]
        solved[b] = terms[0]
    whole = jnp.concatenate(
        solved[0:3] + [solved[3][0:4]] + solved[4:7] + [solved[3][4:8]], axis=0
    )
    upd_ref[...] = whole

    lane1 = iota((1, LANES), 1)
    first = [jnp.where(lane1 == 0, value, 0.0) for value in answer]
    second = [jnp.where(lane1 == 1, value, 0.0) for value in answer]
    zeros = jnp.zeros((SIZE, LANES), F32)
    zero16 = jnp.zeros((16, LANES), F32)
    gap = [jnp.zeros((2, LANES), F32)]
    left = jnp.concatenate(picks + [(lanes128 < 2).astype(jnp.bfloat16)], axis=1)
    right = jnp.concatenate(
        [
            jnp.concatenate([whole, zeros, zero16], axis=0),
            jnp.concatenate([zeros, whole, zero16], axis=0),
            jnp.concatenate([zeros, zeros] + first + gap + second + gap, axis=0),
        ],
        axis=1,
    )
    left = jnp.concatenate([left] * 3, axis=1)
    resp_ref[...] = dot16(left, jnp.concatenate(split3(right), axis=1), ((1,), (1,)))


def star_kernel(base_ref, gain_ref, power_ref, where_ref, scale_ref, update_ref, resp_ref,
                star_ref, det_ref, update_out, coeff, model, sem):
    write = pltpu.make_async_copy(update_ref, update_out, sem)
    write.start()
    tiles = base_ref.shape[1]
    rows128 = iota((LANES, LANES), 0)
    turned = resp_ref[...].T
    det_ref[:, 0:LANES] = turned[112:118]
    det_ref[:, LANES:NCCD] = turned[120:126, 0 : NCCD - LANES]
    dest = where_ref[0:1]
    copy_at = where_ref[1:2]
    ccd = where_ref[2:3]
    picks = [((rows128 == dest) & (copy_at == c)).astype(jnp.bfloat16) for c in range(2)]
    dets = [(rows128 + LANES * c == ccd).astype(jnp.bfloat16) for c in range(2)]
    halves = split3(jnp.concatenate([turned[0:56], turned[56:112]], axis=1))
    exposure = dot16(jnp.concatenate(halves, axis=1), jnp.concatenate(picks * 3, axis=0), ((1,), (0,)))
    halves = split3(jnp.concatenate([turned[112:120], turned[120:128]], axis=1))
    detector = dot16(jnp.concatenate(halves, axis=1), jnp.concatenate(dets * 3, axis=0), ((1,), (0,)))
    scale = scale_ref[...]
    coeff[0:28, :] = exposure[0:28] * scale[0:28]
    coeff[32:60, :] = exposure[28:56] * scale[0:28]
    for axis in range(2):
        for m, term in enumerate(((0, 0), (1, 0), (0, 1))):
            row = 32 * axis + TERM_INDEX[term]
            coeff[row : row + 1, :] = coeff[row : row + 1, :] + detector[3 * axis + m : 3 * axis + m + 1]

    for g in range(LANES // 8):
        at = pl.ds(g * 8, 8)
        in_u = [None] + [power_ref[0, i, at, :] for i in range(ORDER)]
        in_v = [None] + [power_ref[1, i, at, :] for i in range(ORDER)]
        for axis in range(2):
            total = None
            for i in range(ORDER + 1):
                inner = None
                for j in range(ORDER - i + 1):
                    row = 32 * axis + TERM_INDEX[(i, j)]
                    term = coeff[row : row + 1, :]
                    if j:
                        term = term * in_v[j]
                    inner = term if inner is None else inner + term
                if i:
                    inner = inner * in_u[i]
                total = inner if total is None else total + inner
            model[axis, at, :] = total
    model_x = model[0].T
    model_y = model[1].T
    out_x = base_ref[0]
    out_y = base_ref[1]
    for visit in range(VISITS):
        at = slice(visit * tiles, (visit + 1) * tiles)
        out_x = out_x - (gain_ref[0, at, :] * model_x[at] + gain_ref[1, at, :] * model_y[at])
        out_y = out_y - (gain_ref[2, at, :] * model_x[at] + gain_ref[3, at, :] * model_y[at])
    star_ref[:, 0, :] = out_x
    star_ref[:, 1, :] = out_y
    write.wait()


def vmem(count):
    return [pl.BlockSpec(memory_space=pltpu.VMEM)] * count


def shards(focal_uv, offsets, w_diag, w_corr, star_count, exposure_ids, ccd_ids, exp_slot):
    tiles = offsets.shape[0]
    flat = (tiles * VISITS * 2, LANES)
    inputs = (
        focal_uv.reshape(flat),
        offsets.reshape(flat),
        w_diag.reshape(flat),
        jnp.transpose(w_corr, (1, 0, 2)),
        star_count.reshape(1, tiles),
        exposure_ids.T,
        ccd_ids.T,
        exp_slot.reshape(LANES, LANES),
    )
    shape = jax.ShapeDtypeStruct
    tables = (jnp.asarray(expansion()), jnp.asarray(scale_rows()))
    outgoing, powers, where, base, gain, expand, scale = pl.pallas_call(
        moments_kernel,
        out_shape=(
            shape((6 * LANES, LANES), F32),
            shape((2, ORDER, LANES, LANES), F32),
            shape((8, LANES), jnp.int32),
            shape((2, tiles, LANES), F32),
            shape((4, tiles * VISITS, LANES), F32),
            *(shape(array.shape, array.dtype) for array in tables),
        ),
        in_specs=[pl.BlockSpec(memory_space=pltpu.HBM)] * 10,
        out_specs=tuple(vmem(7)),
        scratch_shapes=[pltpu.VMEM(array.shape, array.dtype) for array in inputs]
        + [
            pltpu.SemaphoreType.DMA((10,)),
            pltpu.VMEM((7, LANES, LANES), F32),
            pltpu.VMEM((2, ORDER, LANES, LANES), F32),
            pltpu.VMEM((ROW_DET * 8, LANES), F32),
            pltpu.VMEM((ROW_DET, LANES), F32),
        ],
        compiler_params=pltpu.CompilerParams(vmem_limit_bytes=12 << 20),
        name="moments",
    )(*(pltpu.with_memory_space_constraint(array, pltpu.HBM) for array in (*inputs, *tables)))
    arrived = lax.all_to_all(outgoing.reshape(LANES, 1, 6 * LANES), ("shard", "field"), 0, 0, tiled=True)
    arrived = arrived.reshape(6 * LANES, LANES)
    update, answers = pl.pallas_call(
        solve_kernel,
        out_shape=(shape((SIZE, LANES), F32), shape((LANES, LANES), F32)),
        in_specs=vmem(3),
        out_specs=tuple(vmem(2)),
        scratch_shapes=[
            pltpu.VMEM((POLY * 32, 3 * LANES), F32),
            pltpu.VMEM((SIZE * SIZE, LANES), F32),
            pltpu.VMEM((SIZE, LANES), F32),
            pltpu.VMEM((SIZE, LANES), F32),
            pltpu.VMEM((SIZE * 8, LANES), F32),
        ],
        compiler_params=pltpu.CompilerParams(vmem_limit_bytes=12 << 20),
        name="solve",
    )(arrived, expand, scale)
    replies = lax.all_to_all(answers.reshape(LANES, 1, LANES), ("shard", "field"), 0, 0, tiled=True)
    star_update, ccd_update, update = pl.pallas_call(
        star_kernel,
        out_shape=(shape((tiles, 2, LANES), F32), shape((6, NCCD), F32), shape((SIZE, LANES), F32)),
        in_specs=vmem(7),
        out_specs=(*vmem(2), pl.BlockSpec(memory_space=pltpu.HBM)),
        scratch_shapes=[
            pltpu.VMEM((64, LANES), F32),
            pltpu.VMEM((2, LANES, LANES), F32),
            pltpu.SemaphoreType.DMA,
        ],
        compiler_params=pltpu.CompilerParams(vmem_limit_bytes=12 << 20),
        name="stars",
    )(base, gain, powers, where, scale, update, replies.reshape(LANES, LANES))
    return star_update, update, ccd_update.T


def solution(mesh):
    both = ("field", "shard")
    in_specs = (
        P(both, None, None, None),
        P(both, None, None, None),
        P(both, None, None, None),
        P(both, None, None),
        P(both),
        P(both, None),
        P(both, None),
        P(),
    )
    out_specs = (P(both, None, None), P(None, both), P())
    return jax.shard_map(shards, mesh=mesh, in_specs=in_specs, out_specs=out_specs, check_vma=False)
```

```python
import math

import jax
import jax.numpy as jnp
import numpy as np
from jax import lax
from jax.experimental import pallas as pl
from jax.experimental.pallas import tpu as pltpu
from jax.sharding import PartitionSpec as P

ORDER = 6
POLY = 28
VISITS = 6
NCCD = 189
LANES = 128
STAR_DAMP = 0.1
EXPOSURE_DAMP = 1.0
DETECTOR_DAMP = 1.0
DEG2 = 2 * ORDER
UNROLL = 8
F32 = jnp.float32

TERMS = [(i, n - i) for n in range(DEG2 + 1) for i in range(n + 1)]
TERM_INDEX = {term: at for at, term in enumerate(TERMS)}
LEAD = [math.factorial(2 * n) / (2**n * math.factorial(n) ** 2) for n in range(DEG2 + 1)]
NORM = [math.sqrt((2 * i + 1) * (2 * j + 1)) for i, j in TERMS[:POLY]]
SCALE = [norm * LEAD[i] * LEAD[j] for norm, (i, j) in zip(NORM, TERMS)]

ROW_GX = 96
ROW_GY = 224
ROW_DET = 352
MARK = 95


def linearisation():
    from numpy.polynomial import legendre

    table = np.zeros((ORDER + 1, ORDER + 1, DEG2 + 1))
    for m in range(ORDER + 1):
        for n in range(ORDER + 1):
            product = legendre.legmul([0] * m + [1], [0] * n + [1])
            table[m, n, : len(product)] = product
    return table


def expansion():
    table = linearisation()
    matrix = np.zeros((POLY * 32, LANES))
    for q, (iq, jq) in enumerate(TERMS[:POLY]):
        for p, (ip, jp) in enumerate(TERMS[:POLY]):
            for at, (a, b) in enumerate(TERMS):
                product = table[ip, iq, a] * LEAD[a] * table[jp, jq, b] * LEAD[b]
                matrix[q * 32 + p, at] = NORM[p] * NORM[q] * product
    parts = []
    rest = matrix
    for _ in range(3):
        part = rest.astype(jnp.bfloat16)
        parts.append(part)
        rest = rest - part.astype(np.float64)
    high, middle, low = parts
    return np.concatenate([high, middle, low], 1)


def scale_rows():
    rows = np.zeros((32, LANES), np.float32)
    rows[:POLY] = np.array(SCALE, np.float32)[:, None]
    return rows


def split3(value):
    high = value.astype(jnp.bfloat16)
    rest = value - high.astype(F32)
    middle = rest.astype(jnp.bfloat16)
    return high, middle, (rest - middle.astype(F32)).astype(jnp.bfloat16)


def dot16(a, b, dims):
    return lax.dot_general(a, b, (dims, ((), ())), preferred_element_type=F32)


def rows_of(part):
    return pl.ds(part, LANES, stride=6)


def iota(shape, axis):
    return lax.broadcasted_iota(jnp.int32, shape, axis)


def legendre(value, count):
    values = [None, value]
    for degree in range(1, count - 1):
        before = values[degree - 1] if degree > 1 else 1.0
        values.append(value * values[degree] - (degree * degree / (4 * degree * degree - 1)) * before)
    return values


def star_terms(off_ref, diag_ref, corr_ref, counts):
    tiles = corr_ref.shape[1]
    lanes = iota((tiles, LANES), 1)
    counts = jnp.broadcast_to(counts.astype(F32), (tiles, tiles))
    square = (iota((tiles, tiles), 0) == iota((tiles, tiles), 1)).astype(F32)
    column = jnp.sum(counts * square, axis=1, keepdims=True)
    present = (lanes.astype(F32) < column).astype(F32)

    def rows(ref, visit, part):
        return ref[pl.ds(2 * visit + part, tiles, stride=2 * VISITS), :]

    weights = []
    resid = []
    for visit in range(VISITS):
        d0 = rows(diag_ref, visit, 0)
        d1 = rows(diag_ref, visit, 1)
        weights.append((d0 * present, d1 * present, corr_ref[visit] * jnp.sqrt(d0 * d1) * present))
        resid.append((rows(off_ref, visit, 0), rows(off_ref, visit, 1)))
    hess_xx = sum(w[0] for w in weights) + STAR_DAMP
    hess_yy = sum(w[1] for w in weights) + STAR_DAMP
    hess_xy = sum(w[2] for w in weights)
    determ = hess_xx * hess_yy - hess_xy * hess_xy
    inverse = (hess_yy / determ, hess_xx / determ, -hess_xy / determ)
    return weights, resid, inverse


def apply_inverse(inverse, x, y):
    inv_xx, inv_yy, inv_xy = inverse
    return inv_xx * x + inv_xy * y, inv_xy * x + inv_yy * y


def combine(values, sub):
    for shift in (4, 2, 1):
        low = (sub & shift) == 0
        half = len(values) // 2
        merged = []
        for at in range(half):
            a, b = values[at], values[at + half]
            if shift == 4:
                merged.append(jnp.where(low, a, b) + pltpu.roll(jnp.where(low, b, a), 4, 0))
            else:
                merged.append(jnp.where(low, a + pltpu.roll(a, 8 - shift, 0), b + pltpu.roll(b, shift, 0)))
        values = merged
    return values[0]


def moments_kernel(*refs):
    sources, out_refs, buffers, (sems, *scratch) = refs[:10], refs[10:17], refs[17:25], refs[25:]
    copies = [
        pltpu.make_async_copy(source, buffer, sems.at[at])
        for at, (source, buffer) in enumerate(zip(sources, (*buffers, *out_refs[5:])))
    ]
    for copy in copies:
        copy.start()
    for copy in copies[:8]:
        copy.wait()
    moments_body(*buffers, *out_refs[:5], *scratch)
    for copy in copies[8:]:
        copy.wait()


def moments_body(uv_ref, off_ref, diag_ref, corr_ref, count_ref, ids_ref, ccd_ref, slot_ref,
                 out_ref, power_ref, where_ref, base_ref, gain_ref, chan, high_power, acc, mom):
    tiles = corr_ref.shape[1]
    visits_all = tiles * VISITS
    sub8 = iota((8, LANES), 0)

    pad = jnp.zeros((LANES - visits_all, LANES), F32)
    mine = iota((VISITS, LANES), 1) // tiles == iota((VISITS, LANES), 0)

    def along_lanes(ref):
        spread = jnp.concatenate([ref[...]] * (LANES // tiles), axis=1)
        return jnp.sum(jnp.where(mine, spread, 0), axis=0, keepdims=True)

    ident = along_lanes(ids_ref)
    ccd = along_lanes(ccd_ref)
    rows128 = iota((LANES, LANES), 0)
    lanes128 = iota((LANES, LANES), 1)
    valid = iota((1, LANES), 1) < visits_all
    slot = slot_ref[...]
    digits = jnp.concatenate([slot // LANES, slot % LANES], axis=1).astype(F32).astype(jnp.bfloat16)
    picked = dot16(digits, (rows128 == ident // LANES).astype(jnp.bfloat16), ((0,), (0,)))
    inside = rows128 == ident % LANES

    def digit(at):
        chosen = jnp.where(inside, picked[at * LANES : (at + 1) * LANES], 0.0)
        return (jnp.sum(chosen, axis=0, keepdims=True) + 0.5).astype(jnp.int32)

    home, place_in = digit(0), digit(1)
    dest = jnp.where(valid, home % 32 * 4 + home // 32, -1)
    ccd = jnp.where(valid, ccd, -1)
    dest_t = jnp.broadcast_to(dest.astype(F32), (LANES, LANES)).T.astype(jnp.int32)
    same = (dest_t == dest) & (rows128 < lanes128)
    copy_at = jnp.sum(same.astype(F32), axis=0, keepdims=True).astype(jnp.int32)
    mark = (place_in + 1).astype(F32)
    counts = jnp.concatenate([count_ref[...]] * (LANES // tiles), axis=1)
    where_ref[...] = jnp.where(
        sub8 == 0, dest, jnp.where(sub8 == 1, copy_at, jnp.where(sub8 == 2, ccd, counts))
    )

    weights, resid, inverse = star_terms(off_ref, diag_ref, corr_ref, count_ref[...])
    grad_x = sum(w[0] * r[0] + w[2] * r[1] for w, r in zip(weights, resid))
    grad_y = sum(w[2] * r[0] + w[1] * r[1] for w, r in zip(weights, resid))
    shift_x, shift_y = apply_inverse(inverse, grad_x, grad_y)
    base_ref[0] = shift_x
    base_ref[1] = shift_y
    inv_xx, inv_yy, inv_xy = inverse
    channels = [[] for _ in range(7)]
    for visit in range(VISITS):
        w_xx, w_yy, w_xy = weights[visit]
        left_x = resid[visit][0] - shift_x
        left_y = resid[visit][1] - shift_y
        prod_11 = inv_xx * w_xx + inv_xy * w_xy
        prod_12 = inv_xx * w_xy + inv_xy * w_yy
        prod_21 = inv_xy * w_xx + inv_yy * w_xy
        prod_22 = inv_xy * w_xy + inv_yy * w_yy
        for at, product in enumerate((prod_11, prod_12, prod_21, prod_22)):
            gain_ref[at, pl.ds(visit * tiles, tiles), :] = product
        values = (
            uv_ref[pl.ds(2 * visit, tiles, stride=2 * VISITS), :],
            uv_ref[pl.ds(2 * visit + 1, tiles, stride=2 * VISITS), :],
            w_xx - (w_xx * prod_11 + w_xy * prod_21),
            w_yy - (w_xy * prod_12 + w_yy * prod_22),
            w_xy - (w_xx * prod_12 + w_xy * prod_22),
            w_xx * left_x + w_xy * left_y,
            w_xy * left_x + w_yy * left_y,
        )
        for at, value in enumerate(values):
            channels[at].append(value)
    for at in range(7):
        chan[at] = jnp.concatenate(channels[at] + [pad], axis=0).T

    groups = LANES // 8

    for g in range(groups):
        at = pl.ds(g * 8, 8)
        for source in range(2):
            for degree, value in enumerate(legendre(chan[source, at, :], DEG2 + 1)):
                if degree > ORDER:
                    high_power[source, degree - ORDER - 1, at, :] = value
                elif degree:
                    power_ref[source, degree - 1, at, :] = value

    def power(source, degree, at):
        if degree > ORDER:
            return high_power[source, degree - ORDER - 1, at, :]
        return power_ref[source, degree - 1, at, :]

    def sweep(i, top, first, count, row0, width):
        heights = top - i + 1

        def step(g, sums):
            at = pl.ds(pl.multiple_of(g * 8, 8), 8)
            scaled = [chan[first + w, at, :] for w in range(count)]
            if i:
                factor = power(0, i, at)
                scaled = [value * factor for value in scaled]
            new = []
            for j in range(heights):
                other = power(1, j, at) if j else None
                for w in range(count):
                    term = scaled[w] * other if j else scaled[w]
                    new.append(sums[j * count + w] + term)
            return tuple(new)

        start = tuple(jnp.zeros((8, LANES), F32) for _ in range(heights * count))
        sums = lax.fori_loop(0, groups, step, start, unroll=UNROLL)
        for j in range(heights):
            for w in range(count):
                row = row0 + w * width + TERM_INDEX[(i, j)]
                acc[pl.ds(row * 8, 8), :] = sums[j * count + w]

    for i in range(DEG2 + 1):
        sweep(i, DEG2, 2, 3, 0, LANES)
    for i in range(ORDER + 1):
        sweep(i, ORDER, 5, 2, ROW_GX, LANES)
    zero = jnp.zeros((8, LANES), F32)
    for block in range(3):
        for row in range(len(TERMS), 96):
            acc[pl.ds((block * LANES + row) * 8, 8), :] = zero
    for block in range(2):
        for row in range(POLY, 32):
            acc[pl.ds((ROW_GX + block * LANES + row) * 8, 8), :] = zero

    for g in range(ROW_DET // 8):
        mom[pl.ds(g * 8, 8), :] = combine([acc[pl.ds(g * 64 + 8 * s, 8), :] for s in range(8)], sub8)
    mom[88:96, :] = jnp.where(sub8 == 7, mark, mom[88:96, :])

    pulls = jnp.where(sub8 < 4, mom[ROW_GX : ROW_GX + 8], pltpu.roll(mom[ROW_GY : ROW_GY + 8], 4, 0))
    zero32 = jnp.zeros((32, LANES), F32)
    zero96 = jnp.zeros((96, LANES), F32)
    first = split3(mom[0:256])
    third = split3(jnp.concatenate([mom[256:352], zero32], axis=0))
    fourth = split3(jnp.concatenate([zero96, mom[0:8], mom[128:136], mom[256:264], pulls], axis=0))
    first = jnp.concatenate(first, axis=1)
    last = jnp.concatenate([piece for parts in zip(third, fourth) for piece in parts], axis=1)
    for copy in range(2):
        place = ((rows128 == dest) & (copy_at == copy)).astype(jnp.bfloat16)
        place_det = (rows128 + LANES * copy == ccd).astype(jnp.bfloat16)
        front = dot16(jnp.concatenate([place] * 3, axis=1), first, ((1,), (1,)))
        out_ref[rows_of(3 * copy), :] = front[:, 0:LANES]
        out_ref[rows_of(3 * copy + 1), :] = front[:, LANES:]
        both = jnp.concatenate([place, place_det] * 3, axis=1)
        out_ref[rows_of(3 * copy + 2), :] = dot16(both, last, ((1,), (1,)))


def detector_solve(table):
    def moment(block, i, j):
        return table[8 * block + TERM_INDEX[(i, j)] : 8 * block + TERM_INDEX[(i, j)] + 1]

    def block_of(block):
        one, u, v = moment(block, 0, 0), moment(block, 1, 0), moment(block, 0, 1)
        uu = moment(block, 2, 0) + one * (1.0 / 3.0)
        vv = moment(block, 0, 2) + one * (1.0 / 3.0)
        uv = moment(block, 1, 1)
        return [[one, u, v], [u, uu, uv], [v, uv, vv]]

    part_xx, part_yy, part_xy = block_of(0), block_of(1), block_of(2)
    matrix = [part_xx[p] + part_xy[p] for p in range(3)] + [part_xy[p] + part_yy[p] for p in range(3)]
    at = [TERM_INDEX[term] for term in ((0, 0), (1, 0), (0, 1))]
    rhs = [table[24 + a : 25 + a] for a in at] + [table[28 + a : 29 + a] for a in at]
    for p in range(6):
        matrix[p][p] = matrix[p][p] + DETECTOR_DAMP
    inverse = [None] * 6
    lower = [[None] * 6 for _ in range(6)]
    for step in range(6):
        pivot = matrix[step][step]
        for before in range(step):
            pivot = pivot - lower[step][before] * lower[step][before]
        inverse[step] = 1.0 / jnp.sqrt(pivot)
        for row in range(step + 1, 6):
            value = matrix[row][step]
            for before in range(step):
                value = value - lower[row][before] * lower[step][before]
            lower[row][step] = value * inverse[step]
    forward = []
    for step in range(6):
        value = rhs[step]
        for before in range(step):
            value = value - lower[step][before] * forward[before]
        forward.append(value * inverse[step])
    answer = [None] * 6
    for step in range(5, -1, -1):
        value = forward[step]
        for after in range(step + 1, 6):
            value = value - lower[after][step] * answer[after]
        answer[step] = value * inverse[step]
    return answer


UNKNOWNS = [("x", q) for q in range(28)] + [("y", q) for q in range(24, 28)] + [("y", q) for q in range(24)]
SIZE = 2 * POLY
BLOCKS = SIZE // 8
PANEL = 4


def solve_kernel(arr_ref, expand_ref, scale_ref, upd_ref, resp_ref, wide, mat, rhs, invs, inv_rows):
    sub8 = iota((8, LANES), 0)
    rows128 = iota((LANES, LANES), 0)
    lanes128 = iota((LANES, LANES), 1)

    marks = [arr_ref[rows_of(3 * copy), :] for copy in range(2)]
    picks = [(mark[:, MARK : MARK + 1].astype(jnp.int32) == lanes128 + 1).astype(jnp.bfloat16) for mark in marks]
    pick = [
        (mark.T[MARK : MARK + 1].astype(jnp.int32) == rows128 + 1).astype(jnp.bfloat16) for mark in marks
    ]
    slots = [
        jnp.concatenate([marks[copy]] + [arr_ref[rows_of(3 * copy + block), :] for block in (1, 2)], axis=1)
        for copy in range(2)
    ]
    slots = split3(jnp.concatenate(slots, axis=0))
    table = dot16(jnp.concatenate(pick * 3, axis=1), jnp.concatenate(slots, axis=0), ((1,), (0,)))

    sums = [jnp.sum(arr_ref[rows_of(3 * copy + 2), :], axis=0, keepdims=True) for copy in range(2)]
    turned = jnp.where(rows128 == 0, sums[0], jnp.where(rows128 == 1, sums[1], 0.0)).T
    answer = detector_solve(turned[96:128])

    pieces = []
    for block in range(3):
        high, middle, low = split3(table[:, block * LANES : (block + 1) * LANES])
        pieces.append(jnp.concatenate([high, middle, high, middle, low, high], axis=1))
    parts = jnp.concatenate(pieces, axis=0)

    def expand(q0):
        at = pl.ds(q0 * 32, PANEL * 32)
        left = [expand_ref[at, side * LANES : (side + 1) * LANES] for side in (0, 0, 1, 1, 0, 2)]
        wide[at, :] = dot16(jnp.concatenate(left, axis=1), parts, ((1,), (1,)))

    def part(which, q, group):
        return wide[q * 32 + group * 8 : q * 32 + group * 8 + 8, which * LANES : (which + 1) * LANES]

    def entry(col, group):
        kind, q = UNKNOWNS[col]
        if kind == "x":
            if group < 3:
                value = part(0, q, group)
            elif group == 3:
                value = jnp.where(sub8 < 4, part(0, q, 3), pltpu.roll(part(2, q, 3), 4, 0))
            else:
                value = part(2, q, group - 4)
        elif group == 3:
            value = jnp.where(sub8 < 4, 0.0, pltpu.roll(part(1, q, 3), 4, 0))
        else:
            value = part(1, q, group - 4)
        if group == col // 8:
            value = value + jnp.where(sub8 == col % 8, EXPOSURE_DAMP, 0.0)
        return value

    expand(0)
    expand(PANEL)
    grad_x = table[:, 0:LANES].T[96:128] * scale_ref[...]
    grad_y = table[:, LANES : 2 * LANES].T[96:128] * scale_ref[...]
    rhs[0:24, :] = grad_x[0:24]
    rhs[24:32, :] = jnp.where(sub8 < 4, grad_x[24:32], pltpu.roll(grad_y[24:32], 4, 0))
    rhs[32:56, :] = grad_y[0:24]

    for k0 in range(0, SIZE, PANEL):
        g0 = k0 // 8
        count = BLOCKS - g0

        def update(j, carry):
            base = j * SIZE
            column = [mat[pl.ds(base + g * 8, 8), :] for g in range(g0, BLOCKS)]
            new = []
            for c in range(PANEL):
                factor = mat[pl.ds(base + k0 + c, 1), :]
                for g in range(count):
                    new.append(carry[c * count + g] - column[g] * factor)
            return tuple(new)

        if k0 + 2 * PANEL < POLY:
            expand(k0 + 2 * PANEL)
        panel = tuple(entry(k0 + c, g) for c in range(PANEL) for g in range(g0, BLOCKS))
        for j in range(k0):
            panel = update(j, panel)
        panel = [list(panel[c * count : (c + 1) * count]) for c in range(PANEL)]
        right = [rhs[pl.ds(g * 8, 8), :] for g in range(g0, BLOCKS)]
        for c in range(PANEL):
            k = k0 + c
            row = k % 8
            inverse = lax.rsqrt(panel[c][0][row : row + 1])
            column = [value * inverse for value in panel[c]]
            for other in range(c + 1, PANEL):
                factor = column[0][k0 % 8 + other : k0 % 8 + other + 1]
                panel[other] = [panel[other][g] - column[g] * factor for g in range(count)]
            forward = right[0][row : row + 1] * inverse
            keep = jnp.where(sub8 <= row, right[0], right[0] - column[0] * forward)
            keep = jnp.where(sub8 == row, forward, keep)
            right = [keep] + [right[g] - column[g] * forward for g in range(1, count)]
            invs[k : k + 1, :] = inverse
            for g in range(count):
                mat[pl.ds(k * SIZE + (g0 + g) * 8, 8), :] = column[g]
        if (k0 + PANEL) % 8 == 0:
            inverted = []
            for row in range(8):
                value = jnp.where(sub8 == row, 1.0, 0.0)
                for before in range(row):
                    factor = mat[pl.ds((g0 * 8 + before) * SIZE + g0 * 8 + row, 1), :]
                    value = value - factor * inverted[before]
                value = value * invs[pl.ds(g0 * 8 + row, 1), :]
                inverted.append(value)
                inv_rows[pl.ds((g0 * 8 + row) * 8, 8), :] = value
        for g in range(count):
            rhs[pl.ds((g0 + g) * 8, 8), :] = right[g]

    solved = [None] * BLOCKS
    for b in range(BLOCKS - 1, -1, -1):
        right = rhs[b * 8 : b * 8 + 8]
        if b < BLOCKS - 1:
            partial = []
            for c in range(8):
                total = None
                for g in range(b + 1, BLOCKS):
                    term = mat[pl.ds((b * 8 + c) * SIZE + g * 8, 8), :] * solved[g]
                    total = term if total is None else total + term
                partial.append(total)
            right = right - combine(partial, sub8)
        terms = [inv_rows[pl.ds((b * 8 + c) * 8, 8), :] * right[c : c + 1] for c in range(8)]
        while len(terms) > 1:
            terms = [terms[at] + terms[at + 1] for at in range(0, len(terms), 2)]
        solved[b] = terms[0]
    whole = jnp.concatenate(
        solved[0:3] + [solved[3][0:4]] + solved[4:7] + [solved[3][4:8]], axis=0
    )
    upd_ref[...] = whole

    lane1 = iota((1, LANES), 1)
    first = [jnp.where(lane1 == 0, value, 0.0) for value in answer]
    second = [jnp.where(lane1 == 1, value, 0.0) for value in answer]
    zeros = jnp.zeros((SIZE, LANES), F32)
    zero16 = jnp.zeros((16, LANES), F32)
    gap = [jnp.zeros((2, LANES), F32)]
    left = jnp.concatenate(picks + [(lanes128 < 2).astype(jnp.bfloat16)], axis=1)
    right = jnp.concatenate(
        [
            jnp.concatenate([whole, zeros, zero16], axis=0),
            jnp.concatenate([zeros, whole, zero16], axis=0),
            jnp.concatenate([zeros, zeros] + first + gap + second + gap, axis=0),
        ],
        axis=1,
    )
    left = jnp.concatenate([left] * 3, axis=1)
    resp_ref[...] = dot16(left, jnp.concatenate(split3(right), axis=1), ((1,), (1,)))


def star_kernel(base_ref, gain_ref, power_ref, where_ref, scale_ref, update_ref, resp_ref,
                star_ref, det_ref, update_out, coeff, model, sem):
    write = pltpu.make_async_copy(update_ref, update_out, sem)
    write.start()
    tiles = base_ref.shape[1]
    rows128 = iota((LANES, LANES), 0)
    turned = resp_ref[...].T
    det_ref[:, 0:LANES] = turned[112:118]
    det_ref[:, LANES:NCCD] = turned[120:126, 0 : NCCD - LANES]
    dest = where_ref[0:1]
    copy_at = where_ref[1:2]
    ccd = where_ref[2:3]
    picks = [((rows128 == dest) & (copy_at == c)).astype(jnp.bfloat16) for c in range(2)]
    dets = [(rows128 + LANES * c == ccd).astype(jnp.bfloat16) for c in range(2)]
    halves = split3(jnp.concatenate([turned[0:56], turned[56:112]], axis=1))
    exposure = dot16(jnp.concatenate(halves, axis=1), jnp.concatenate(picks * 3, axis=0), ((1,), (0,)))
    halves = split3(jnp.concatenate([turned[112:120], turned[120:128]], axis=1))
    detector = dot16(jnp.concatenate(halves, axis=1), jnp.concatenate(dets * 3, axis=0), ((1,), (0,)))
    scale = scale_ref[...]
    coeff[0:28, :] = exposure[0:28] * scale[0:28]
    coeff[32:60, :] = exposure[28:56] * scale[0:28]
    for axis in range(2):
        for m, term in enumerate(((0, 0), (1, 0), (0, 1))):
            row = 32 * axis + TERM_INDEX[term]
            coeff[row : row + 1, :] = coeff[row : row + 1, :] + detector[3 * axis + m : 3 * axis + m + 1]

    for g in range(LANES // 8):
        at = pl.ds(g * 8, 8)
        in_u = [None] + [power_ref[0, i, at, :] for i in range(ORDER)]
        in_v = [None] + [power_ref[1, i, at, :] for i in range(ORDER)]
        for axis in range(2):
            total = None
            for i in range(ORDER + 1):
                inner = None
                for j in range(ORDER - i + 1):
                    row = 32 * axis + TERM_INDEX[(i, j)]
                    term = coeff[row : row + 1, :]
                    if j:
                        term = term * in_v[j]
                    inner = term if inner is None else inner + term
                if i:
                    inner = inner * in_u[i]
                total = inner if total is None else total + inner
            model[axis, at, :] = total
    model_x = model[0].T
    model_y = model[1].T
    out_x = base_ref[0]
    out_y = base_ref[1]
    for visit in range(VISITS):
        at = slice(visit * tiles, (visit + 1) * tiles)
        out_x = out_x - (gain_ref[0, at, :] * model_x[at] + gain_ref[1, at, :] * model_y[at])
        out_y = out_y - (gain_ref[2, at, :] * model_x[at] + gain_ref[3, at, :] * model_y[at])
    star_ref[:, 0, :] = out_x
    star_ref[:, 1, :] = out_y
    write.wait()


def vmem(count):
    return [pl.BlockSpec(memory_space=pltpu.VMEM)] * count


def shards(focal_uv, offsets, w_diag, w_corr, star_count, exposure_ids, ccd_ids, exp_slot):
    tiles = offsets.shape[0]
    flat = (tiles * VISITS * 2, LANES)
    inputs = (
        focal_uv.reshape(flat),
        offsets.reshape(flat),
        w_diag.reshape(flat),
        jnp.transpose(w_corr, (1, 0, 2)),
        star_count.reshape(1, tiles),
        exposure_ids.T,
        ccd_ids.T,
        exp_slot.reshape(LANES, LANES),
    )
    shape = jax.ShapeDtypeStruct
    tables = (jnp.asarray(expansion()), jnp.asarray(scale_rows()))
    outgoing, powers, where, base, gain, expand, scale = pl.pallas_call(
        moments_kernel,
        out_shape=(
            shape((6 * LANES, LANES), F32),
            shape((2, ORDER, LANES, LANES), F32),
            shape((8, LANES), jnp.int32),
            shape((2, tiles, LANES), F32),
            shape((4, tiles * VISITS, LANES), F32),
            *(shape(array.shape, array.dtype) for array in tables),
        ),
        in_specs=[pl.BlockSpec(memory_space=pltpu.HBM)] * 10,
        out_specs=tuple(vmem(7)),
        scratch_shapes=[pltpu.VMEM(array.shape, array.dtype) for array in inputs]
        + [
            pltpu.SemaphoreType.DMA((10,)),
            pltpu.VMEM((7, LANES, LANES), F32),
            pltpu.VMEM((2, ORDER, LANES, LANES), F32),
            pltpu.VMEM((ROW_DET * 8, LANES), F32),
            pltpu.VMEM((ROW_DET, LANES), F32),
        ],
        compiler_params=pltpu.CompilerParams(vmem_limit_bytes=12 << 20),
        name="moments",
    )(*(pltpu.with_memory_space_constraint(array, pltpu.HBM) for array in (*inputs, *tables)))
    arrived = lax.all_to_all(outgoing.reshape(LANES, 1, 6 * LANES), ("shard", "field"), 0, 0, tiled=True)
    arrived = arrived.reshape(6 * LANES, LANES)
    update, answers = pl.pallas_call(
        solve_kernel,
        out_shape=(shape((SIZE, LANES), F32), shape((LANES, LANES), F32)),
        in_specs=vmem(3),
        out_specs=tuple(vmem(2)),
        scratch_shapes=[
            pltpu.VMEM((POLY * 32, 3 * LANES), F32),
            pltpu.VMEM((SIZE * SIZE, LANES), F32),
            pltpu.VMEM((SIZE, LANES), F32),
            pltpu.VMEM((SIZE, LANES), F32),
            pltpu.VMEM((SIZE * 8, LANES), F32),
        ],
        compiler_params=pltpu.CompilerParams(vmem_limit_bytes=12 << 20),
        name="solve",
    )(arrived, expand, scale)
    replies = lax.all_to_all(answers.reshape(LANES, 1, LANES), ("shard", "field"), 0, 0, tiled=True)
    star_update, ccd_update, update = pl.pallas_call(
        star_kernel,
        out_shape=(shape((tiles, 2, LANES), F32), shape((6, NCCD), F32), shape((SIZE, LANES), F32)),
        in_specs=vmem(7),
        out_specs=(*vmem(2), pl.BlockSpec(memory_space=pltpu.HBM)),
        scratch_shapes=[
            pltpu.VMEM((64, LANES), F32),
            pltpu.VMEM((2, LANES, LANES), F32),
            pltpu.SemaphoreType.DMA,
        ],
        compiler_params=pltpu.CompilerParams(vmem_limit_bytes=12 << 20),
        name="stars",
    )(base, gain, powers, where, scale, update, replies.reshape(LANES, LANES))
    return star_update, update, ccd_update.T


def solution(mesh):
    both = ("field", "shard")
    in_specs = (
        P(both, None, None, None),
        P(both, None, None, None),
        P(both, None, None, None),
        P(both, None, None),
        P(both),
        P(both, None),
        P(both, None),
        P(),
    )
    out_specs = (P(both, None, None), P(None, both), P())
    return jax.shard_map(shards, mesh=mesh, in_specs=in_specs, out_specs=out_specs, check_vma=False)
```

```python
import math

import jax
import jax.numpy as jnp
import numpy as np
from jax import lax
from jax.experimental import pallas as pl
from jax.experimental.pallas import tpu as pltpu
from jax.sharding import PartitionSpec as P

ORDER = 6
POLY = 28
VISITS = 6
NCCD = 189
LANES = 128
STAR_DAMP = 0.1
EXPOSURE_DAMP = 1.0
DETECTOR_DAMP = 1.0
DEG2 = 2 * ORDER
UNROLL = 4
F32 = jnp.float32

TERMS = [(i, n - i) for n in range(DEG2 + 1) for i in range(n + 1)]
TERM_INDEX = {term: at for at, term in enumerate(TERMS)}
LEAD = [math.factorial(2 * n) / (2**n * math.factorial(n) ** 2) for n in range(DEG2 + 1)]
NORM = [math.sqrt((2 * i + 1) * (2 * j + 1)) for i, j in TERMS[:POLY]]
SCALE = [norm * LEAD[i] * LEAD[j] for norm, (i, j) in zip(NORM, TERMS)]

ROW_GX = 96
ROW_GY = 224
ROW_DET = 352
MARK = 95


def linearisation():
    from numpy.polynomial import legendre

    table = np.zeros((ORDER + 1, ORDER + 1, DEG2 + 1))
    for m in range(ORDER + 1):
        for n in range(ORDER + 1):
            product = legendre.legmul([0] * m + [1], [0] * n + [1])
            table[m, n, : len(product)] = product
    return table


def expansion():
    table = linearisation()
    matrix = np.zeros((POLY * 32, LANES))
    for q, (iq, jq) in enumerate(TERMS[:POLY]):
        for p, (ip, jp) in enumerate(TERMS[:POLY]):
            for at, (a, b) in enumerate(TERMS):
                product = table[ip, iq, a] * LEAD[a] * table[jp, jq, b] * LEAD[b]
                matrix[q * 32 + p, at] = NORM[p] * NORM[q] * product
    parts = []
    rest = matrix
    for _ in range(3):
        part = rest.astype(jnp.bfloat16)
        parts.append(part)
        rest = rest - part.astype(np.float64)
    high, middle, low = parts
    return np.concatenate([high, middle, low], 1)


def scale_rows():
    rows = np.zeros((32, LANES), np.float32)
    rows[:POLY] = np.array(SCALE, np.float32)[:, None]
    return rows


def split3(value):
    high = value.astype(jnp.bfloat16)
    rest = value - high.astype(F32)
    middle = rest.astype(jnp.bfloat16)
    return high, middle, (rest - middle.astype(F32)).astype(jnp.bfloat16)


def dot16(a, b, dims):
    return lax.dot_general(a, b, (dims, ((), ())), preferred_element_type=F32)


def rows_of(part):
    return pl.ds(part, LANES, stride=6)


def iota(shape, axis):
    return lax.broadcasted_iota(jnp.int32, shape, axis)


def legendre(value, count):
    values = [None, value]
    for degree in range(1, count - 1):
        before = values[degree - 1] if degree > 1 else 1.0
        values.append(value * values[degree] - (degree * degree / (4 * degree * degree - 1)) * before)
    return values


def star_terms(off_ref, diag_ref, corr_ref, counts):
    tiles = corr_ref.shape[1]
    lanes = iota((tiles, LANES), 1)
    counts = jnp.broadcast_to(counts.astype(F32), (tiles, tiles))
    square = (iota((tiles, tiles), 0) == iota((tiles, tiles), 1)).astype(F32)
    column = jnp.sum(counts * square, axis=1, keepdims=True)
    present = (lanes.astype(F32) < column).astype(F32)

    def rows(ref, visit, part):
        return ref[pl.ds(2 * visit + part, tiles, stride=2 * VISITS), :]

    weights = []
    resid = []
    for visit in range(VISITS):
        d0 = rows(diag_ref, visit, 0)
        d1 = rows(diag_ref, visit, 1)
        weights.append((d0 * present, d1 * present, corr_ref[visit] * jnp.sqrt(d0 * d1) * present))
        resid.append((rows(off_ref, visit, 0), rows(off_ref, visit, 1)))
    hess_xx = sum(w[0] for w in weights) + STAR_DAMP
    hess_yy = sum(w[1] for w in weights) + STAR_DAMP
    hess_xy = sum(w[2] for w in weights)
    determ = hess_xx * hess_yy - hess_xy * hess_xy
    inverse = (hess_yy / determ, hess_xx / determ, -hess_xy / determ)
    return weights, resid, inverse


def apply_inverse(inverse, x, y):
    inv_xx, inv_yy, inv_xy = inverse
    return inv_xx * x + inv_xy * y, inv_xy * x + inv_yy * y


def combine(values, sub):
    for shift in (4, 2, 1):
        low = (sub & shift) == 0
        half = len(values) // 2
        merged = []
        for at in range(half):
            a, b = values[at], values[at + half]
            if shift == 4:
                merged.append(jnp.where(low, a, b) + pltpu.roll(jnp.where(low, b, a), 4, 0))
            else:
                merged.append(jnp.where(low, a + pltpu.roll(a, 8 - shift, 0), b + pltpu.roll(b, shift, 0)))
        values = merged
    return values[0]


def moments_kernel(*refs):
    sources, out_refs, buffers, (sems, *scratch) = refs[:10], refs[10:17], refs[17:25], refs[25:]
    copies = [
        pltpu.make_async_copy(source, buffer, sems.at[at])
        for at, (source, buffer) in enumerate(zip(sources, (*buffers, *out_refs[5:])))
    ]
    for copy in copies:
        copy.start()
    for copy in copies[:8]:
        copy.wait()
    moments_body(*buffers, *out_refs[:5], *scratch)
    for copy in copies[8:]:
        copy.wait()


def moments_body(uv_ref, off_ref, diag_ref, corr_ref, count_ref, ids_ref, ccd_ref, slot_ref,
                 out_ref, power_ref, where_ref, base_ref, gain_ref, chan, high_power, acc, mom):
    tiles = corr_ref.shape[1]
    visits_all = tiles * VISITS
    sub8 = iota((8, LANES), 0)

    pad = jnp.zeros((LANES - visits_all, LANES), F32)
    mine = iota((VISITS, LANES), 1) // tiles == iota((VISITS, LANES), 0)

    def along_lanes(ref):
        spread = jnp.concatenate([ref[...]] * (LANES // tiles), axis=1)
        return jnp.sum(jnp.where(mine, spread, 0), axis=0, keepdims=True)

    ident = along_lanes(ids_ref)
    ccd = along_lanes(ccd_ref)
    rows128 = iota((LANES, LANES), 0)
    lanes128 = iota((LANES, LANES), 1)
    valid = iota((1, LANES), 1) < visits_all
    slot = slot_ref[...]
    digits = jnp.concatenate([slot // LANES, slot % LANES], axis=1).astype(F32).astype(jnp.bfloat16)
    picked = dot16(digits, (rows128 == ident // LANES).astype(jnp.bfloat16), ((0,), (0,)))
    inside = rows128 == ident % LANES

    def digit(at):
        chosen = jnp.where(inside, picked[at * LANES : (at + 1) * LANES], 0.0)
        return (jnp.sum(chosen, axis=0, keepdims=True) + 0.5).astype(jnp.int32)

    home, place_in = digit(0), digit(1)
    dest = jnp.where(valid, home % 32 * 4 + home // 32, -1)
    ccd = jnp.where(valid, ccd, -1)
    dest_t = jnp.broadcast_to(dest.astype(F32), (LANES, LANES)).T.astype(jnp.int32)
    same = (dest_t == dest) & (rows128 < lanes128)
    copy_at = jnp.sum(same.astype(F32), axis=0, keepdims=True).astype(jnp.int32)
    mark = (place_in + 1).astype(F32)
    counts = jnp.concatenate([count_ref[...]] * (LANES // tiles), axis=1)
    where_ref[...] = jnp.where(
        sub8 == 0, dest, jnp.where(sub8 == 1, copy_at, jnp.where(sub8 == 2, ccd, counts))
    )

    weights, resid, inverse = star_terms(off_ref, diag_ref, corr_ref, count_ref[...])
    grad_x = sum(w[0] * r[0] + w[2] * r[1] for w, r in zip(weights, resid))
    grad_y = sum(w[2] * r[0] + w[1] * r[1] for w, r in zip(weights, resid))
    shift_x, shift_y = apply_inverse(inverse, grad_x, grad_y)
    base_ref[0] = shift_x
    base_ref[1] = shift_y
    inv_xx, inv_yy, inv_xy = inverse
    channels = [[] for _ in range(7)]
    for visit in range(VISITS):
        w_xx, w_yy, w_xy = weights[visit]
        left_x = resid[visit][0] - shift_x
        left_y = resid[visit][1] - shift_y
        prod_11 = inv_xx * w_xx + inv_xy * w_xy
        prod_12 = inv_xx * w_xy + inv_xy * w_yy
        prod_21 = inv_xy * w_xx + inv_yy * w_xy
        prod_22 = inv_xy * w_xy + inv_yy * w_yy
        for at, product in enumerate((prod_11, prod_12, prod_21, prod_22)):
            gain_ref[at, pl.ds(visit * tiles, tiles), :] = product
        values = (
            uv_ref[pl.ds(2 * visit, tiles, stride=2 * VISITS), :],
            uv_ref[pl.ds(2 * visit + 1, tiles, stride=2 * VISITS), :],
            w_xx - (w_xx * prod_11 + w_xy * prod_21),
            w_yy - (w_xy * prod_12 + w_yy * prod_22),
            w_xy - (w_xx * prod_12 + w_xy * prod_22),
            w_xx * left_x + w_xy * left_y,
            w_xy * left_x + w_yy * left_y,
        )
        for at, value in enumerate(values):
            channels[at].append(value)
    for at in range(7):
        chan[at] = jnp.concatenate(channels[at] + [pad], axis=0).T

    groups = LANES // 8

    for g in range(groups):
        at = pl.ds(g * 8, 8)
        for source in range(2):
            for degree, value in enumerate(legendre(chan[source, at, :], DEG2 + 1)):
                if degree > ORDER:
                    high_power[source, degree - ORDER - 1, at, :] = value
                elif degree:
                    power_ref[source, degree - 1, at, :] = value

    def power(source, degree, at):
        if degree > ORDER:
            return high_power[source, degree - ORDER - 1, at, :]
        return power_ref[source, degree - 1, at, :]

    def sweep(i, top, first, count, row0, width):
        heights = top - i + 1

        def step(g, sums):
            at = pl.ds(pl.multiple_of(g * 8, 8), 8)
            scaled = [chan[first + w, at, :] for w in range(count)]
            if i:
                factor = power(0, i, at)
                scaled = [value * factor for value in scaled]
            new = []
            for j in range(heights):
                other = power(1, j, at) if j else None
                for w in range(count):
                    term = scaled[w] * other if j else scaled[w]
                    new.append(sums[j * count + w] + term)
            return tuple(new)

        start = tuple(jnp.zeros((8, LANES), F32) for _ in range(heights * count))
        sums = lax.fori_loop(0, groups, step, start, unroll=UNROLL)
        for j in range(heights):
            for w in range(count):
                row = row0 + w * width + TERM_INDEX[(i, j)]
                acc[pl.ds(row * 8, 8), :] = sums[j * count + w]

    for i in range(DEG2 + 1):
        sweep(i, DEG2, 2, 3, 0, LANES)
    for i in range(ORDER + 1):
        sweep(i, ORDER, 5, 2, ROW_GX, LANES)
    zero = jnp.zeros((8, LANES), F32)
    for block in range(3):
        for row in range(len(TERMS), 96):
            acc[pl.ds((block * LANES + row) * 8, 8), :] = zero
    for block in range(2):
        for row in range(POLY, 32):
            acc[pl.ds((ROW_GX + block * LANES + row) * 8, 8), :] = zero

    for g in range(ROW_DET // 8):
        mom[pl.ds(g * 8, 8), :] = combine([acc[pl.ds(g * 64 + 8 * s, 8), :] for s in range(8)], sub8)
    mom[88:96, :] = jnp.where(sub8 == 7, mark, mom[88:96, :])

    pulls = jnp.where(sub8 < 4, mom[ROW_GX : ROW_GX + 8], pltpu.roll(mom[ROW_GY : ROW_GY + 8], 4, 0))
    zero32 = jnp.zeros((32, LANES), F32)
    zero96 = jnp.zeros((96, LANES), F32)
    first = split3(mom[0:256])
    third = split3(jnp.concatenate([mom[256:352], zero32], axis=0))
    fourth = split3(jnp.concatenate([zero96, mom[0:8], mom[128:136], mom[256:264], pulls], axis=0))
    first = jnp.concatenate(first, axis=1)
    last = jnp.concatenate([piece for parts in zip(third, fourth) for piece in parts], axis=1)
    for copy in range(2):
        place = ((rows128 == dest) & (copy_at == copy)).astype(jnp.bfloat16)
        place_det = (rows128 + LANES * copy == ccd).astype(jnp.bfloat16)
        front = dot16(jnp.concatenate([place] * 3, axis=1), first, ((1,), (1,)))
        out_ref[rows_of(3 * copy), :] = front[:, 0:LANES]
        out_ref[rows_of(3 * copy + 1), :] = front[:, LANES:]
        both = jnp.concatenate([place, place_det] * 3, axis=1)
        out_ref[rows_of(3 * copy + 2), :] = dot16(both, last, ((1,), (1,)))


def detector_solve(table):
    def moment(block, i, j):
        return table[8 * block + TERM_INDEX[(i, j)] : 8 * block + TERM_INDEX[(i, j)] + 1]

    def block_of(block):
        one, u, v = moment(block, 0, 0), moment(block, 1, 0), moment(block, 0, 1)
        uu = moment(block, 2, 0) + one * (1.0 / 3.0)
        vv = moment(block, 0, 2) + one * (1.0 / 3.0)
        uv = moment(block, 1, 1)
        return [[one, u, v], [u, uu, uv], [v, uv, vv]]

    part_xx, part_yy, part_xy = block_of(0), block_of(1), block_of(2)
    matrix = [part_xx[p] + part_xy[p] for p in range(3)] + [part_xy[p] + part_yy[p] for p in range(3)]
    at = [TERM_INDEX[term] for term in ((0, 0), (1, 0), (0, 1))]
    rhs = [table[24 + a : 25 + a] for a in at] + [table[28 + a : 29 + a] for a in at]
    for p in range(6):
        matrix[p][p] = matrix[p][p] + DETECTOR_DAMP
    inverse = [None] * 6
    lower = [[None] * 6 for _ in range(6)]
    for step in range(6):
        pivot = matrix[step][step]
        for before in range(step):
            pivot = pivot - lower[step][before] * lower[step][before]
        inverse[step] = 1.0 / jnp.sqrt(pivot)
        for row in range(step + 1, 6):
            value = matrix[row][step]
            for before in range(step):
                value = value - lower[row][before] * lower[step][before]
            lower[row][step] = value * inverse[step]
    forward = []
    for step in range(6):
        value = rhs[step]
        for before in range(step):
            value = value - lower[step][before] * forward[before]
        forward.append(value * inverse[step])
    answer = [None] * 6
    for step in range(5, -1, -1):
        value = forward[step]
        for after in range(step + 1, 6):
            value = value - lower[after][step] * answer[after]
        answer[step] = value * inverse[step]
    return answer


UNKNOWNS = [("x", q) for q in range(28)] + [("y", q) for q in range(24, 28)] + [("y", q) for q in range(24)]
SIZE = 2 * POLY
BLOCKS = SIZE // 8
PANEL = 4


def solve_kernel(arr_ref, expand_ref, scale_ref, upd_ref, resp_ref, wide, mat, rhs, invs, inv_rows):
    sub8 = iota((8, LANES), 0)
    rows128 = iota((LANES, LANES), 0)
    lanes128 = iota((LANES, LANES), 1)

    marks = [arr_ref[rows_of(3 * copy), :] for copy in range(2)]
    picks = [(mark[:, MARK : MARK + 1].astype(jnp.int32) == lanes128 + 1).astype(jnp.bfloat16) for mark in marks]
    pick = [
        (mark.T[MARK : MARK + 1].astype(jnp.int32) == rows128 + 1).astype(jnp.bfloat16) for mark in marks
    ]
    slots = [
        jnp.concatenate([marks[copy]] + [arr_ref[rows_of(3 * copy + block), :] for block in (1, 2)], axis=1)
        for copy in range(2)
    ]
    slots = split3(jnp.concatenate(slots, axis=0))
    table = dot16(jnp.concatenate(pick * 3, axis=1), jnp.concatenate(slots, axis=0), ((1,), (0,)))

    sums = [jnp.sum(arr_ref[rows_of(3 * copy + 2), :], axis=0, keepdims=True) for copy in range(2)]
    turned = jnp.where(rows128 == 0, sums[0], jnp.where(rows128 == 1, sums[1], 0.0)).T
    answer = detector_solve(turned[96:128])

    pieces = []
    for block in range(3):
        high, middle, low = split3(table[:, block * LANES : (block + 1) * LANES])
        pieces.append(jnp.concatenate([high, middle, high, middle, low, high], axis=1))
    parts = jnp.concatenate(pieces, axis=0)

    def expand(q0):
        at = pl.ds(q0 * 32, PANEL * 32)
        left = [expand_ref[at, side * LANES : (side + 1) * LANES] for side in (0, 0, 1, 1, 0, 2)]
        wide[at, :] = dot16(jnp.concatenate(left, axis=1), parts, ((1,), (1,)))

    def part(which, q, group):
        return wide[q * 32 + group * 8 : q * 32 + group * 8 + 8, which * LANES : (which + 1) * LANES]

    def entry(col, group):
        kind, q = UNKNOWNS[col]
        if kind == "x":
            if group < 3:
                value = part(0, q, group)
            elif group == 3:
                value = jnp.where(sub8 < 4, part(0, q, 3), pltpu.roll(part(2, q, 3), 4, 0))
            else:
                value = part(2, q, group - 4)
        elif group == 3:
            value = jnp.where(sub8 < 4, 0.0, pltpu.roll(part(1, q, 3), 4, 0))
        else:
            value = part(1, q, group - 4)
        if group == col // 8:
            value = value + jnp.where(sub8 == col % 8, EXPOSURE_DAMP, 0.0)
        return value

    expand(0)
    expand(PANEL)
    grad_x = table[:, 0:LANES].T[96:128] * scale_ref[...]
    grad_y = table[:, LANES : 2 * LANES].T[96:128] * scale_ref[...]
    rhs[0:24, :] = grad_x[0:24]
    rhs[24:32, :] = jnp.where(sub8 < 4, grad_x[24:32], pltpu.roll(grad_y[24:32], 4, 0))
    rhs[32:56, :] = grad_y[0:24]

    for k0 in range(0, SIZE, PANEL):
        g0 = k0 // 8
        count = BLOCKS - g0

        def update(j, carry):
            base = j * SIZE
            column = [mat[pl.ds(base + g * 8, 8), :] for g in range(g0, BLOCKS)]
            new = []
            for c in range(PANEL):
                factor = mat[pl.ds(base + k0 + c, 1), :]
                for g in range(count):
                    new.append(carry[c * count + g] - column[g] * factor)
            return tuple(new)

        if k0 + 2 * PANEL < POLY:
            expand(k0 + 2 * PANEL)
        panel = tuple(entry(k0 + c, g) for c in range(PANEL) for g in range(g0, BLOCKS))
        for j in range(k0):
            panel = update(j, panel)
        panel = [list(panel[c * count : (c + 1) * count]) for c in range(PANEL)]
        right = [rhs[pl.ds(g * 8, 8), :] for g in range(g0, BLOCKS)]
        for c in range(PANEL):
            k = k0 + c
            row = k % 8
            inverse = lax.rsqrt(panel[c][0][row : row + 1])
            column = [value * inverse for value in panel[c]]
            for other in range(c + 1, PANEL):
                factor = column[0][k0 % 8 + other : k0 % 8 + other + 1]
                panel[other] = [panel[other][g] - column[g] * factor for g in range(count)]
            forward = right[0][row : row + 1] * inverse
            keep = jnp.where(sub8 <= row, right[0], right[0] - column[0] * forward)
            keep = jnp.where(sub8 == row, forward, keep)
            right = [keep] + [right[g] - column[g] * forward for g in range(1, count)]
            invs[k : k + 1, :] = inverse
            for g in range(count):
                mat[pl.ds(k * SIZE + (g0 + g) * 8, 8), :] = column[g]
        if (k0 + PANEL) % 8 == 0:
            inverted = []
            for row in range(8):
                value = jnp.where(sub8 == row, 1.0, 0.0)
                for before in range(row):
                    factor = mat[pl.ds((g0 * 8 + before) * SIZE + g0 * 8 + row, 1), :]
                    value = value - factor * inverted[before]
                value = value * invs[pl.ds(g0 * 8 + row, 1), :]
                inverted.append(value)
                inv_rows[pl.ds((g0 * 8 + row) * 8, 8), :] = value
        for g in range(count):
            rhs[pl.ds((g0 + g) * 8, 8), :] = right[g]

    solved = [None] * BLOCKS
    for b in range(BLOCKS - 1, -1, -1):
        right = rhs[b * 8 : b * 8 + 8]
        if b < BLOCKS - 1:
            partial = []
            for c in range(8):
                total = None
                for g in range(b + 1, BLOCKS):
                    term = mat[pl.ds((b * 8 + c) * SIZE + g * 8, 8), :] * solved[g]
                    total = term if total is None else total + term
                partial.append(total)
            right = right - combine(partial, sub8)
        terms = [inv_rows[pl.ds((b * 8 + c) * 8, 8), :] * right[c : c + 1] for c in range(8)]
        while len(terms) > 1:
            terms = [terms[at] + terms[at + 1] for at in range(0, len(terms), 2)]
        solved[b] = terms[0]
    whole = jnp.concatenate(
        solved[0:3] + [solved[3][0:4]] + solved[4:7] + [solved[3][4:8]], axis=0
    )
    upd_ref[...] = whole

    lane1 = iota((1, LANES), 1)
    first = [jnp.where(lane1 == 0, value, 0.0) for value in answer]
    second = [jnp.where(lane1 == 1, value, 0.0) for value in answer]
    zeros = jnp.zeros((SIZE, LANES), F32)
    zero16 = jnp.zeros((16, LANES), F32)
    gap = [jnp.zeros((2, LANES), F32)]
    left = jnp.concatenate(picks + [(lanes128 < 2).astype(jnp.bfloat16)], axis=1)
    right = jnp.concatenate(
        [
            jnp.concatenate([whole, zeros, zero16], axis=0),
            jnp.concatenate([zeros, whole, zero16], axis=0),
            jnp.concatenate([zeros, zeros] + first + gap + second + gap, axis=0),
        ],
        axis=1,
    )
    left = jnp.concatenate([left] * 3, axis=1)
    resp_ref[...] = dot16(left, jnp.concatenate(split3(right), axis=1), ((1,), (1,)))


def star_kernel(base_ref, gain_ref, power_ref, where_ref, scale_ref, update_ref, resp_ref,
                star_ref, det_ref, update_out, coeff, model, sem):
    write = pltpu.make_async_copy(update_ref, update_out, sem)
    write.start()
    tiles = base_ref.shape[1]
    rows128 = iota((LANES, LANES), 0)
    turned = resp_ref[...].T
    det_ref[:, 0:LANES] = turned[112:118]
    det_ref[:, LANES:NCCD] = turned[120:126, 0 : NCCD - LANES]
    dest = where_ref[0:1]
    copy_at = where_ref[1:2]
    ccd = where_ref[2:3]
    picks = [((rows128 == dest) & (copy_at == c)).astype(jnp.bfloat16) for c in range(2)]
    dets = [(rows128 + LANES * c == ccd).astype(jnp.bfloat16) for c in range(2)]
    halves = split3(jnp.concatenate([turned[0:56], turned[56:112]], axis=1))
    exposure = dot16(jnp.concatenate(halves, axis=1), jnp.concatenate(picks * 3, axis=0), ((1,), (0,)))
    halves = split3(jnp.concatenate([turned[112:120], turned[120:128]], axis=1))
    detector = dot16(jnp.concatenate(halves, axis=1), jnp.concatenate(dets * 3, axis=0), ((1,), (0,)))
    scale = scale_ref[...]
    coeff[0:28, :] = exposure[0:28] * scale[0:28]
    coeff[32:60, :] = exposure[28:56] * scale[0:28]
    for axis in range(2):
        for m, term in enumerate(((0, 0), (1, 0), (0, 1))):
            row = 32 * axis + TERM_INDEX[term]
            coeff[row : row + 1, :] = coeff[row : row + 1, :] + detector[3 * axis + m : 3 * axis + m + 1]

    for g in range(LANES // 8):
        at = pl.ds(g * 8, 8)
        in_u = [None] + [power_ref[0, i, at, :] for i in range(ORDER)]
        in_v = [None] + [power_ref[1, i, at, :] for i in range(ORDER)]
        for axis in range(2):
            total = None
            for i in range(ORDER + 1):
                inner = None
                for j in range(ORDER - i + 1):
                    row = 32 * axis + TERM_INDEX[(i, j)]
                    term = coeff[row : row + 1, :]
                    if j:
                        term = term * in_v[j]
                    inner = term if inner is None else inner + term
                if i:
                    inner = inner * in_u[i]
                total = inner if total is None else total + inner
            model[axis, at, :] = total
    model_x = model[0].T
    model_y = model[1].T
    out_x = base_ref[0]
    out_y = base_ref[1]
    for visit in range(VISITS):
        at = slice(visit * tiles, (visit + 1) * tiles)
        out_x = out_x - (gain_ref[0, at, :] * model_x[at] + gain_ref[1, at, :] * model_y[at])
        out_y = out_y - (gain_ref[2, at, :] * model_x[at] + gain_ref[3, at, :] * model_y[at])
    star_ref[:, 0, :] = out_x
    star_ref[:, 1, :] = out_y
    write.wait()


def vmem(count):
    return [pl.BlockSpec(memory_space=pltpu.VMEM)] * count


def shards(focal_uv, offsets, w_diag, w_corr, star_count, exposure_ids, ccd_ids, exp_slot):
    tiles = offsets.shape[0]
    flat = (tiles * VISITS * 2, LANES)
    inputs = (
        focal_uv.reshape(flat),
        offsets.reshape(flat),
        w_diag.reshape(flat),
        jnp.transpose(w_corr, (1, 0, 2)),
        star_count.reshape(1, tiles),
        exposure_ids.T,
        ccd_ids.T,
        exp_slot.reshape(LANES, LANES),
    )
    shape = jax.ShapeDtypeStruct
    tables = (jnp.asarray(expansion()), jnp.asarray(scale_rows()))
    outgoing, powers, where, base, gain, expand, scale = pl.pallas_call(
        moments_kernel,
        out_shape=(
            shape((6 * LANES, LANES), F32),
            shape((2, ORDER, LANES, LANES), F32),
            shape((8, LANES), jnp.int32),
            shape((2, tiles, LANES), F32),
            shape((4, tiles * VISITS, LANES), F32),
            *(shape(array.shape, array.dtype) for array in tables),
        ),
        in_specs=[pl.BlockSpec(memory_space=pltpu.HBM)] * 10,
        out_specs=tuple(vmem(7)),
        scratch_shapes=[pltpu.VMEM(array.shape, array.dtype) for array in inputs]
        + [
            pltpu.SemaphoreType.DMA((10,)),
            pltpu.VMEM((7, LANES, LANES), F32),
            pltpu.VMEM((2, ORDER, LANES, LANES), F32),
            pltpu.VMEM((ROW_DET * 8, LANES), F32),
            pltpu.VMEM((ROW_DET, LANES), F32),
        ],
        compiler_params=pltpu.CompilerParams(vmem_limit_bytes=12 << 20),
        name="moments",
    )(*(pltpu.with_memory_space_constraint(array, pltpu.HBM) for array in (*inputs, *tables)))
    arrived = lax.all_to_all(outgoing.reshape(LANES, 1, 6 * LANES), ("shard", "field"), 0, 0, tiled=True)
    arrived = arrived.reshape(6 * LANES, LANES)
    update, answers = pl.pallas_call(
        solve_kernel,
        out_shape=(shape((SIZE, LANES), F32), shape((LANES, LANES), F32)),
        in_specs=vmem(3),
        out_specs=tuple(vmem(2)),
        scratch_shapes=[
            pltpu.VMEM((POLY * 32, 3 * LANES), F32),
            pltpu.VMEM((SIZE * SIZE, LANES), F32),
            pltpu.VMEM((SIZE, LANES), F32),
            pltpu.VMEM((SIZE, LANES), F32),
            pltpu.VMEM((SIZE * 8, LANES), F32),
        ],
        compiler_params=pltpu.CompilerParams(vmem_limit_bytes=12 << 20),
        name="solve",
    )(arrived, expand, scale)
    replies = lax.all_to_all(answers.reshape(LANES, 1, LANES), ("shard", "field"), 0, 0, tiled=True)
    star_update, ccd_update, update = pl.pallas_call(
        star_kernel,
        out_shape=(shape((tiles, 2, LANES), F32), shape((6, NCCD), F32), shape((SIZE, LANES), F32)),
        in_specs=vmem(7),
        out_specs=(*vmem(2), pl.BlockSpec(memory_space=pltpu.HBM)),
        scratch_shapes=[
            pltpu.VMEM((64, LANES), F32),
            pltpu.VMEM((2, LANES, LANES), F32),
            pltpu.SemaphoreType.DMA,
        ],
        compiler_params=pltpu.CompilerParams(vmem_limit_bytes=12 << 20),
        name="stars",
    )(base, gain, powers, where, scale, update, replies.reshape(LANES, LANES))
    return star_update, update, ccd_update.T


def solution(mesh):
    both = ("field", "shard")
    in_specs = (
        P(both, None, None, None),
        P(both, None, None, None),
        P(both, None, None, None),
        P(both, None, None),
        P(both),
        P(both, None),
        P(both, None),
        P(),
    )
    out_specs = (P(both, None, None), P(None, both), P())
    return jax.shard_map(shards, mesh=mesh, in_specs=in_specs, out_specs=out_specs, check_vma=False)
```
